128 devices in a mesh: src: 8 (over z, core), tgt: 16 (over y, x).
Axes of the slice: x: 4, y: 4, z: 4, core: 2. Of those that a mesh axis runs over, the one named last changes fastest.
Arguments:
- source: bfloat16 [16384, 512], P(('src', 'tgt')), may hold values from -64 to 64
- target: bfloat16 [16384, 512], P('tgt', 'src'), may hold values from -64 to 64
- rotation: float32 [512, 512], replicated, may hold values from -0.06 to 1.06
Outputs:
- aligned: float32 [512, 512], replicated
- moved: float32 [16384, 512], P(('src', 'tgt'))
The draws below stay inside these ranges and needn't reach their ends.
All inputs are finite; a program needn't handle non-finite values.
Results may differ from the reference program's by a relative error of at most 0.013.
Values may be sent and summed in bfloat16 or wider, within the bound.
A program may use at most 64 MiB of HBM per device.

```python
import math
import jax
import jax.numpy as jnp
from jax import lax

D = 512
ROUNDS = 2
BALANCE_ITERS = 2
NS = 16384
NT = 16384


def paired_sample(key):
    base = jax.random.fold_in(key, 11)
    key_source, key_target, key_turn = jax.random.split(base, 3)
    noise = jnp.clip(jax.random.normal(key_turn, (D, D), jnp.float32), -6.0, 6.0)
    turn_matrix = jnp.eye(D, dtype=jnp.float32) + 0.009 * noise
    position = (jnp.arange(NS, dtype=jnp.float32) + 0.5) / NS - 0.5
    phase = jnp.cos(2.0 * math.pi * 3.0 * jnp.arange(D, dtype=jnp.float32) / D)
    profile = jnp.exp(math.log(3.0) * position[:, None] * phase[None, :])
    source_rows = jnp.clip(jax.random.normal(key_source, (NS, D), jnp.float32), -6.0, 6.0)
    target_rows = jnp.clip(jax.random.normal(key_target, (NT, D), jnp.float32), -6.0, 6.0)
    source_rows = source_rows * profile
    source_rows = jnp.clip(source_rows, -64.0, 64.0)
    target_rows = jnp.clip(target_rows, -64.0, 64.0)
    return (source_rows, target_rows, turn_matrix)


def draw_source(key, part):
    return paired_sample(key)[0].astype(jnp.bfloat16)


def draw_target(key, part):
    return paired_sample(key)[1].astype(jnp.bfloat16)


def draw_rotation(key, part):
    return paired_sample(key)[2]


def setup_inputs(seed: int = 0) -> dict:
    key_list = jax.random.split(jax.random.key(seed), 4)
    return {
        "source": draw_source(jax.random.fold_in(key_list[3], 71), 0),
        "target": draw_target(jax.random.fold_in(key_list[3], 71), 0),
        "rotation": draw_rotation(jax.random.fold_in(key_list[3], 71), 0),
    }


full_precision = lax.Precision.HIGHEST
step_rate = 0.1

def scores_of(rotated_block, features, scaling):
    return jnp.dot(rotated_block, features.T, precision=full_precision) * scaling

def reference(source, target, rotation):
    source_float = source.astype(jnp.float32)
    features = target.astype(jnp.float32)
    source_count = source.shape[0]
    target_count = target.shape[0]
    width = source.shape[1]
    scaling = 1.0 / math.sqrt(width)
    log_source = -math.log(source_count)
    log_target = -math.log(target_count)
    block_rows = math.gcd(source_count, 512)
    block_count = source_count // block_rows
    current = rotation
    moved = jnp.zeros((source_count, width), jnp.float32)
    for round_index in range(ROUNDS):
        rotated = jnp.dot(source_float, current, precision=full_precision)
        rotated = lax.optimization_barrier(rotated.astype(jnp.bfloat16)).astype(jnp.float32)
        rotated_blocks = rotated.reshape(block_count, block_rows, width)
        row_shift = jnp.zeros((source_count,), jnp.float32)
        row_log = jnp.zeros((source_count,), jnp.float32)
        col_shift = jnp.zeros((target_count,), jnp.float32)
        for balance_pass in range(BALANCE_ITERS):
            shift_blocks = row_shift.reshape(block_count, block_rows)

            def col_step(running, segment_list):
                highest, summed = running
                values = scores_of(segment_list[0], features, scaling) + segment_list[1][:, None]
                newest = jnp.maximum(highest, lax.optimization_barrier(jnp.max(values, axis=0)))
                summed = summed * jnp.exp(highest - newest) + lax.optimization_barrier(jnp.sum(jnp.exp(values - newest[None, :]), axis=0))
                return ((newest, summed), None)
            start_state = (jnp.full((target_count,), -jnp.inf, jnp.float32), jnp.zeros((target_count,), jnp.float32))
            (col_top, col_all), unused = lax.scan(col_step, start_state, (rotated_blocks, shift_blocks))
            col_shift = log_target - (col_top + jnp.log(col_all))

            def row_block(rotated_block):
                values = scores_of(rotated_block, features, scaling) + col_shift[None, :]
                highest = lax.optimization_barrier(jnp.max(values, axis=1))
                return highest + jnp.log(lax.optimization_barrier(jnp.sum(jnp.exp(values - highest[:, None]), axis=1)))
            row_log = lax.map(row_block, rotated_blocks).reshape(source_count)
            row_shift = log_source - row_log
        log_blocks = row_log.reshape(block_count, block_rows)

        def plan_block(segment_list):
            values = scores_of(segment_list[0], features, scaling) + col_shift[None, :]
            weights = jnp.exp(values - segment_list[1][:, None])
            weights = lax.optimization_barrier(weights.astype(jnp.bfloat16)).astype(jnp.float32)
            return jnp.dot(weights, features, precision=full_precision)
        moved = lax.map(plan_block, (rotated_blocks, log_blocks)).reshape(source_count, width)
        cross = jnp.dot(source_float.T, moved, precision=full_precision)
        spread = jnp.sqrt(jnp.mean(cross * cross) + 1e-06)
        guess = current + step_rate * cross / (spread * math.sqrt(width))
        gram = jnp.dot(guess.T, guess, precision=full_precision)
        current = 1.5 * guess - 0.5 * jnp.dot(guess, gram, precision=full_precision)
    return (current, moved)
```

```python
import functools
import math

import jax
import jax.numpy as jnp
from jax import lax
from jax.experimental import pallas as pl
from jax.experimental.pallas import tpu as pltpu
from jax.sharding import PartitionSpec as P

ROUNDS = 2
MESH = pl.DeviceIdType.MESH
F32, BF16 = jnp.float32, jnp.bfloat16
NSRC, NTGT = 8, 16
D = 512
OWN = 128
ROWS = 2048
COLS = 1024
CH = 256
RB = 32
LOG_N = 14.0
SCALE = 1.0 / math.sqrt(D) * math.log2(math.e)
NT_DIMS = (((1,), (1,)), ((), ()))


def mm(a, b):
    return jnp.dot(a, b, preferred_element_type=F32)


def split3(w):
    hi = w.astype(BF16)
    rest = w - hi.astype(F32)
    mid = rest.astype(BF16)
    lo = (rest - mid.astype(F32)).astype(BF16)
    return hi, mid, lo


def split2(w):
    hi = w.astype(BF16)
    return hi, (w - hi.astype(F32)).astype(BF16)


def kernel(
    src_in, tpk_in, rot_in, aligned, moved,
    sblk, sblk_t, tpk, feats, scores, plan, planb, probs, ucol, mrow, lrow,
    col_m, col_s, vrow, w3, cur, colx, rowx, sib1, tgt1, zred, mhalf, mother, gbuf, mvx, mhold, mkeep, rlse,
    src_send, src_recv, tpk_send, tpk_recv, col_send, col_recv, row_send, row_recv,
    ar_send, ar_recv, mv_send, mv_recv,
):
    si, ti = lax.axis_index("src"), lax.axis_index("tgt")
    core, zed = lax.rem(si, 2), si // 2
    sibling = zed * 2 + 1 - core

    def tgt_peer(d):
        return lax.rem(ti + d, NTGT)

    def src_peer(d):
        return lax.rem(si + d, NSRC)

    barrier = pltpu.get_barrier_semaphore()

    @pl.loop(1, NTGT)
    def _(d):
        pl.semaphore_signal(barrier, inc=1, device_id=(si, tgt_peer(d)), device_id_type=MESH)

    @pl.loop(1, NSRC)
    def _(d):
        pl.semaphore_signal(barrier, inc=1, device_id=(src_peer(d), ti), device_id_type=MESH)

    pl.semaphore_wait(barrier, NTGT + NSRC - 2)

    def to(src, dst, send, recv, s, t):
        return pltpu.make_async_remote_copy(
            src_ref=src, dst_ref=dst, send_sem=send, recv_sem=recv,
            device_id=(s, t), device_id_type=MESH)

    def slot128(k):
        return pl.ds(pl.multiple_of(k * OWN, OWN), OWN)

    @pl.loop(1, NSRC)
    def _(d):
        to(tpk_in, tpk.at[si], tpk_send, tpk_recv, src_peer(d), ti).start()

    @pl.loop(1, NTGT)
    def _(d):
        to(src_in, sblk.at[slot128(ti), :], src_send, src_recv.at[ti], si, tgt_peer(d)).start()

    sblk[slot128(ti), :] = src_in[...]
    tpk[si] = tpk_in[...]
    cur[...] = rot_in[...]
    for part, piece in enumerate(split3(rot_in[...])):
        w3[part * D:(part + 1) * D, :] = piece

    pltpu.make_async_copy(tpk.at[pl.ds(0, NSRC - 1)], tpk.at[pl.ds(0, NSRC - 1)], tpk_recv).wait()
    lanes = lax.broadcasted_iota(jnp.int32, (512, 128), 1)
    for pair in range(4):
        even, odd = tpk[2 * pair].astype(F32), tpk[2 * pair + 1].astype(F32)
        cut = pl.ds(128 * pair, 128)
        feats[0:512, cut] = jnp.where(lanes < 64, even, pltpu.roll(odd, 64, 1)).astype(BF16)
        feats[512:1024, cut] = jnp.where(lanes < 64, pltpu.roll(even, 64, 1), odd).astype(BF16)

    def chunk(j):
        return pl.ds(pl.multiple_of(j * CH, CH), CH)

    def reset_cols():
        col_m[...] = jnp.full((8, COLS), -jnp.inf, F32)
        col_s[...] = jnp.zeros((8, COLS), F32)

    def col_update(rows, shifted):
        for ct in range(COLS // 128):
            cut = pl.ds(128 * ct, 128)
            x = scores[rows, cut]
            if shifted:
                x = x + ucol[rows, :]
            x = x.reshape(CH // 8, 8, 128)
            old = col_m[:, cut]
            new = jnp.maximum(old, jnp.max(x, axis=0))
            col_s[:, cut] = col_s[:, cut] * jnp.exp2(old - new) + jnp.sum(jnp.exp2(x - new[None]), axis=0)
            col_m[:, cut] = new

    def col_exchange(slot):
        for ct in range(COLS // 128):
            cut = pl.ds(128 * ct, 128)
            high = jnp.max(col_m[:, cut], axis=0, keepdims=True)
            total = jnp.sum(col_s[:, cut] * jnp.exp2(col_m[:, cut] - high), axis=0, keepdims=True)
            colx[slot, si, ct:ct + 1, :] = high + jnp.log2(total)

        @pl.loop(1, NSRC)
        def _(d):
            to(colx.at[slot, si], colx.at[slot, si], col_send.at[slot], col_recv.at[slot], src_peer(d), ti).start()

        seven = colx.at[slot, pl.ds(0, NSRC - 1)]
        pltpu.make_async_copy(seven, seven, col_recv.at[slot]).wait()
        every = colx[slot]
        high = jnp.max(every, axis=0)
        v = -LOG_N - (high + jnp.log2(jnp.sum(jnp.exp2(every - high[None]), axis=0)))
        for ct in range(COLS // 128):
            vrow[:, 128 * ct:128 * (ct + 1)] = jnp.broadcast_to(v[ct:ct + 1, :], (8, 128))

    def row_strip(rows, last):
        x = scores[rows, :].reshape(RB // 8, 8, COLS) + vrow[...][None]
        x = x.reshape(RB, COLS)
        high = jnp.max(x, axis=1, keepdims=True)
        p = jnp.exp2(x - high)
        lrow[rows, :] = jnp.broadcast_to(high + jnp.log2(jnp.sum(p, axis=1, keepdims=True)), (RB, 128))
        if last:
            mrow[rows, :] = jnp.broadcast_to(high, (RB, 128))
        return p

    def row_send_all(slot):
        @pl.loop(0, NTGT)
        def _(k):
            rowx[slot, ti, pl.ds(k, 1), :] = jnp.transpose(lrow[slot128(k), :])[0:1, :]

        @pl.loop(1, NTGT)
        def _(d):
            to(rowx.at[slot, ti], rowx.at[slot, ti], row_send.at[slot], row_recv.at[slot], si, tgt_peer(d)).start()

    def row_combine(slot):
        most = rowx.at[slot, pl.ds(0, NTGT - 1)]
        pltpu.make_async_copy(most, most, row_recv.at[slot]).wait()
        every = rowx[slot]
        high = jnp.max(every, axis=0)
        rlse[...] = high + jnp.log2(jnp.sum(jnp.exp2(every - high[None]), axis=0))

    def row_expanded(k):
        row = rlse[pl.ds(k, 1), :]
        return jnp.transpose(jnp.broadcast_to(row, (128, 128)))

    @pl.loop(0, ROUNDS)
    def _(r):
        first, final = r == 0, r == ROUNDS - 1
        reset_cols()

        @pl.loop(0, ROWS // CH)
        def _(step):
            j = lax.rem(ti // 2 + ROWS // CH - step, ROWS // CH)
            rows = chunk(j)

            @pl.when(first)
            def _():
                for side in range(CH // OWN):
                    k = j * (CH // OWN) + side

                    @pl.when(k != ti)
                    def _():
                        land = sblk.at[slot128(k), :]
                        pltpu.make_async_copy(land, land, src_recv.at[k]).wait()

                sblk_t[:, rows] = jnp.transpose(sblk[rows, :])

            piece = sblk[rows, :]
            z = mm(jnp.concatenate([piece] * 3, axis=1), w3[...]).astype(BF16)
            scores[rows, :] = lax.dot_general(z, feats[...], NT_DIMS, preferred_element_type=F32) * SCALE
            col_update(rows, False)

        col_exchange(2 * r)

        @pl.loop(0, ROWS // RB)
        def _(step):
            row_strip(pl.ds(pl.multiple_of(step * RB, RB), RB), False)

        row_send_all(2 * r)
        row_combine(2 * r)

        @pl.loop(0, NTGT)
        def _(k):
            ucol[slot128(k), :] = -LOG_N - row_expanded(k)

        reset_cols()

        @pl.loop(0, ROWS // CH)
        def _(j):
            col_update(chunk(j), True)

        col_exchange(2 * r + 1)

        @pl.loop(0, ROWS // CH)
        def _(j):
            @pl.loop(0, CH // RB)
            def _(step):
                rows = pl.ds(pl.multiple_of(j * CH + step * RB, RB), RB)
                p = row_strip(rows, True)
                probs[pl.ds(pl.multiple_of(step * RB, RB), RB), :] = p.astype(BF16)

            plan[chunk(j), :] = mm(probs[...], feats[...])

        row_send_all(2 * r + 1)
        row_combine(2 * r + 1)

        @pl.loop(0, NTGT)
        def _(k):
            rows = slot128(k)
            factor = jnp.exp2(mrow[rows, :] - row_expanded(k))
            for cut in range(D // 128):
                lane = pl.ds(128 * cut, 128)
                planb[rows, lane] = (plan[rows, lane] * factor).astype(BF16)

        @pl.when(final)
        def _():
            @pl.loop(1, NTGT)
            def _(d):
                t = tgt_peer(d)
                to(planb.at[slot128(t), :], mvx.at[slot128(ti), :], mv_send, mv_recv, si, t).start()

        theirs = pl.ds(pl.multiple_of((1 - core) * 256, 256), 256)
        ours = pl.ds(pl.multiple_of(core * 256, 256), 256)
        mhold[r] = mm(sblk_t[theirs, :], planb[...]).astype(BF16)
        pair = to(mhold.at[r], sib1.at[r], ar_send.at[0, r], ar_recv.at[0, r], sibling, ti)
        pair.start()
        mine = mm(sblk_t[ours, :], planb[...])
        pair.wait_recv()
        mkeep[r] = (mine + sib1[r].astype(F32)).astype(BF16)

        def lot(k):
            return pl.ds(pl.multiple_of(k * 16, 16), 16)

        @pl.loop(1, NTGT)
        def _(d):
            t = tgt_peer(d)
            to(mkeep.at[r, lot(t), :], tgt1.at[r, ti], ar_send.at[1, r], ar_recv.at[1, r], si, t).start()

        tgt1[r, ti] = mkeep[r, lot(ti), :]
        most = tgt1.at[r, pl.ds(0, NTGT - 1)]
        pltpu.make_async_copy(most, most, ar_recv.at[1, r]).wait()
        zred[r, zed] = jnp.sum(tgt1[r].astype(F32), axis=0).astype(BF16)

        @pl.loop(1, 4)
        def _(d):
            other = lax.rem(zed + d, 4) * 2 + core
            to(zred.at[r, zed], zred.at[r, zed], ar_send.at[2, r], ar_recv.at[2, r], other, ti).start()

        most_z = zred.at[r, pl.ds(0, 3)]
        pltpu.make_async_copy(most_z, most_z, ar_recv.at[2, r]).wait()
        mhalf[r, lot(ti), :] = jnp.sum(zred[r].astype(F32), axis=0).astype(BF16)

        @pl.loop(1, NTGT)
        def _(d):
            to(mhalf.at[r, lot(ti), :], mhalf.at[r, lot(ti), :], ar_send.at[3, r], ar_recv.at[3, r],
               si, tgt_peer(d)).start()

        most_h = mhalf.at[r, pl.ds(0, 240), :]
        pltpu.make_async_copy(most_h, most_h, ar_recv.at[3, r]).wait()
        back = to(mhalf.at[r], mother.at[r], ar_send.at[4, r], ar_recv.at[4, r], sibling, ti)
        back.start()
        gbuf[ours, :] = mhalf[r].astype(F32)
        back.wait_recv()
        gbuf[theirs, :] = mother[r].astype(F32)

        cross = gbuf[...]
        spread = jnp.sqrt(jnp.mean(cross * cross, axis=(0, 1), keepdims=True) + 1e-06)
        g = cur[...] + 0.1 * cross / (spread * math.sqrt(D))
        gh, gl = split2(g)
        gth, gtl = jnp.transpose(gh), jnp.transpose(gl)
        gram = mm(jnp.concatenate([gth, gth, gtl], axis=1), jnp.concatenate([gh, gl, gh], axis=0))
        rh, rl = split2(gram)
        step = mm(jnp.concatenate([gh, gh, gl], axis=1), jnp.concatenate([rh, rl, rh], axis=0))
        new = 1.5 * g - 0.5 * step
        cur[...] = new

        @pl.when(jnp.logical_not(final))
        def _():
            for part, piece in enumerate(split3(cur[...])):
                w3[part * D:(part + 1) * D, :] = piece

        for slot in (2 * r, 2 * r + 1):
            seven = colx.at[slot, pl.ds(0, NSRC - 1)]
            pltpu.make_async_copy(seven, seven, col_send.at[slot]).wait()
            fifteen = rowx.at[slot, pl.ds(0, NTGT - 1)]
            pltpu.make_async_copy(fifteen, fifteen, row_send.at[slot]).wait()
        pair.wait_send()
        pltpu.make_async_copy(most, most, ar_send.at[1, r]).wait()
        pltpu.make_async_copy(most_z, most_z, ar_send.at[2, r]).wait()
        pltpu.make_async_copy(most_h, most_h, ar_send.at[3, r]).wait()
        back.wait_send()

    aligned[...] = cur[...]
    mvx[slot128(ti), :] = planb[slot128(ti), :]
    most_mv = mvx.at[pl.ds(0, ROWS - OWN), :]
    pltpu.make_async_copy(most_mv, most_mv, mv_recv).wait()
    total = mvx[0:OWN, :].astype(F32)
    for k in range(1, NTGT):
        total = total + mvx[k * OWN:(k + 1) * OWN, :].astype(F32)
    moved[...] = total
    pltpu.make_async_copy(most_mv, most_mv, mv_send).wait()
    seven_tpk = tpk.at[pl.ds(0, NSRC - 1)]
    pltpu.make_async_copy(seven_tpk, seven_tpk, tpk_send).wait()
    most_src = sblk.at[pl.ds(0, ROWS - OWN), :]
    pltpu.make_async_copy(most_src, most_src, src_send).wait()


def shards(source, target, rotation):
    packed = jnp.concatenate([target[:512], target[512:]], axis=1)
    vmem = pl.BlockSpec(memory_space=pltpu.VMEM)
    dma = pltpu.SemaphoreType.DMA
    v = pltpu.VMEM
    return pl.pallas_call(
        kernel,
        out_shape=(jax.ShapeDtypeStruct((D, D), F32), jax.ShapeDtypeStruct((OWN, D), F32)),
        in_specs=[vmem] * 3,
        out_specs=(vmem, vmem),
        scratch_shapes=[
            v((ROWS, D), BF16),
            v((D, ROWS), BF16),
            v((NSRC, 512, 128), BF16),
            v((COLS, D), BF16),
            v((ROWS, COLS), F32),
            v((ROWS, D), F32),
            v((ROWS, D), BF16),
            v((CH, COLS), BF16),
            v((ROWS, 128), F32),
            v((ROWS, 128), F32),
            v((ROWS, 128), F32),
            v((8, COLS), F32),
            v((8, COLS), F32),
            v((8, COLS), F32),
            v((3 * D, D), BF16),
            v((D, D), F32),
            v((4, NSRC, 8, 128), F32),
            v((4, NTGT, 16, 128), F32),
            v((2, 256, D), BF16),
            v((2, NTGT, 16, D), BF16),
            v((2, 4, 16, D), BF16),
            v((2, 256, D), BF16),
            v((2, 256, D), BF16),
            v((D, D), F32),
            v((ROWS, D), BF16),
            v((2, 256, D), BF16),
            v((2, 256, D), BF16),
            v((16, 128), F32),
            dma(()), dma((NTGT,)), dma(()), dma(()),
            dma((4,)), dma((4,)), dma((4,)), dma((4,)),
            dma((5, 2)), dma((5, 2)), dma(()), dma(()),
        ],
        compiler_params=pltpu.CompilerParams(
            collective_id=0, has_side_effects=True, vmem_limit_bytes=60 * 1024 * 1024),
    )(source, packed, rotation)


def solution(mesh):
    return jax.shard_map(
        shards, mesh=mesh, in_specs=(P(("src", "tgt"), None), P("tgt", "src"), P()),
        out_specs=(P(), P(("src", "tgt"), None)), check_vma=False)
```

```python
import functools
import math

import jax
import jax.numpy as jnp
from jax import lax
from jax.experimental import pallas as pl
from jax.experimental.pallas import tpu as pltpu
from jax.sharding import PartitionSpec as P

ROUNDS = 2
MESH = pl.DeviceIdType.MESH
F32, BF16 = jnp.float32, jnp.bfloat16
NSRC, NTGT = 8, 16
D = 512
OWN = 128
ROWS = 2048
COLS = 1024
CH = 256
RB = 32
LOG_N = 14.0
SCALE = 1.0 / math.sqrt(D) * math.log2(math.e)


def mm(a, b):
    return jnp.dot(a, b, preferred_element_type=F32)


def split3(w):
    hi = w.astype(BF16)
    rest = w - hi.astype(F32)
    mid = rest.astype(BF16)
    lo = (rest - mid.astype(F32)).astype(BF16)
    return hi, mid, lo


def split2(w):
    hi = w.astype(BF16)
    return hi, (w - hi.astype(F32)).astype(BF16)


def kernel(
    src_in, tgt_in, rot_in, aligned, moved,
    sblk, sblk_t, feats_t, feats, scores, plan, planb, probs, ucol, mrow, lrow,
    col_m, col_s, vrow, w3, cur, colx, rowx, sib1, tgt1, zred, mhalf, mother, gbuf, mvx, mhold, mkeep, rlse,
    src_send, src_recv, tgt_send, tgt_recv, col_send, col_recv, row_send, row_recv,
    ar_send, ar_recv, mv_send, mv_recv,
):
    si, ti = lax.axis_index("src"), lax.axis_index("tgt")
    core, zed = lax.rem(si, 2), si // 2
    sibling = zed * 2 + 1 - core

    def tgt_peer(d):
        return lax.rem(ti + d, NTGT)

    def src_peer(d):
        return lax.rem(si + d, NSRC)

    barrier = pltpu.get_barrier_semaphore()

    @pl.loop(1, NTGT)
    def _(d):
        pl.semaphore_signal(barrier, inc=1, device_id=(si, tgt_peer(d)), device_id_type=MESH)

    @pl.loop(1, NSRC)
    def _(d):
        pl.semaphore_signal(barrier, inc=1, device_id=(src_peer(d), ti), device_id_type=MESH)

    pl.semaphore_wait(barrier, NTGT + NSRC - 2)

    def to(src, dst, send, recv, s, t):
        return pltpu.make_async_remote_copy(
            src_ref=src, dst_ref=dst, send_sem=send, recv_sem=recv,
            device_id=(s, t), device_id_type=MESH)

    def slot128(k):
        return pl.ds(pl.multiple_of(k * OWN, OWN), OWN)

    def slot64(k):
        return pl.ds(pl.multiple_of(k * 64, 64), 64)

    @pl.loop(1, NSRC)
    def _(d):
        to(tgt_in, feats_t.at[slot64(si), :], tgt_send, tgt_recv, src_peer(d), ti).start()

    @pl.loop(1, NTGT)
    def _(d):
        to(src_in, sblk.at[slot128(ti), :], src_send, src_recv.at[ti], si, tgt_peer(d)).start()

    sblk[slot128(ti), :] = src_in[...]
    feats_t[slot64(si), :] = tgt_in[...]
    cur[...] = rot_in[...]
    for part, piece in enumerate(split3(rot_in[...])):
        w3[part * D:(part + 1) * D, :] = piece

    most_tgt = feats_t.at[pl.ds(0, D - 64), :]
    pltpu.make_async_copy(most_tgt, most_tgt, tgt_recv).wait()
    for part in range(D // 128):
        feats[:, 128 * part:128 * (part + 1)] = jnp.transpose(feats_t[128 * part:128 * (part + 1), :])

    def chunk(j):
        return pl.ds(pl.multiple_of(j * CH, CH), CH)

    def reset_cols():
        col_m[...] = jnp.full((8, COLS), -jnp.inf, F32)
        col_s[...] = jnp.zeros((8, COLS), F32)

    def col_update(rows, shifted):
        for ct in range(COLS // 128):
            cut = pl.ds(128 * ct, 128)
            x = scores[rows, cut]
            if shifted:
                x = x + ucol[rows, :]
            x = x.reshape(CH // 8, 8, 128)
            old = col_m[:, cut]
            new = jnp.maximum(old, jnp.max(x, axis=0))
            col_s[:, cut] = col_s[:, cut] * jnp.exp2(old - new) + jnp.sum(jnp.exp2(x - new[None]), axis=0)
            col_m[:, cut] = new

    def col_exchange(slot):
        for ct in range(COLS // 128):
            cut = pl.ds(128 * ct, 128)
            high = jnp.max(col_m[:, cut], axis=0, keepdims=True)
            total = jnp.sum(col_s[:, cut] * jnp.exp2(col_m[:, cut] - high), axis=0, keepdims=True)
            colx[slot, si, ct:ct + 1, :] = high + jnp.log2(total)

        @pl.loop(1, NSRC)
        def _(d):
            to(colx.at[slot, si], colx.at[slot, si], col_send.at[slot], col_recv.at[slot], src_peer(d), ti).start()

        seven = colx.at[slot, pl.ds(0, NSRC - 1)]
        pltpu.make_async_copy(seven, seven, col_recv.at[slot]).wait()
        every = colx[slot]
        high = jnp.max(every, axis=0)
        v = -LOG_N - (high + jnp.log2(jnp.sum(jnp.exp2(every - high[None]), axis=0)))
        for ct in range(COLS // 128):
            vrow[:, 128 * ct:128 * (ct + 1)] = jnp.broadcast_to(v[ct:ct + 1, :], (8, 128))

    def lane_max(rows):
        top = None
        for ct in range(COLS // 128):
            x = row_tile(rows, ct)
            top = x if top is None else jnp.maximum(top, x)
        return top

    def row_tile(rows, ct):
        cut = pl.ds(128 * ct, 128)
        x = scores[rows, cut].reshape(RB // 8, 8, 128) + vrow[:, cut][None]
        return x.reshape(RB, 128)

    def row_pass(step):
        rows = pl.ds(pl.multiple_of(step * RB, RB), RB)
        top = lane_max(rows)
        total = jnp.exp2(row_tile(rows, 0) - top)
        for ct in range(1, COLS // 128):
            total = total + jnp.exp2(row_tile(rows, ct) - top)
        mrow[rows, :] = top
        lrow[rows, :] = total

    def row_send_all(slot, shared):
        for k in range(NTGT):
            rows = slot128(k)
            if shared:
                high = jnp.transpose(mrow[rows, :])[0:1, :]
                total = jnp.transpose(lrow[rows, :])[0:1, :]
            else:
                tops = jnp.transpose(mrow[rows, :])
                high = jnp.max(tops, axis=0, keepdims=True)
                total = jnp.sum(jnp.transpose(lrow[rows, :]) * jnp.exp2(tops - high), axis=0, keepdims=True)
            rowx[slot, ti, k:k + 1, :] = high + jnp.log2(total)

        @pl.loop(1, NTGT)
        def _(d):
            to(rowx.at[slot, ti], rowx.at[slot, ti], row_send.at[slot], row_recv.at[slot], si, tgt_peer(d)).start()

    def row_combine(slot):
        most = rowx.at[slot, pl.ds(0, NTGT - 1)]
        pltpu.make_async_copy(most, most, row_recv.at[slot]).wait()
        every = rowx[slot]
        high = jnp.max(every, axis=0)
        rlse[...] = high + jnp.log2(jnp.sum(jnp.exp2(every - high[None]), axis=0))

    def row_expanded(k):
        row = rlse[pl.ds(k, 1), :]
        return jnp.transpose(jnp.broadcast_to(row, (128, 128)))

    @pl.loop(0, ROUNDS)
    def _(r):
        first, final = r == 0, r == ROUNDS - 1
        reset_cols()

        @pl.loop(0, ROWS // CH)
        def _(step):
            j = lax.rem(ti // 2 + ROWS // CH - step, ROWS // CH)
            rows = chunk(j)

            @pl.when(first)
            def _():
                for side in range(CH // OWN):
                    k = j * (CH // OWN) + side

                    @pl.when(k != ti)
                    def _():
                        land = sblk.at[slot128(k), :]
                        pltpu.make_async_copy(land, land, src_recv.at[k]).wait()

                sblk_t[:, rows] = jnp.transpose(sblk[rows, :])

            piece = sblk[rows, :]
            z = mm(jnp.concatenate([piece] * 3, axis=1), w3[...]).astype(BF16)
            scores[rows, :] = mm(z, feats_t[...]) * SCALE
            col_update(rows, False)

        col_exchange(2 * r)

        @pl.loop(0, ROWS // RB)
        def _(step):
            row_pass(step)

        row_send_all(2 * r, False)
        row_combine(2 * r)

        @pl.loop(0, NTGT)
        def _(k):
            ucol[slot128(k), :] = -LOG_N - row_expanded(k)

        reset_cols()

        @pl.loop(0, ROWS // CH)
        def _(j):
            col_update(chunk(j), True)

        col_exchange(2 * r + 1)

        @pl.loop(0, ROWS // RB)
        def _(step):
            rows = pl.ds(pl.multiple_of(step * RB, RB), RB)
            mrow[rows, :] = lane_max(rows)

        @pl.loop(0, ROWS // 512)
        def _(step):
            rows = pl.ds(pl.multiple_of(step * 512, 512), 512)
            mrow[rows, :] = jnp.broadcast_to(jnp.max(mrow[rows, :], axis=1, keepdims=True), (512, 128))

        @pl.loop(0, ROWS // CH)
        def _(turn):
            j = lax.rem(ti // 2 + turn, ROWS // CH)
            for step in range(CH // RB):
                rows = pl.ds(pl.multiple_of(j * CH + step * RB, RB), RB)
                top = mrow[rows, :]
                total = None
                for ct in range(COLS // 128):
                    p = jnp.exp2(row_tile(rows, ct) - top)
                    total = p if total is None else total + p
                    probs[step * RB:(step + 1) * RB, 128 * ct:128 * (ct + 1)] = p.astype(BF16)
                lrow[rows, :] = total

            rows = chunk(j)
            sums = jnp.broadcast_to(jnp.sum(lrow[rows, :], axis=1, keepdims=True), (CH, 128))
            lrow[rows, :] = sums
            image = mm(probs[...], feats[...])
            inverse = 1.0 / sums
            for cut in range(D // 128):
                lane = slice(128 * cut, 128 * (cut + 1))
                plan[rows, lane] = (image[:, lane] * inverse).astype(BF16)

            @pl.when(final)
            def _():
                for side in range(CH // OWN):
                    t = j * (CH // OWN) + side

                    @pl.when(t != ti)
                    def _():
                        to(plan.at[slot128(t), :], mvx.at[slot128(ti), :], mv_send, mv_recv, si, t).start()

        row_send_all(2 * r + 1, True)
        row_combine(2 * r + 1)

        @pl.loop(0, NTGT)
        def _(k):
            rows = slot128(k)
            factor = jnp.exp2(mrow[rows, :] + jnp.log2(lrow[rows, :]) - row_expanded(k))
            for cut in range(D // 128):
                lane = pl.ds(128 * cut, 128)
                planb[rows, lane] = (plan[rows, lane].astype(F32) * factor).astype(BF16)

        theirs = pl.ds(pl.multiple_of((1 - core) * 256, 256), 256)
        ours = pl.ds(pl.multiple_of(core * 256, 256), 256)
        mhold[r] = mm(sblk_t[theirs, :], planb[...]).astype(BF16)
        pair = to(mhold.at[r], sib1.at[r], ar_send.at[0, r], ar_recv.at[0, r], sibling, ti)
        pair.start()
        mine = mm(sblk_t[ours, :], planb[...])
        pair.wait_recv()
        mkeep[r] = (mine + sib1[r].astype(F32)).astype(BF16)

        def lot(k):
            return pl.ds(pl.multiple_of(k * 16, 16), 16)

        @pl.loop(1, NTGT)
        def _(d):
            t = tgt_peer(d)
            to(mkeep.at[r, lot(t), :], tgt1.at[r, ti], ar_send.at[1, r], ar_recv.at[1, r], si, t).start()

        tgt1[r, ti] = mkeep[r, lot(ti), :]
        most = tgt1.at[r, pl.ds(0, NTGT - 1)]
        pltpu.make_async_copy(most, most, ar_recv.at[1, r]).wait()
        zred[r, zed] = jnp.sum(tgt1[r].astype(F32), axis=0).astype(BF16)

        @pl.loop(1, 4)
        def _(d):
            other = lax.rem(zed + d, 4) * 2 + core
            to(zred.at[r, zed], zred.at[r, zed], ar_send.at[2, r], ar_recv.at[2, r], other, ti).start()

        most_z = zred.at[r, pl.ds(0, 3)]
        pltpu.make_async_copy(most_z, most_z, ar_recv.at[2, r]).wait()
        mhalf[r, lot(ti), :] = jnp.sum(zred[r].astype(F32), axis=0).astype(BF16)

        @pl.loop(1, NTGT)
        def _(d):
            to(mhalf.at[r, lot(ti), :], mhalf.at[r, lot(ti), :], ar_send.at[3, r], ar_recv.at[3, r],
               si, tgt_peer(d)).start()

        most_h = mhalf.at[r, pl.ds(0, 240), :]
        pltpu.make_async_copy(most_h, most_h, ar_recv.at[3, r]).wait()
        back = to(mhalf.at[r], mother.at[r], ar_send.at[4, r], ar_recv.at[4, r], sibling, ti)
        back.start()
        gbuf[ours, :] = mhalf[r].astype(F32)
        back.wait_recv()
        gbuf[theirs, :] = mother[r].astype(F32)

        cross = gbuf[...]
        spread = jnp.sqrt(jnp.mean(cross * cross, axis=(0, 1), keepdims=True) + 1e-06)
        g = cur[...] + 0.1 * cross / (spread * math.sqrt(D))
        gh, gl = split2(g)
        gth, gtl = jnp.transpose(gh), jnp.transpose(gl)
        gram = mm(jnp.concatenate([gth, gth, gtl], axis=1), jnp.concatenate([gh, gl, gh], axis=0))
        rh, rl = split2(gram)
        step = mm(jnp.concatenate([gh, gh, gl], axis=1), jnp.concatenate([rh, rl, rh], axis=0))
        new = 1.5 * g - 0.5 * step
        cur[...] = new

        @pl.when(jnp.logical_not(final))
        def _():
            for part, piece in enumerate(split3(cur[...])):
                w3[part * D:(part + 1) * D, :] = piece

        for slot in (2 * r, 2 * r + 1):
            seven = colx.at[slot, pl.ds(0, NSRC - 1)]
            pltpu.make_async_copy(seven, seven, col_send.at[slot]).wait()
            fifteen = rowx.at[slot, pl.ds(0, NTGT - 1)]
            pltpu.make_async_copy(fifteen, fifteen, row_send.at[slot]).wait()
        pair.wait_send()
        pltpu.make_async_copy(most, most, ar_send.at[1, r]).wait()
        pltpu.make_async_copy(most_z, most_z, ar_send.at[2, r]).wait()
        pltpu.make_async_copy(most_h, most_h, ar_send.at[3, r]).wait()
        back.wait_send()

    aligned[...] = 0.5 * cur[...]
    mvx[slot128(ti), :] = plan[slot128(ti), :]
    most_mv = mvx.at[pl.ds(0, ROWS - OWN), :]
    pltpu.make_async_copy(most_mv, most_mv, mv_recv).wait()
    moved[...] = jnp.zeros((OWN, D), F32)
    whole = rlse[pl.ds(ti, 1), :]

    @pl.loop(0, NTGT)
    def _(k):
        share = 0.5 * jnp.exp2(rowx[2 * ROUNDS - 1, k, pl.ds(ti, 1), :] - whole)
        factor = jnp.transpose(jnp.broadcast_to(share, (128, 128)))
        for cut in range(D // 128):
            lane = pl.ds(128 * cut, 128)
            moved[:, lane] = moved[:, lane] + mvx[slot128(k), lane].astype(F32) * factor

    pltpu.make_async_copy(most_mv, most_mv, mv_send).wait()
    pltpu.make_async_copy(most_tgt, most_tgt, tgt_send).wait()
    most_src = sblk.at[pl.ds(0, ROWS - OWN), :]
    pltpu.make_async_copy(most_src, most_src, src_send).wait()


def shards(source, target, rotation):
    vmem = pl.BlockSpec(memory_space=pltpu.VMEM)
    dma = pltpu.SemaphoreType.DMA
    v = pltpu.VMEM
    halves = pl.pallas_call(
        kernel,
        out_shape=(jax.ShapeDtypeStruct((D, D), F32), jax.ShapeDtypeStruct((OWN, D), F32)),
        in_specs=[vmem] * 3,
        out_specs=(vmem, vmem),
        scratch_shapes=[
            v((ROWS, D), BF16),
            v((D, ROWS), BF16),
            v((D, COLS), BF16),
            v((COLS, D), BF16),
            v((ROWS, COLS), F32),
            v((ROWS, D), BF16),
            v((ROWS, D), BF16),
            v((CH, COLS), BF16),
            v((ROWS, 128), F32),
            v((ROWS, 128), F32),
            v((ROWS, 128), F32),
            v((8, COLS), F32),
            v((8, COLS), F32),
            v((8, COLS), F32),
            v((3 * D, D), BF16),
            v((D, D), F32),
            v((4, NSRC, 8, 128), F32),
            v((4, NTGT, 16, 128), F32),
            v((2, 256, D), BF16),
            v((2, NTGT, 16, D), BF16),
            v((2, 4, 16, D), BF16),
            v((2, 256, D), BF16),
            v((2, 256, D), BF16),
            v((D, D), F32),
            v((ROWS, D), BF16),
            v((2, 256, D), BF16),
            v((2, 256, D), BF16),
            v((16, 128), F32),
            dma(()), dma((NTGT,)), dma(()), dma(()),
            dma((4,)), dma((4,)), dma((4,)), dma((4,)),
            dma((5, 2)), dma((5, 2)), dma(()), dma(()),
        ],
        compiler_params=pltpu.CompilerParams(
            collective_id=0, has_side_effects=True, vmem_limit_bytes=48 * 1024 * 1024),
    )(source, target.T, rotation)
    return tuple(2.0 * half for half in halves)


def solution(mesh):
    return jax.shard_map(
        shards, mesh=mesh, in_specs=(P(("src", "tgt"), None), P("tgt", "src"), P()),
        out_specs=(P(), P(("src", "tgt"), None)), check_vma=False)
```

```python
import functools
import math

import jax
import jax.numpy as jnp
from jax import lax
from jax.experimental import pallas as pl
from jax.experimental.pallas import tpu as pltpu
from jax.sharding import PartitionSpec as P

ROUNDS = 2
MESH = pl.DeviceIdType.MESH
F32, BF16 = jnp.float32, jnp.bfloat16
NSRC, NTGT = 8, 16
D = 512
OWN = 128
ROWS = 2048
COLS = 1024
CH = 256
RB = 32
LOG_N = 14.0
SCALE = 1.0 / math.sqrt(D) * math.log2(math.e)


def mm(a, b):
    return jnp.dot(a, b, preferred_element_type=F32)


def split3(w):
    hi = w.astype(BF16)
    rest = w - hi.astype(F32)
    mid = rest.astype(BF16)
    lo = (rest - mid.astype(F32)).astype(BF16)
    return hi, mid, lo


def split2(w):
    hi = w.astype(BF16)
    return hi, (w - hi.astype(F32)).astype(BF16)


def kernel(
    src_in, tgt_in, rot_in, aligned, moved,
    sblk, sblk_t, feats_t, feats, scores, plan, planb, probs, ucol, mrow, lrow,
    col_m, col_s, vrow, w3, cur, colx, rowx, sib1, tgt1, zred, mhalf, mother, gbuf, mvx, mhold, mkeep, rlse,
    src_send, src_recv, tgt_send, tgt_recv, col_send, col_recv, row_send_sem, row_recv,
    ar_send, ar_recv, mv_send, mv_recv,
):
    si, ti = lax.axis_index("src"), lax.axis_index("tgt")
    core, zed = lax.rem(si, 2), si // 2
    sibling = zed * 2 + 1 - core

    def tgt_peer(d):
        return lax.rem(ti + d, NTGT)

    def src_peer(d):
        return lax.rem(si + d, NSRC)

    barrier = pltpu.get_barrier_semaphore()

    @pl.loop(1, NTGT)
    def _(d):
        pl.semaphore_signal(barrier, inc=1, device_id=(si, tgt_peer(d)), device_id_type=MESH)

    @pl.loop(1, NSRC)
    def _(d):
        pl.semaphore_signal(barrier, inc=1, device_id=(src_peer(d), ti), device_id_type=MESH)

    pl.semaphore_wait(barrier, NTGT + NSRC - 2)

    def to(src, dst, send, recv, s, t):
        return pltpu.make_async_remote_copy(
            src_ref=src, dst_ref=dst, send_sem=send, recv_sem=recv,
            device_id=(s, t), device_id_type=MESH)

    def slot128(k):
        return pl.ds(pl.multiple_of(k * OWN, OWN), OWN)

    def slot64(k):
        return pl.ds(pl.multiple_of(k * 64, 64), 64)

    def z_peer(d):
        return lax.rem(zed + d, 4) * 2 + core

    for d in (1, 3, 2):
        to(tgt_in, feats_t.at[slot64(si), :], tgt_send, tgt_recv.at[si], z_peer(d), ti).start()
    to(tgt_in, feats_t.at[slot64(si), :], tgt_send, tgt_recv.at[si], sibling, ti).start()

    @pl.loop(1, NTGT)
    def _(d):
        to(src_in, sblk.at[slot128(ti), :], src_send, src_recv.at[ti], si, tgt_peer(d)).start()

    sblk[slot128(ti), :] = src_in[...]
    feats_t[slot64(si), :] = tgt_in[...]
    cur[...] = rot_in[...]
    for part, piece in enumerate(split3(rot_in[...])):
        w3[part * D:(part + 1) * D, :] = piece

    most_tgt = feats_t.at[pl.ds(0, D - 64), :]
    for d in (1, 3, 2):
        land = feats_t.at[slot64(z_peer(d)), :]
        pltpu.make_async_copy(land, land, tgt_recv.at[z_peer(d)]).wait()
        to(land, land, tgt_send, tgt_recv.at[z_peer(d)], sibling, ti).start()
    for d in range(4):
        k = lax.rem(zed + d, 4) * 2 + 1 - core
        land = feats_t.at[slot64(k), :]
        pltpu.make_async_copy(land, land, tgt_recv.at[k]).wait()
    for part in range(D // 128):
        feats[:, 128 * part:128 * (part + 1)] = jnp.transpose(feats_t[128 * part:128 * (part + 1), :])

    def chunk(j):
        return pl.ds(pl.multiple_of(j * CH, CH), CH)

    def reset_cols():
        col_m[...] = jnp.full((8, COLS), -jnp.inf, F32)
        col_s[...] = jnp.zeros((8, COLS), F32)

    def col_update(rows, shifted):
        for ct in range(COLS // 128):
            cut = pl.ds(128 * ct, 128)
            x = scores[rows, cut]
            if shifted:
                x = x + ucol[rows, :]
            x = x.reshape(CH // 8, 8, 128)
            old = col_m[:, cut]
            new = jnp.maximum(old, jnp.max(x, axis=0))
            col_s[:, cut] = col_s[:, cut] * jnp.exp2(old - new) + jnp.sum(jnp.exp2(x - new[None]), axis=0)
            col_m[:, cut] = new

    def col_exchange(slot):
        for ct in range(COLS // 128):
            cut = pl.ds(128 * ct, 128)
            high = jnp.max(col_m[:, cut], axis=0, keepdims=True)
            total = jnp.sum(col_s[:, cut] * jnp.exp2(col_m[:, cut] - high), axis=0, keepdims=True)
            colx[slot, si, ct:ct + 1, :] = high + jnp.log2(total)

        @pl.loop(1, NSRC)
        def _(d):
            to(colx.at[slot, si], colx.at[slot, si], col_send.at[slot], col_recv.at[slot], src_peer(d), ti).start()

        seven = colx.at[slot, pl.ds(0, NSRC - 1)]
        pltpu.make_async_copy(seven, seven, col_recv.at[slot]).wait()
        every = colx[slot]
        high = jnp.max(every, axis=0)
        v = -LOG_N - (high + jnp.log2(jnp.sum(jnp.exp2(every - high[None]), axis=0)))
        for ct in range(COLS // 128):
            vrow[:, 128 * ct:128 * (ct + 1)] = jnp.broadcast_to(v[ct:ct + 1, :], (8, 128))

    def lane_max(rows):
        top = None
        for ct in range(COLS // 128):
            x = row_tile(rows, ct)
            top = x if top is None else jnp.maximum(top, x)
        return top

    def row_tile(rows, ct):
        cut = pl.ds(128 * ct, 128)
        x = scores[rows, cut].reshape(RB // 8, 8, 128) + vrow[:, cut][None]
        return x.reshape(RB, 128)

    def row_pass(step):
        rows = pl.ds(pl.multiple_of(step * RB, RB), RB)
        top = lane_max(rows)
        total = jnp.exp2(row_tile(rows, 0) - top)
        for ct in range(1, COLS // 128):
            total = total + jnp.exp2(row_tile(rows, ct) - top)
        mrow[rows, :] = top
        lrow[rows, :] = total

    def row_send(slot, half, shared):
        for k in range(8 * half, 8 * half + 8):
            rows = slot128(k)
            if shared:
                high = jnp.transpose(mrow[rows, :])[0:1, :]
                total = jnp.transpose(lrow[rows, :])[0:1, :]
            else:
                tops = jnp.transpose(mrow[rows, :])
                high = jnp.max(tops, axis=0, keepdims=True)
                total = jnp.sum(jnp.transpose(lrow[rows, :]) * jnp.exp2(tops - high), axis=0, keepdims=True)
            rowx[slot, ti, k:k + 1, :] = high + jnp.log2(total)

        own = rowx.at[slot, ti, pl.ds(8 * half, 8), :]

        @pl.loop(1, NTGT)
        def _(d):
            to(own, own, row_send_sem.at[slot, half], row_recv.at[slot, half], si, tgt_peer(d)).start()

    def row_most(slot, half):
        return rowx.at[slot, pl.ds(0, NTGT - 1), pl.ds(8 * half, 8), :]

    def row_combine(slot, half):
        most = row_most(slot, half)
        pltpu.make_async_copy(most, most, row_recv.at[slot, half]).wait()
        every = rowx[slot, :, 8 * half:8 * half + 8, :]
        high = jnp.max(every, axis=0)
        rlse[8 * half:8 * half + 8, :] = high + jnp.log2(jnp.sum(jnp.exp2(every - high[None]), axis=0))

    def row_expanded(k):
        row = rlse[pl.ds(k, 1), :]
        return jnp.transpose(jnp.broadcast_to(row, (128, 128)))

    @pl.loop(0, ROUNDS)
    def _(r):
        first, final = r == 0, r == ROUNDS - 1
        reset_cols()

        @pl.loop(0, ROWS // CH)
        def _(step):
            j = lax.rem(ti // 2 + ROWS // CH - step, ROWS // CH)
            rows = chunk(j)

            @pl.when(first)
            def _():
                for side in range(CH // OWN):
                    k = j * (CH // OWN) + side

                    @pl.when(k != ti)
                    def _():
                        land = sblk.at[slot128(k), :]
                        pltpu.make_async_copy(land, land, src_recv.at[k]).wait()

                sblk_t[:, rows] = jnp.transpose(sblk[rows, :])

            piece = sblk[rows, :]
            z = mm(jnp.concatenate([piece] * 3, axis=1), w3[...]).astype(BF16)
            scores[rows, :] = mm(z, feats_t[...]) * SCALE
            col_update(rows, False)

        col_exchange(2 * r)

        for half in range(2):
            @pl.loop(half * ROWS // RB // 2, (half + 1) * ROWS // RB // 2)
            def _(step):
                row_pass(step)

            row_send(2 * r, half, False)

        reset_cols()
        for half in range(2):
            row_combine(2 * r, half)
            for k in range(8 * half, 8 * half + 8):
                ucol[slot128(k), :] = -LOG_N - row_expanded(k)

            @pl.loop(half * ROWS // CH // 2, (half + 1) * ROWS // CH // 2)
            def _(j):
                col_update(chunk(j), True)

        col_exchange(2 * r + 1)

        @pl.loop(0, ROWS // RB)
        def _(step):
            rows = pl.ds(pl.multiple_of(step * RB, RB), RB)
            mrow[rows, :] = lane_max(rows)

        @pl.loop(0, ROWS // 512)
        def _(step):
            rows = pl.ds(pl.multiple_of(step * 512, 512), 512)
            mrow[rows, :] = jnp.broadcast_to(jnp.max(mrow[rows, :], axis=1, keepdims=True), (512, 128))

        def images(j):
            for step in range(CH // RB):
                rows = pl.ds(pl.multiple_of(j * CH + step * RB, RB), RB)
                top = mrow[rows, :]
                total = None
                for ct in range(COLS // 128):
                    p = jnp.exp2(row_tile(rows, ct) - top)
                    total = p if total is None else total + p
                    probs[step * RB:(step + 1) * RB, 128 * ct:128 * (ct + 1)] = p.astype(BF16)
                lrow[rows, :] = total

            rows = chunk(j)
            sums = jnp.broadcast_to(jnp.sum(lrow[rows, :], axis=1, keepdims=True), (CH, 128))
            lrow[rows, :] = sums
            image = mm(probs[...], feats[...])
            inverse = 1.0 / sums
            for cut in range(D // 128):
                lane = slice(128 * cut, 128 * (cut + 1))
                plan[rows, lane] = (image[:, lane] * inverse).astype(BF16)

        for half in range(2):
            pl.loop(half * ROWS // CH // 2, (half + 1) * ROWS // CH // 2)(images)
            row_send(2 * r + 1, half, True)

        def send_images(offsets):
            @pl.when(final)
            def _():
                for dy, dx in offsets:
                    t = lax.rem(ti // 4 + dy, 4) * 4 + lax.rem(ti + dx, 4)
                    to(plan.at[slot128(t), :], mvx.at[slot128(ti), :], mv_send, mv_recv, si, t).start()

        send_images(((0, 1), (0, 3), (1, 0), (3, 0), (1, 1), (3, 3), (1, 3), (3, 1)))
        for half in range(2):
            row_combine(2 * r + 1, half)
            for k in range(8 * half, 8 * half + 8):
                rows = slot128(k)
                factor = jnp.exp2(mrow[rows, :] + jnp.log2(lrow[rows, :]) - row_expanded(k))
                for cut in range(D // 128):
                    lane = pl.ds(128 * cut, 128)
                    planb[rows, lane] = (plan[rows, lane].astype(F32) * factor).astype(BF16)

        theirs = pl.ds(pl.multiple_of((1 - core) * 256, 256), 256)
        ours = pl.ds(pl.multiple_of(core * 256, 256), 256)
        mhold[r] = mm(sblk_t[theirs, :], planb[...]).astype(BF16)
        pair = to(mhold.at[r], sib1.at[r], ar_send.at[0, r], ar_recv.at[0, r], sibling, ti)
        pair.start()
        mine = mm(sblk_t[ours, :], planb[...])
        pair.wait_recv()
        mkeep[r] = (mine + sib1[r].astype(F32)).astype(BF16)

        def lot(k):
            return pl.ds(pl.multiple_of(k * 16, 16), 16)

        @pl.loop(1, NTGT)
        def _(d):
            t = tgt_peer(d)
            to(mkeep.at[r, lot(t), :], tgt1.at[r, ti], ar_send.at[1, r], ar_recv.at[1, r], si, t).start()

        send_images(((0, 2), (2, 0), (2, 2)))
        tgt1[r, ti] = mkeep[r, lot(ti), :]
        most = tgt1.at[r, pl.ds(0, NTGT - 1)]
        pltpu.make_async_copy(most, most, ar_recv.at[1, r]).wait()
        zred[r, zed] = jnp.sum(tgt1[r].astype(F32), axis=0).astype(BF16)

        @pl.loop(1, 4)
        def _(d):
            other = lax.rem(zed + d, 4) * 2 + core
            to(zred.at[r, zed], zred.at[r, zed], ar_send.at[2, r], ar_recv.at[2, r], other, ti).start()

        most_z = zred.at[r, pl.ds(0, 3)]
        pltpu.make_async_copy(most_z, most_z, ar_recv.at[2, r]).wait()
        mhalf[r, lot(ti), :] = jnp.sum(zred[r].astype(F32), axis=0).astype(BF16)

        @pl.loop(1, NTGT)
        def _(d):
            to(mhalf.at[r, lot(ti), :], mhalf.at[r, lot(ti), :], ar_send.at[3, r], ar_recv.at[3, r],
               si, tgt_peer(d)).start()

        send_images(((1, 2), (3, 2), (2, 1), (2, 3)))
        most_h = mhalf.at[r, pl.ds(0, 240), :]
        pltpu.make_async_copy(most_h, most_h, ar_recv.at[3, r]).wait()
        back = to(mhalf.at[r], mother.at[r], ar_send.at[4, r], ar_recv.at[4, r], sibling, ti)
        back.start()
        gbuf[ours, :] = mhalf[r].astype(F32)
        back.wait_recv()
        gbuf[theirs, :] = mother[r].astype(F32)

        cross = gbuf[...]
        spread = jnp.sqrt(jnp.mean(cross * cross, axis=(0, 1), keepdims=True) + 1e-06)
        g = cur[...] + 0.1 * cross / (spread * math.sqrt(D))
        gh, gl = split2(g)
        gth, gtl = jnp.transpose(gh), jnp.transpose(gl)
        gram = mm(jnp.concatenate([gth, gth, gtl], axis=1), jnp.concatenate([gh, gl, gh], axis=0))
        rh, rl = split2(gram)
        step = mm(jnp.concatenate([gh, gh, gl], axis=1), jnp.concatenate([rh, rl, rh], axis=0))
        new = 1.5 * g - 0.5 * step
        cur[...] = new

        @pl.when(jnp.logical_not(final))
        def _():
            for part, piece in enumerate(split3(cur[...])):
                w3[part * D:(part + 1) * D, :] = piece

        for slot in (2 * r, 2 * r + 1):
            seven = colx.at[slot, pl.ds(0, NSRC - 1)]
            pltpu.make_async_copy(seven, seven, col_send.at[slot]).wait()
            for half in range(2):
                most_r = row_most(slot, half)
                pltpu.make_async_copy(most_r, most_r, row_send_sem.at[slot, half]).wait()
        pair.wait_send()
        pltpu.make_async_copy(most, most, ar_send.at[1, r]).wait()
        pltpu.make_async_copy(most_z, most_z, ar_send.at[2, r]).wait()
        pltpu.make_async_copy(most_h, most_h, ar_send.at[3, r]).wait()
        back.wait_send()

    aligned[...] = 0.5 * cur[...]
    mvx[slot128(ti), :] = plan[slot128(ti), :]
    most_mv = mvx.at[pl.ds(0, ROWS - OWN), :]
    pltpu.make_async_copy(most_mv, most_mv, mv_recv).wait()
    moved[...] = jnp.zeros((OWN, D), F32)
    whole = rlse[pl.ds(ti, 1), :]

    @pl.loop(0, NTGT)
    def _(k):
        share = 0.5 * jnp.exp2(rowx[2 * ROUNDS - 1, k, pl.ds(ti, 1), :] - whole)
        factor = jnp.transpose(jnp.broadcast_to(share, (128, 128)))
        for cut in range(D // 128):
            lane = pl.ds(128 * cut, 128)
            moved[:, lane] = moved[:, lane] + mvx[slot128(k), lane].astype(F32) * factor

    pltpu.make_async_copy(most_mv, most_mv, mv_send).wait()
    pltpu.make_async_copy(most_tgt, most_tgt, tgt_send).wait()
    most_src = sblk.at[pl.ds(0, ROWS - OWN), :]
    pltpu.make_async_copy(most_src, most_src, src_send).wait()


def shards(source, target, rotation):
    vmem = pl.BlockSpec(memory_space=pltpu.VMEM)
    dma = pltpu.SemaphoreType.DMA
    v = pltpu.VMEM
    halves = pl.pallas_call(
        kernel,
        out_shape=(jax.ShapeDtypeStruct((D, D), F32), jax.ShapeDtypeStruct((OWN, D), F32)),
        in_specs=[vmem] * 3,
        out_specs=(vmem, vmem),
        scratch_shapes=[
            v((ROWS, D), BF16),
            v((D, ROWS), BF16),
            v((D, COLS), BF16),
            v((COLS, D), BF16),
            v((ROWS, COLS), F32),
            v((ROWS, D), BF16),
            v((ROWS, D), BF16),
            v((CH, COLS), BF16),
            v((ROWS, 128), F32),
            v((ROWS, 128), F32),
            v((ROWS, 128), F32),
            v((8, COLS), F32),
            v((8, COLS), F32),
            v((8, COLS), F32),
            v((3 * D, D), BF16),
            v((D, D), F32),
            v((4, NSRC, 8, 128), F32),
            v((4, NTGT, 16, 128), F32),
            v((2, 256, D), BF16),
            v((2, NTGT, 16, D), BF16),
            v((2, 4, 16, D), BF16),
            v((2, 256, D), BF16),
            v((2, 256, D), BF16),
            v((D, D), F32),
            v((ROWS, D), BF16),
            v((2, 256, D), BF16),
            v((2, 256, D), BF16),
            v((16, 128), F32),
            dma(()), dma((NTGT,)), dma(()), dma((NSRC,)),
            dma((4,)), dma((4,)), dma((4, 2)), dma((4, 2)),
            dma((5, 2)), dma((5, 2)), dma(()), dma(()),
        ],
        compiler_params=pltpu.CompilerParams(
            collective_id=0, has_side_effects=True, vmem_limit_bytes=48 * 1024 * 1024),
    )(source, target.T, rotation)
    return tuple(2.0 * half for half in halves)


def solution(mesh):
    return jax.shard_map(
        shards, mesh=mesh, in_specs=(P(("src", "tgt"), None), P("tgt", "src"), P()),
        out_specs=(P(), P(("src", "tgt"), None)), check_vma=False)
```

```python
import functools
import math

import jax
import jax.numpy as jnp
from jax import lax
from jax.experimental import pallas as pl
from jax.experimental.pallas import tpu as pltpu
from jax.sharding import PartitionSpec as P

ROUNDS = 2
MESH = pl.DeviceIdType.MESH
F32, BF16 = jnp.float32, jnp.bfloat16
NSRC, NTGT = 8, 16
D = 512
OWN = 128
ROWS = 2048
COLS = 1024
CH = 256
RB = 32
LOG_N = 14.0
SCALE = 1.0 / math.sqrt(D) * math.log2(math.e)


def mm(a, b):
    return jnp.dot(a, b, preferred_element_type=F32)


def split3(w):
    hi = w.astype(BF16)
    rest = w - hi.astype(F32)
    mid = rest.astype(BF16)
    lo = (rest - mid.astype(F32)).astype(BF16)
    return hi, mid, lo


def split2(w):
    hi = w.astype(BF16)
    return hi, (w - hi.astype(F32)).astype(BF16)


def kernel(
    src_in, tgt_in, rot_in, aligned, moved,
    sblk, sblk_t, feats_t, feats, scores, plan, planb, probs, ucol, mrow, lrow,
    col_m, col_s, vrow, w3, cur, colx, rowx, sib1, tgt1, zred, mhalf, mother, gbuf, mvx, mhold, mkeep, rlse,
    src_send, near, far, tgt_send, tgt_recv, col_send, col_recv, row_send_sem, row_recv,
    ar_send, ar_recv, mv_send, mv_recv,
):
    si, ti = lax.axis_index("src"), lax.axis_index("tgt")
    core, zed = lax.rem(si, 2), si // 2
    sibling = zed * 2 + 1 - core
    ty, tx = ti // 4, lax.rem(ti, 4)
    across = 4 * tx + ty

    def tgt_peer(d):
        return lax.rem(ti + d, NTGT)

    def src_peer(d):
        return lax.rem(si + d, NSRC)

    barrier = pltpu.get_barrier_semaphore()

    @pl.loop(1, NTGT)
    def _(d):
        pl.semaphore_signal(barrier, inc=1, device_id=(si, tgt_peer(d)), device_id_type=MESH)

    @pl.loop(1, NSRC)
    def _(d):
        pl.semaphore_signal(barrier, inc=1, device_id=(src_peer(d), ti), device_id_type=MESH)

    pl.semaphore_wait(barrier, NTGT + NSRC - 2)

    def to(src, dst, send, recv, s, t):
        return pltpu.make_async_remote_copy(
            src_ref=src, dst_ref=dst, send_sem=send, recv_sem=recv,
            device_id=(s, t), device_id_type=MESH)

    def slot128(k):
        return pl.ds(pl.multiple_of(k * OWN, OWN), OWN)

    def slot64(k):
        return pl.ds(pl.multiple_of(k * 64, 64), 64)

    def beside(c, d):
        return lax.rem(c + d, 4)

    x_ways = [(si, 4 * ty + beside(tx, d)) for d in (1, 3)]
    y_ways = [(si, 4 * beside(ty, d) + tx) for d in (1, 3)]
    z_ways = [(2 * beside(zed, d) + core, ti) for d in (1, 3)]

    def both_ways(ring, src, dst, ways, send):
        for side in range(2):
            to(src, dst, send, near.at[ring, side], *ways[side]).start()

    def relay(ring, ref, at, count, c, ways, send, after):
        for side, k in ((0, beside(c, 3)), (1, beside(c, 1))):
            land = ref.at[pl.ds(pl.multiple_of(at(k), count), count), :]
            pltpu.make_async_copy(land, land, near.at[ring, side]).wait()
            half = ref.at[pl.ds(pl.multiple_of(at(k) + side * (count // 2), count // 2), count // 2), :]
            to(half, half, send, far.at[ring, side], *ways[side]).start()
            after(land, k)

    def relayed(ring, ref, at, count, c, after):
        k = beside(c, 2)
        for side in range(2):
            half = ref.at[pl.ds(pl.multiple_of(at(k) + side * (count // 2), count // 2), count // 2), :]
            pltpu.make_async_copy(half, half, far.at[ring, side]).wait()
        after(ref.at[pl.ds(pl.multiple_of(at(k), count), count), :], k)

    def nothing(land, k):
        pass

    upper, lower = src_in.at[pl.ds(0, 64), :], src_in.at[pl.ds(64, 64), :]
    own_up, own_low = sblk.at[slot64(ti), :], sblk.at[slot64(16 + across), :]
    own_feats = feats_t.at[slot64(si), :]
    both_ways(2, tgt_in, own_feats, z_ways, tgt_send)
    both_ways(0, upper, own_up, x_ways, src_send)
    both_ways(1, lower, own_low, y_ways, src_send)
    both_ways(3, upper, own_up, y_ways, src_send)
    both_ways(4, lower, own_low, x_ways, src_send)
    to(tgt_in, own_feats, tgt_send, tgt_recv.at[zed], sibling, ti).start()

    sblk[slot64(ti), :] = src_in[0:64, :]
    sblk[slot64(16 + across), :] = src_in[64:128, :]
    feats_t[slot64(si), :] = tgt_in[...]
    cur[...] = rot_in[...]
    for part, piece in enumerate(split3(rot_in[...])):
        w3[part * D:(part + 1) * D, :] = piece

    def up_on(land, k):
        both_ways(3, land, land, y_ways, src_send)

    def low_on(land, k):
        both_ways(4, land, land, x_ways, src_send)

    def to_sibling(land, k):
        to(land, land, tgt_send, tgt_recv.at[k], sibling, ti).start()

    def up_at(k):
        return 64 * (4 * ty + k)

    def low_at(k):
        return ROWS // 2 + 64 * (4 * tx + k)

    def feats_at(k):
        return 64 * (2 * k + core)

    relay(0, sblk, up_at, 64, tx, x_ways, src_send, up_on)
    relay(1, sblk, low_at, 64, ty, y_ways, src_send, low_on)
    relay(2, feats_t, feats_at, 64, zed, z_ways, tgt_send, to_sibling)
    relayed(0, sblk, up_at, 64, tx, up_on)
    relayed(1, sblk, low_at, 64, ty, low_on)
    relayed(2, feats_t, feats_at, 64, zed, to_sibling)
    for k in range(4):
        land = feats_t.at[slot64(2 * k + 1 - core), :]
        pltpu.make_async_copy(land, land, tgt_recv.at[k]).wait()
    most_tgt = feats_t.at[pl.ds(0, D - 64), :]
    for part in range(D // 128):
        feats[:, 128 * part:128 * (part + 1)] = jnp.transpose(feats_t[128 * part:128 * (part + 1), :])

    def chunk(j):
        return pl.ds(pl.multiple_of(j * CH, CH), CH)

    def reset_cols():
        col_m[...] = jnp.full((8, COLS), -jnp.inf, F32)
        col_s[...] = jnp.zeros((8, COLS), F32)

    def col_update(rows, shifted):
        for ct in range(COLS // 128):
            cut = pl.ds(128 * ct, 128)
            x = scores[rows, cut]
            if shifted:
                x = x + ucol[rows, :]
            x = x.reshape(CH // 8, 8, 128)
            old = col_m[:, cut]
            new = jnp.maximum(old, jnp.max(x, axis=0))
            col_s[:, cut] = col_s[:, cut] * jnp.exp2(old - new) + jnp.sum(jnp.exp2(x - new[None]), axis=0)
            col_m[:, cut] = new

    def col_exchange(slot):
        for ct in range(COLS // 128):
            cut = pl.ds(128 * ct, 128)
            high = jnp.max(col_m[:, cut], axis=0, keepdims=True)
            total = jnp.sum(col_s[:, cut] * jnp.exp2(col_m[:, cut] - high), axis=0, keepdims=True)
            colx[slot, si, ct:ct + 1, :] = high + jnp.log2(total)

        @pl.loop(1, NSRC)
        def _(d):
            to(colx.at[slot, si], colx.at[slot, si], col_send.at[slot], col_recv.at[slot], src_peer(d), ti).start()

        seven = colx.at[slot, pl.ds(0, NSRC - 1)]
        pltpu.make_async_copy(seven, seven, col_recv.at[slot]).wait()
        every = colx[slot]
        high = jnp.max(every, axis=0)
        v = -LOG_N - (high + jnp.log2(jnp.sum(jnp.exp2(every - high[None]), axis=0)))
        for ct in range(COLS // 128):
            vrow[:, 128 * ct:128 * (ct + 1)] = jnp.broadcast_to(v[ct:ct + 1, :], (8, 128))

    def lane_max(rows):
        top = None
        for ct in range(COLS // 128):
            x = row_tile(rows, ct)
            top = x if top is None else jnp.maximum(top, x)
        return top

    def row_tile(rows, ct):
        cut = pl.ds(128 * ct, 128)
        x = scores[rows, cut].reshape(RB // 8, 8, 128) + vrow[:, cut][None]
        return x.reshape(RB, 128)

    def row_pass(step):
        rows = pl.ds(pl.multiple_of(step * RB, RB), RB)
        top = lane_max(rows)
        total = jnp.exp2(row_tile(rows, 0) - top)
        for ct in range(1, COLS // 128):
            total = total + jnp.exp2(row_tile(rows, ct) - top)
        mrow[rows, :] = top
        lrow[rows, :] = total

    def row_send(slot, half, shared):
        for k in range(8 * half, 8 * half + 8):
            rows = slot128(k)
            if shared:
                high = jnp.transpose(mrow[rows, :])[0:1, :]
                total = jnp.transpose(lrow[rows, :])[0:1, :]
            else:
                tops = jnp.transpose(mrow[rows, :])
                high = jnp.max(tops, axis=0, keepdims=True)
                total = jnp.sum(jnp.transpose(lrow[rows, :]) * jnp.exp2(tops - high), axis=0, keepdims=True)
            rowx[slot, ti, k:k + 1, :] = high + jnp.log2(total)

        own = rowx.at[slot, ti, pl.ds(8 * half, 8), :]

        @pl.loop(1, NTGT)
        def _(d):
            to(own, own, row_send_sem.at[slot, half], row_recv.at[slot, half], si, tgt_peer(d)).start()

    def row_most(slot, half):
        return rowx.at[slot, pl.ds(0, NTGT - 1), pl.ds(8 * half, 8), :]

    def row_combine(slot, half):
        most = row_most(slot, half)
        pltpu.make_async_copy(most, most, row_recv.at[slot, half]).wait()
        every = rowx[slot, :, 8 * half:8 * half + 8, :]
        high = jnp.max(every, axis=0)
        rlse[8 * half:8 * half + 8, :] = high + jnp.log2(jnp.sum(jnp.exp2(every - high[None]), axis=0))

    def row_expanded(k):
        row = rlse[pl.ds(k, 1), :]
        return jnp.transpose(jnp.broadcast_to(row, (128, 128)))

    @pl.loop(0, ROUNDS)
    def _(r):
        first, final = r == 0, r == ROUNDS - 1
        reset_cols()

        @pl.loop(0, ROWS // CH)
        def _(step):
            phase, kind = step // 2, lax.rem(step, 2)
            start = ty + kind * (tx - ty)
            j = 4 * kind + lax.rem(start + phase + phase // 2 - 2 * (phase // 3), 4)
            rows = chunk(j)

            @pl.when(jnp.logical_and(first, step == 2))
            def _():
                relay(3, sblk, lambda k: CH * k, CH, ty, y_ways, src_send, nothing)
                relay(4, sblk, lambda k: ROWS // 2 + CH * k, CH, tx, x_ways, src_send, nothing)

            @pl.when(jnp.logical_and(first, step == 6))
            def _():
                relayed(3, sblk, lambda k: CH * k, CH, ty, nothing)
                relayed(4, sblk, lambda k: ROWS // 2 + CH * k, CH, tx, nothing)

            @pl.when(first)
            def _():
                sblk_t[:, rows] = jnp.transpose(sblk[rows, :])

            piece = sblk[rows, :]
            z = mm(jnp.concatenate([piece] * 3, axis=1), w3[...]).astype(BF16)
            scores[rows, :] = mm(z, feats_t[...]) * SCALE
            col_update(rows, False)

        col_exchange(2 * r)

        for half in range(2):
            @pl.loop(half * ROWS // RB // 2, (half + 1) * ROWS // RB // 2)
            def _(step):
                row_pass(step)

            row_send(2 * r, half, False)

        reset_cols()
        for half in range(2):
            row_combine(2 * r, half)
            for k in range(8 * half, 8 * half + 8):
                ucol[slot128(k), :] = -LOG_N - row_expanded(k)

            @pl.loop(half * ROWS // CH // 2, (half + 1) * ROWS // CH // 2)
            def _(j):
                col_update(chunk(j), True)

        col_exchange(2 * r + 1)

        @pl.loop(0, ROWS // RB)
        def _(step):
            rows = pl.ds(pl.multiple_of(step * RB, RB), RB)
            mrow[rows, :] = lane_max(rows)

        @pl.loop(0, ROWS // 512)
        def _(step):
            rows = pl.ds(pl.multiple_of(step * 512, 512), 512)
            mrow[rows, :] = jnp.broadcast_to(jnp.max(mrow[rows, :], axis=1, keepdims=True), (512, 128))

        def images(j):
            for step in range(CH // RB):
                rows = pl.ds(pl.multiple_of(j * CH + step * RB, RB), RB)
                top = mrow[rows, :]
                total = None
                for ct in range(COLS // 128):
                    p = jnp.exp2(row_tile(rows, ct) - top)
                    total = p if total is None else total + p
                    probs[step * RB:(step + 1) * RB, 128 * ct:128 * (ct + 1)] = p.astype(BF16)
                lrow[rows, :] = total

            rows = chunk(j)
            sums = jnp.broadcast_to(jnp.sum(lrow[rows, :], axis=1, keepdims=True), (CH, 128))
            lrow[rows, :] = sums
            image = mm(probs[...], feats[...])
            inverse = 1.0 / sums
            for cut in range(D // 128):
                lane = slice(128 * cut, 128 * (cut + 1))
                plan[rows, lane] = (image[:, lane] * inverse).astype(BF16)

        for half in range(2):
            pl.loop(half * ROWS // CH // 2, (half + 1) * ROWS // CH // 2)(images)
            row_send(2 * r + 1, half, True)

        def send_images(offsets):
            @pl.when(final)
            def _():
                for dy, dx in offsets:
                    y, x = beside(ty, dy), beside(tx, dx)
                    for src, dst in ((4 * y + x, ti), (16 + 4 * x + y, 16 + ti)):
                        to(plan.at[slot64(src), :], mvx.at[slot64(dst), :], mv_send, mv_recv, si, 4 * y + x).start()

        send_images(((0, 1), (0, 3), (1, 0), (3, 0), (1, 1), (3, 3), (1, 3), (3, 1)))
        for half in range(2):
            row_combine(2 * r + 1, half)
            for k in range(8 * half, 8 * half + 8):
                rows = slot128(k)
                factor = jnp.exp2(mrow[rows, :] + jnp.log2(lrow[rows, :]) - row_expanded(k))
                for cut in range(D // 128):
                    lane = pl.ds(128 * cut, 128)
                    planb[rows, lane] = (plan[rows, lane].astype(F32) * factor).astype(BF16)

        theirs = pl.ds(pl.multiple_of((1 - core) * 256, 256), 256)
        ours = pl.ds(pl.multiple_of(core * 256, 256), 256)
        mhold[r] = mm(sblk_t[theirs, :], planb[...]).astype(BF16)
        pair = to(mhold.at[r], sib1.at[r], ar_send.at[0, r], ar_recv.at[0, r], sibling, ti)
        pair.start()
        mine = mm(sblk_t[ours, :], planb[...])
        pair.wait_recv()
        mkeep[r] = (mine + sib1[r].astype(F32)).astype(BF16)

        def lot(k):
            return pl.ds(pl.multiple_of(k * 16, 16), 16)

        @pl.loop(1, NTGT)
        def _(d):
            t = tgt_peer(d)
            to(mkeep.at[r, lot(t), :], tgt1.at[r, ti], ar_send.at[1, r], ar_recv.at[1, r], si, t).start()

        send_images(((0, 2), (2, 0), (2, 2)))
        tgt1[r, ti] = mkeep[r, lot(ti), :]
        most = tgt1.at[r, pl.ds(0, NTGT - 1)]
        pltpu.make_async_copy(most, most, ar_recv.at[1, r]).wait()
        zred[r, zed] = jnp.sum(tgt1[r].astype(F32), axis=0).astype(BF16)

        @pl.loop(1, 4)
        def _(d):
            other = lax.rem(zed + d, 4) * 2 + core
            to(zred.at[r, zed], zred.at[r, zed], ar_send.at[2, r], ar_recv.at[2, r], other, ti).start()

        most_z = zred.at[r, pl.ds(0, 3)]
        pltpu.make_async_copy(most_z, most_z, ar_recv.at[2, r]).wait()
        mhalf[r, lot(ti), :] = jnp.sum(zred[r].astype(F32), axis=0).astype(BF16)

        @pl.loop(1, NTGT)
        def _(d):
            to(mhalf.at[r, lot(ti), :], mhalf.at[r, lot(ti), :], ar_send.at[3, r], ar_recv.at[3, r],
               si, tgt_peer(d)).start()

        send_images(((1, 2), (3, 2), (2, 1), (2, 3)))
        most_h = mhalf.at[r, pl.ds(0, 240), :]
        pltpu.make_async_copy(most_h, most_h, ar_recv.at[3, r]).wait()
        back = to(mhalf.at[r], mother.at[r], ar_send.at[4, r], ar_recv.at[4, r], sibling, ti)
        back.start()
        gbuf[ours, :] = mhalf[r].astype(F32)
        back.wait_recv()
        gbuf[theirs, :] = mother[r].astype(F32)

        cross = gbuf[...]
        spread = jnp.sqrt(jnp.mean(cross * cross, axis=(0, 1), keepdims=True) + 1e-06)
        g = cur[...] + 0.1 * cross / (spread * math.sqrt(D))
        gh, gl = split2(g)
        gth, gtl = jnp.transpose(gh), jnp.transpose(gl)
        gram = mm(jnp.concatenate([gth, gth, gtl], axis=1), jnp.concatenate([gh, gl, gh], axis=0))
        rh, rl = split2(gram)
        step = mm(jnp.concatenate([gh, gh, gl], axis=1), jnp.concatenate([rh, rl, rh], axis=0))
        new = 1.5 * g - 0.5 * step
        cur[...] = new

        @pl.when(jnp.logical_not(final))
        def _():
            for part, piece in enumerate(split3(cur[...])):
                w3[part * D:(part + 1) * D, :] = piece

        for slot in (2 * r, 2 * r + 1):
            seven = colx.at[slot, pl.ds(0, NSRC - 1)]
            pltpu.make_async_copy(seven, seven, col_send.at[slot]).wait()
            for half in range(2):
                most_r = row_most(slot, half)
                pltpu.make_async_copy(most_r, most_r, row_send_sem.at[slot, half]).wait()
        pair.wait_send()
        pltpu.make_async_copy(most, most, ar_send.at[1, r]).wait()
        pltpu.make_async_copy(most_z, most_z, ar_send.at[2, r]).wait()
        pltpu.make_async_copy(most_h, most_h, ar_send.at[3, r]).wait()
        back.wait_send()

    aligned[...] = 0.5 * cur[...]
    mvx[slot64(ti), :] = plan[slot64(ti), :]
    mvx[slot64(16 + ti), :] = plan[slot64(16 + across), :]
    most_mv = mvx.at[pl.ds(0, ROWS - OWN), :]
    pltpu.make_async_copy(most_mv, most_mv, mv_recv).wait()
    for part, place in ((0, ti), (1, across)):
        stat = 8 * part + place // 2
        odd = lax.rem(place, 2) == 1
        whole = rlse[pl.ds(stat, 1), :]
        total = [0.0] * (D // 128)
        for k in range(NTGT):
            share = 0.5 * jnp.exp2(rowx[2 * ROUNDS - 1, k, pl.ds(stat, 1), :] - whole)
            factor = jnp.transpose(jnp.broadcast_to(share, (128, 128)))
            factor = jnp.where(odd, factor[64:128], factor[0:64])
            at = (16 * part + k) * 64
            for cut in range(D // 128):
                lane = slice(128 * cut, 128 * (cut + 1))
                total[cut] = total[cut] + mvx[at:at + 64, lane].astype(F32) * factor
        for cut in range(D // 128):
            moved[64 * part:64 * (part + 1), 128 * cut:128 * (cut + 1)] = total[cut]

    pltpu.make_async_copy(most_mv, most_mv, mv_send).wait()
    pltpu.make_async_copy(most_tgt, most_tgt, tgt_send).wait()
    most_src = sblk.at[pl.ds(0, ROWS - OWN), :]
    pltpu.make_async_copy(most_src, most_src, src_send).wait()


def shards(source, target, rotation):
    vmem = pl.BlockSpec(memory_space=pltpu.VMEM)
    dma = pltpu.SemaphoreType.DMA
    v = pltpu.VMEM
    halves = pl.pallas_call(
        kernel,
        out_shape=(jax.ShapeDtypeStruct((D, D), F32), jax.ShapeDtypeStruct((OWN, D), F32)),
        in_specs=[vmem] * 3,
        out_specs=(vmem, vmem),
        scratch_shapes=[
            v((ROWS, D), BF16),
            v((D, ROWS), BF16),
            v((D, COLS), BF16),
            v((COLS, D), BF16),
            v((ROWS, COLS), F32),
            v((ROWS, D), BF16),
            v((ROWS, D), BF16),
            v((CH, COLS), BF16),
            v((ROWS, 128), F32),
            v((ROWS, 128), F32),
            v((ROWS, 128), F32),
            v((8, COLS), F32),
            v((8, COLS), F32),
            v((8, COLS), F32),
            v((3 * D, D), BF16),
            v((D, D), F32),
            v((4, NSRC, 8, 128), F32),
            v((4, NTGT, 16, 128), F32),
            v((2, 256, D), BF16),
            v((2, NTGT, 16, D), BF16),
            v((2, 4, 16, D), BF16),
            v((2, 256, D), BF16),
            v((2, 256, D), BF16),
            v((D, D), F32),
            v((ROWS, D), BF16),
            v((2, 256, D), BF16),
            v((2, 256, D), BF16),
            v((16, 128), F32),
            dma(()), dma((5, 2)), dma((5, 2)), dma(()), dma((4,)),
            dma((4,)), dma((4,)), dma((4, 2)), dma((4, 2)),
            dma((5, 2)), dma((5, 2)), dma(()), dma(()),
        ],
        compiler_params=pltpu.CompilerParams(
            collective_id=0, has_side_effects=True, vmem_limit_bytes=48 * 1024 * 1024),
    )(source, target.T, rotation)
    return tuple(2.0 * half for half in halves)


def solution(mesh):
    return jax.shard_map(
        shards, mesh=mesh, in_specs=(P(("src", "tgt"), None), P("tgt", "src"), P()),
        out_specs=(P(), P(("src", "tgt"), None)), check_vma=False)
```

```python
import functools
import math

import jax
import jax.numpy as jnp
from jax import lax
from jax.experimental import pallas as pl
from jax.experimental.pallas import tpu as pltpu
from jax.sharding import PartitionSpec as P

ROUNDS = 2
MESH = pl.DeviceIdType.MESH
VIA = (((1, 2), (0, 3)), ((3, 2), (0, 3)), ((2, 1), (3, 0)), ((2, 3), (3, 0)))
FAR_FIRST = ((2, 2), (1, 2), (3, 2), (2, 1), (2, 3), (1, 1), (3, 3), (1, 3), (3, 1), (0, 2), (2, 0), (0, 1), (0, 3), (1, 0), (3, 0))
F32, BF16 = jnp.float32, jnp.bfloat16
NSRC, NTGT = 8, 16
D = 512
OWN = 128
ROWS = 2048
COLS = 1024
CH = 256
RB = 32
LOG_N = 14.0
SCALE = 1.0 / math.sqrt(D) * math.log2(math.e)


def mm(a, b):
    return jnp.dot(a, b, preferred_element_type=F32)


def split2(w):
    hi = w.astype(BF16)
    return hi, (w - hi.astype(F32)).astype(BF16)


def kernel(
    src_in, tgt_in, rot_in, aligned, moved,
    sblk, sblk_t, feats_t, feats, scores, plan, sblk_s, probs_a, probs_b, parts_a, parts_b, ucol, mrow, lrow,
    col_m, col_s, vrow, w2, cur, colx, rowx, sib1, tgt1, zred, mhalf, mother, gbuf, mvx, mhold, mkeep, rlse, stage,
    src_send, near, far, tgt_send, tgt_recv, col_send, col_recv, row_send_sem, row_recv,
    ar_send, ar_recv, mv_send, mv_recv, st_send, st_recv, pair_recv, lot_recv,
):
    si, ti = lax.axis_index("src"), lax.axis_index("tgt")
    core, zed = lax.rem(si, 2), si // 2
    sibling = zed * 2 + 1 - core
    ty, tx = ti // 4, lax.rem(ti, 4)
    across = 4 * tx + ty

    def tgt_peer(d):
        return lax.rem(ti + d, NTGT)

    def src_peer(d):
        return lax.rem(si + d, NSRC)

    barrier = pltpu.get_barrier_semaphore()

    @pl.loop(1, NTGT)
    def _(d):
        pl.semaphore_signal(barrier, inc=1, device_id=(si, tgt_peer(d)), device_id_type=MESH)

    @pl.loop(1, NSRC)
    def _(d):
        pl.semaphore_signal(barrier, inc=1, device_id=(src_peer(d), ti), device_id_type=MESH)

    pl.semaphore_wait(barrier, NTGT + NSRC - 2)

    def to(src, dst, send, recv, s, t):
        return pltpu.make_async_remote_copy(
            src_ref=src, dst_ref=dst, send_sem=send, recv_sem=recv,
            device_id=(s, t), device_id_type=MESH)

    def slot128(k):
        return pl.ds(pl.multiple_of(k * OWN, OWN), OWN)

    def slot64(k):
        return pl.ds(pl.multiple_of(k * 64, 64), 64)

    def beside(c, d):
        return lax.rem(c + d, 4)

    x_ways = [(si, 4 * ty + beside(tx, d)) for d in (1, 3)]
    y_ways = [(si, 4 * beside(ty, d) + tx) for d in (1, 3)]
    z_ways = [(2 * beside(zed, d) + core, ti) for d in (1, 3)]

    def both_ways(ring, src, dst, ways, send):
        for side in range(2):
            to(src, dst, send, near.at[ring, side], *ways[side]).start()

    def relay(ring, ref, at, count, c, ways, send, after):
        for side, k in ((0, beside(c, 3)), (1, beside(c, 1))):
            land = ref.at[pl.ds(pl.multiple_of(at(k), count), count), :]
            pltpu.make_async_copy(land, land, near.at[ring, side]).wait()
            half = ref.at[pl.ds(pl.multiple_of(at(k) + side * (count // 2), count // 2), count // 2), :]
            to(half, half, send, far.at[ring, side], *ways[side]).start()
            after(land, k)

    def relayed(ring, ref, at, count, c, after):
        k = beside(c, 2)
        for side in range(2):
            half = ref.at[pl.ds(pl.multiple_of(at(k) + side * (count // 2), count // 2), count // 2), :]
            pltpu.make_async_copy(half, half, far.at[ring, side]).wait()
        after(ref.at[pl.ds(pl.multiple_of(at(k), count), count), :], k)

    def nothing(land, k):
        pass

    upper, lower = src_in.at[pl.ds(0, 64), :], src_in.at[pl.ds(64, 64), :]
    own_up, own_low = sblk.at[slot64(ti), :], sblk.at[slot64(16 + across), :]
    own_feats = feats_t.at[slot64(si), :]
    both_ways(2, tgt_in, own_feats, z_ways, tgt_send)
    both_ways(0, upper, own_up, x_ways, src_send)
    both_ways(1, lower, own_low, y_ways, src_send)
    both_ways(3, upper, own_up, y_ways, src_send)
    both_ways(4, lower, own_low, x_ways, src_send)
    to(tgt_in, own_feats, tgt_send, tgt_recv.at[zed], sibling, ti).start()

    sblk[slot64(ti), :] = src_in[0:64, :]
    sblk[slot64(16 + across), :] = src_in[64:128, :]
    feats_t[slot64(si), :] = tgt_in[...]
    cur[...] = rot_in[...]
    for part, piece in enumerate(split2(rot_in[...])):
        w2[part * D:(part + 1) * D, :] = piece

    def up_on(land, k):
        both_ways(3, land, land, y_ways, src_send)

    def low_on(land, k):
        both_ways(4, land, land, x_ways, src_send)

    def to_sibling(land, k):
        to(land, land, tgt_send, tgt_recv.at[k], sibling, ti).start()

    def up_at(k):
        return 64 * (4 * ty + k)

    def low_at(k):
        return ROWS // 2 + 64 * (4 * tx + k)

    def feats_at(k):
        return 64 * (2 * k + core)

    relay(0, sblk, up_at, 64, tx, x_ways, src_send, up_on)
    relay(1, sblk, low_at, 64, ty, y_ways, src_send, low_on)
    relay(2, feats_t, feats_at, 64, zed, z_ways, tgt_send, to_sibling)
    relayed(0, sblk, up_at, 64, tx, up_on)
    relayed(1, sblk, low_at, 64, ty, low_on)
    relayed(2, feats_t, feats_at, 64, zed, to_sibling)
    for k in range(4):
        land = feats_t.at[slot64(2 * k + 1 - core), :]
        pltpu.make_async_copy(land, land, tgt_recv.at[k]).wait()
    most_tgt = feats_t.at[pl.ds(0, D - 64), :]
    for part in range(D // 128):
        feats[:, 128 * part:128 * (part + 1)] = jnp.transpose(feats_t[128 * part:128 * (part + 1), :])

    def chunk(j):
        return pl.ds(pl.multiple_of(j * CH, CH), CH)

    def reset_cols():
        col_m[...] = jnp.full((8, COLS), -jnp.inf, F32)
        col_s[...] = jnp.zeros((8, COLS), F32)

    def col_update(rows, shifted):
        for ct in range(COLS // 128):
            cut = pl.ds(128 * ct, 128)
            x = scores[rows, cut]
            if shifted:
                x = x + ucol[rows, :]
            x = x.reshape(CH // 8, 8, 128)
            old = col_m[:, cut]
            new = jnp.maximum(old, jnp.max(x, axis=0))
            col_s[:, cut] = col_s[:, cut] * jnp.exp2(old - new) + jnp.sum(jnp.exp2(x - new[None]), axis=0)
            col_m[:, cut] = new

    def col_exchange(slot):
        for ct in range(COLS // 128):
            cut = pl.ds(128 * ct, 128)
            high = jnp.max(col_m[:, cut], axis=0, keepdims=True)
            total = jnp.sum(col_s[:, cut] * jnp.exp2(col_m[:, cut] - high), axis=0, keepdims=True)
            colx[slot, si, ct:ct + 1, :] = high + jnp.log2(total)

        for d in (4, 5, 2, 6, 3, 7, 1):
            s = 2 * beside(zed, d // 2) + lax.rem(core + d, 2)
            to(colx.at[slot, si], colx.at[slot, si], col_send.at[slot], col_recv.at[slot], s, ti).start()

        seven = colx.at[slot, pl.ds(0, NSRC - 1)]
        pltpu.make_async_copy(seven, seven, col_recv.at[slot]).wait()
        every = colx[slot]
        high = jnp.max(every, axis=0)
        v = -LOG_N - (high + jnp.log2(jnp.sum(jnp.exp2(every - high[None]), axis=0)))
        for ct in range(COLS // 128):
            vrow[:, 128 * ct:128 * (ct + 1)] = jnp.broadcast_to(v[ct:ct + 1, :], (8, 128))

    def lane_max(rows):
        top = None
        for ct in range(COLS // 128):
            x = row_tile(rows, ct)
            top = x if top is None else jnp.maximum(top, x)
        return top

    def row_tile(rows, ct):
        cut = pl.ds(128 * ct, 128)
        x = scores[rows, cut].reshape(RB // 8, 8, 128) + vrow[:, cut][None]
        return x.reshape(RB, 128)

    def row_pass(step):
        rows = pl.ds(pl.multiple_of(step * RB, RB), RB)
        top = lane_max(rows)
        total = jnp.exp2(row_tile(rows, 0) - top)
        for ct in range(1, COLS // 128):
            total = total + jnp.exp2(row_tile(rows, ct) - top)
        mrow[rows, :] = top
        lrow[rows, :] = total

    def row_send(slot, half, shared):
        for k in range(8 * half, 8 * half + 8):
            rows = slot128(k)
            if shared:
                high = jnp.transpose(mrow[rows, :])[0:1, :]
                total = jnp.transpose(lrow[rows, :])[0:1, :]
            else:
                tops = jnp.transpose(mrow[rows, :])
                high = jnp.max(tops, axis=0, keepdims=True)
                total = jnp.sum(jnp.transpose(lrow[rows, :]) * jnp.exp2(tops - high), axis=0, keepdims=True)
            rowx[slot, ti, k:k + 1, :] = high + jnp.log2(total)

        own = rowx.at[slot, ti, pl.ds(8 * half, 8), :]

        for dy, dx in FAR_FIRST:
            t = 4 * beside(ty, dy) + beside(tx, dx)
            to(own, own, row_send_sem.at[slot, half], row_recv.at[slot, half], si, t).start()

    def row_most(slot, half):
        return rowx.at[slot, pl.ds(0, NTGT - 1), pl.ds(8 * half, 8), :]

    def row_combine(slot, half):
        most = row_most(slot, half)
        pltpu.make_async_copy(most, most, row_recv.at[slot, half]).wait()
        every = rowx[slot, :, 8 * half:8 * half + 8, :]
        high = jnp.max(every, axis=0)
        rlse[8 * half:8 * half + 8, :] = high + jnp.log2(jnp.sum(jnp.exp2(every - high[None]), axis=0))

    def row_expanded(k):
        row = rlse[pl.ds(k, 1), :]
        return jnp.transpose(jnp.broadcast_to(row, (128, 128)))

    @pl.loop(0, ROUNDS)
    def _(r):
        first, final = r == 0, r == ROUNDS - 1
        reset_cols()

        @pl.loop(0, 4)
        def _(phase):
            offset = phase + phase // 2 - 2 * (phase // 3)
            pair = (chunk(beside(ty, offset)), chunk(4 + beside(tx, offset)))

            @pl.when(jnp.logical_and(first, phase == 1))
            def _():
                relay(3, sblk, lambda k: CH * k, CH, ty, y_ways, src_send, nothing)
                relay(4, sblk, lambda k: ROWS // 2 + CH * k, CH, tx, x_ways, src_send, nothing)

            @pl.when(jnp.logical_and(first, phase == 3))
            def _():
                relayed(3, sblk, lambda k: CH * k, CH, ty, nothing)
                relayed(4, sblk, lambda k: ROWS // 2 + CH * k, CH, tx, nothing)

            @pl.when(first)
            def _():
                for rows in pair:
                    sblk_t[:, rows] = jnp.transpose(sblk[rows, :])

            turned = [mm(jnp.concatenate([sblk[rows, :]] * 2, axis=1), w2[...]).astype(BF16) for rows in pair]
            for rows, z in zip(pair, turned):
                scores[rows, :] = mm(z, feats_t[...]) * SCALE
            for rows in pair:
                col_update(rows, False)

        col_exchange(2 * r)

        for half in range(2):
            @pl.loop(half * ROWS // RB // 2, (half + 1) * ROWS // RB // 2)
            def _(step):
                row_pass(step)

            row_send(2 * r, half, False)

        reset_cols()
        for half in range(2):
            row_combine(2 * r, half)
            for k in range(8 * half, 8 * half + 8):
                ucol[slot128(k), :] = -LOG_N - row_expanded(k)

            @pl.loop(half * ROWS // CH // 2, (half + 1) * ROWS // CH // 2)
            def _(j):
                col_update(chunk(j), True)

        col_exchange(2 * r + 1)

        @pl.loop(0, ROWS // RB)
        def _(step):
            rows = pl.ds(pl.multiple_of(step * RB, RB), RB)
            mrow[rows, :] = lane_max(rows)

        @pl.loop(0, ROWS // 512)
        def _(step):
            rows = pl.ds(pl.multiple_of(step * 512, 512), 512)
            mrow[rows, :] = jnp.broadcast_to(jnp.max(mrow[rows, :], axis=1, keepdims=True), (512, 128))

        def images(i):
            for side, (probs, parts) in enumerate(((probs_a, parts_a), (probs_b, parts_b))):
                j = 2 * i + side
                for step in range(CH // RB):
                    rows = pl.ds(pl.multiple_of(j * CH + step * RB, RB), RB)
                    top = mrow[rows, :]
                    total = None
                    for ct in range(COLS // 128):
                        p = jnp.exp2(row_tile(rows, ct) - top)
                        total = p if total is None else total + p
                        probs[step * RB:(step + 1) * RB, 128 * ct:128 * (ct + 1)] = p.astype(BF16)
                    parts[step * RB:(step + 1) * RB, :] = total
            for side, (probs, parts) in enumerate(((probs_a, parts_a), (probs_b, parts_b))):
                rows = chunk(2 * i + side)
                image = mm(probs[...], feats[...])
                sums = jnp.broadcast_to(jnp.sum(parts[...], axis=1, keepdims=True), (CH, 128))
                lrow[rows, :] = sums
                inverse = 1.0 / sums
                for cut in range(D // 128):
                    lane = slice(128 * cut, 128 * (cut + 1))
                    plan[rows, lane] = (image[:, lane] * inverse).astype(BF16)

        for half in range(2):
            pl.loop(half * ROWS // CH // 4, (half + 1) * ROWS // CH // 4)(images)
            row_send(2 * r + 1, half, True)

        def send_images(offsets):
            @pl.when(final)
            def _():
                for dy, dx in offsets:
                    y, x = beside(ty, dy), beside(tx, dx)
                    for src, dst in ((4 * y + x, ti), (16 + 4 * x + y, 16 + ti)):
                        to(plan.at[slot64(src), :], mvx.at[slot64(dst), :], mv_send, mv_recv, si, 4 * y + x).start()

        def to_stage():
            @pl.when(final)
            def _():
                for q, ((dy, dx), (sy, sx)) in enumerate(VIA):
                    y, x = beside(ty, dy), beside(tx, dx)
                    for half, src in enumerate((4 * y + x, 16 + 4 * x + y)):
                        to(plan.at[slot64(src), :], stage.at[q, pl.ds(64 * half, 64), :], st_send, st_recv.at[q],
                           si, 4 * beside(ty, sy) + beside(tx, sx)).start()

        def from_stage(chosen):
            @pl.when(final)
            def _():
                for q in chosen:
                    (dy, dx), (sy, sx) = VIA[q]
                    pltpu.make_async_copy(stage.at[q], stage.at[q], st_recv.at[q]).wait()
                    sender = 4 * beside(ty, 4 - sy) + beside(tx, 4 - sx)
                    t = 4 * beside(ty, 4 + dy - sy) + beside(tx, 4 + dx - sx)
                    for half, dst in enumerate((sender, 16 + sender)):
                        to(stage.at[q, pl.ds(64 * half, 64), :], mvx.at[slot64(dst), :], mv_send, mv_recv, si, t).start()

        to_stage()
        send_images(((0, 1), (1, 0), (1, 1), (0, 3), (3, 0)))
        for half in range(2):
            row_combine(2 * r + 1, half)
            factor = jnp.exp2(rowx[2 * r + 1, ti, 8 * half:8 * half + 8, :] - rlse[8 * half:8 * half + 8, :])
            for k in range(8):
                lane = slice(128 * (8 * half + k), 128 * (8 * half + k + 1))
                sblk_s[:, lane] = (sblk_t[:, lane].astype(F32) * factor[k:k + 1, :]).astype(BF16)

        theirs = pl.ds(pl.multiple_of((1 - core) * 256, 256), 256)
        ours = pl.ds(pl.multiple_of(core * 256, 256), 256)
        def lot(k):
            return pl.ds(pl.multiple_of(k * 16, 16), 16)

        mhold[r] = mm(sblk_s[theirs, :], plan[...]).astype(BF16)
        for way in (2, 1, 3, 0):
            y = beside(ty, way)
            to(mhold.at[r, slot64(y), :], sib1.at[r, slot64(y), :], ar_send.at[0, r], pair_recv.at[r, y], sibling, ti).start()
        gbuf[0:256, :] = mm(sblk_s[ours, :], plan[...])
        for way in (2, 1, 3, 0):
            y = beside(ty, way)
            land = sib1.at[r, slot64(y), :]
            pltpu.make_async_copy(land, land, pair_recv.at[r, y]).wait()
            mkeep[r, slot64(y), :] = (gbuf[slot64(y), :] + sib1[r, slot64(y), :].astype(F32)).astype(BF16)
            for dx in (2, 1, 3, 0):
                if way == 0 and dx == 0:
                    continue
                t = 4 * y + beside(tx, dx)
                to(mkeep.at[r, lot(t), :], tgt1.at[r, ti], ar_send.at[1, r], ar_recv.at[1, r], si, t).start()

        from_stage((0, 2))
        send_images(((1, 3), (3, 1)))
        tgt1[r, ti] = mkeep[r, lot(ti), :]
        most = tgt1.at[r, pl.ds(0, NTGT - 1)]
        pltpu.make_async_copy(most, most, ar_recv.at[1, r]).wait()
        zred[r, zed] = jnp.sum(tgt1[r].astype(F32), axis=0).astype(BF16)

        @pl.loop(1, 4)
        def _(d):
            other = lax.rem(zed + d, 4) * 2 + core
            to(zred.at[r, zed], zred.at[r, zed], ar_send.at[2, r], ar_recv.at[2, r], other, ti).start()

        most_z = zred.at[r, pl.ds(0, 3)]
        pltpu.make_async_copy(most_z, most_z, ar_recv.at[2, r]).wait()
        mhalf[r, lot(ti), :] = jnp.sum(zred[r].astype(F32), axis=0).astype(BF16)

        for dy, dx in FAR_FIRST:
            t = 4 * beside(ty, dy) + beside(tx, dx)
            to(mhalf.at[r, lot(ti), :], mhalf.at[r, lot(ti), :], ar_send.at[3, r], lot_recv.at[r, ti], si, t).start()

        def share(land):
            to(land, mother.at[r, lot_at, :], ar_send.at[4, r], ar_recv.at[4, r], sibling, ti).start()

        lot_at = lot(ti)
        share(mhalf.at[r, lot_at, :])
        from_stage((1, 3))
        send_images(((3, 3), (0, 2), (2, 0), (2, 2)))
        for dy, dx in FAR_FIRST[::-1]:
            t = 4 * beside(ty, dy) + beside(tx, dx)
            lot_at = lot(t)
            land = mhalf.at[r, lot_at, :]
            pltpu.make_async_copy(land, land, lot_recv.at[r, t]).wait()
            share(land)
        gbuf[ours, :] = mhalf[r].astype(F32)
        pltpu.make_async_copy(mother.at[r], mother.at[r], ar_recv.at[4, r]).wait()
        gbuf[theirs, :] = mother[r].astype(F32)

        cross = gbuf[...]
        spread = jnp.sqrt(jnp.mean(cross * cross, axis=(0, 1), keepdims=True) + 1e-06)
        g = cur[...] + 0.1 * cross / (spread * math.sqrt(D))
        gh, gl = split2(g)
        gth, gtl = jnp.transpose(gh), jnp.transpose(gl)
        gram = mm(jnp.concatenate([gth, gth, gtl], axis=1), jnp.concatenate([gh, gl, gh], axis=0))
        rh, rl = split2(gram)
        step = mm(jnp.concatenate([gh, gh, gl], axis=1), jnp.concatenate([rh, rl, rh], axis=0))
        new = 1.5 * g - 0.5 * step
        cur[...] = new

        @pl.when(jnp.logical_not(final))
        def _():
            for part, piece in enumerate(split2(cur[...])):
                w2[part * D:(part + 1) * D, :] = piece

        for slot in (2 * r, 2 * r + 1):
            seven = colx.at[slot, pl.ds(0, NSRC - 1)]
            pltpu.make_async_copy(seven, seven, col_send.at[slot]).wait()
            for half in range(2):
                most_r = row_most(slot, half)
                pltpu.make_async_copy(most_r, most_r, row_send_sem.at[slot, half]).wait()
        pltpu.make_async_copy(mhold.at[r], mhold.at[r], ar_send.at[0, r]).wait()
        pltpu.make_async_copy(most, most, ar_send.at[1, r]).wait()
        pltpu.make_async_copy(most_z, most_z, ar_send.at[2, r]).wait()
        most_h = mhalf.at[r, pl.ds(0, 240), :]
        pltpu.make_async_copy(most_h, most_h, ar_send.at[3, r]).wait()
        pltpu.make_async_copy(mother.at[r], mother.at[r], ar_send.at[4, r]).wait()

    aligned[...] = 0.5 * cur[...]
    mvx[slot64(ti), :] = plan[slot64(ti), :]
    mvx[slot64(16 + ti), :] = plan[slot64(16 + across), :]
    most_mv = mvx.at[pl.ds(0, ROWS - OWN), :]
    pltpu.make_async_copy(most_mv, most_mv, mv_recv).wait()
    for part, place in ((0, ti), (1, across)):
        stat = 8 * part + place // 2
        odd = lax.rem(place, 2) == 1
        whole = rlse[pl.ds(stat, 1), :]
        total = [0.0] * (D // 128)
        for k in range(NTGT):
            share = 0.5 * jnp.exp2(rowx[2 * ROUNDS - 1, k, pl.ds(stat, 1), :] - whole)
            factor = jnp.transpose(jnp.broadcast_to(share, (128, 128)))
            factor = jnp.where(odd, factor[64:128], factor[0:64])
            at = (16 * part + k) * 64
            for cut in range(D // 128):
                lane = slice(128 * cut, 128 * (cut + 1))
                total[cut] = total[cut] + mvx[at:at + 64, lane].astype(F32) * factor
        for cut in range(D // 128):
            moved[64 * part:64 * (part + 1), 128 * cut:128 * (cut + 1)] = total[cut]

    pltpu.make_async_copy(most_mv, most_mv, mv_send).wait()
    pltpu.make_async_copy(stage, stage, st_send).wait()
    pltpu.make_async_copy(most_tgt, most_tgt, tgt_send).wait()
    most_src = sblk.at[pl.ds(0, ROWS - OWN), :]
    pltpu.make_async_copy(most_src, most_src, src_send).wait()


def shards(source, target, rotation):
    vmem = pl.BlockSpec(memory_space=pltpu.VMEM)
    dma = pltpu.SemaphoreType.DMA
    v = pltpu.VMEM
    halves = pl.pallas_call(
        kernel,
        out_shape=(jax.ShapeDtypeStruct((D, D), F32), jax.ShapeDtypeStruct((OWN, D), F32)),
        in_specs=[vmem] * 3,
        out_specs=(vmem, vmem),
        scratch_shapes=[
            v((ROWS, D), BF16),
            v((D, ROWS), BF16),
            v((D, COLS), BF16),
            v((COLS, D), BF16),
            v((ROWS, COLS), F32),
            v((ROWS, D), BF16),
            v((D, ROWS), BF16),
            v((CH, COLS), BF16),
            v((CH, COLS), BF16),
            v((CH, 128), F32),
            v((CH, 128), F32),
            v((ROWS, 128), F32),
            v((ROWS, 128), F32),
            v((ROWS, 128), F32),
            v((8, COLS), F32),
            v((8, COLS), F32),
            v((8, COLS), F32),
            v((2 * D, D), BF16),
            v((D, D), F32),
            v((4, NSRC, 8, 128), F32),
            v((4, NTGT, 16, 128), F32),
            v((2, 256, D), BF16),
            v((2, NTGT, 16, D), BF16),
            v((2, 4, 16, D), BF16),
            v((2, 256, D), BF16),
            v((2, 256, D), BF16),
            v((D, D), F32),
            v((ROWS, D), BF16),
            v((2, 256, D), BF16),
            v((2, 256, D), BF16),
            v((16, 128), F32),
            v((4, OWN, D), BF16),
            dma(()), dma((5, 2)), dma((5, 2)), dma(()), dma((4,)),
            dma((4,)), dma((4,)), dma((4, 2)), dma((4, 2)),
            dma((5, 2)), dma((5, 2)), dma(()), dma(()), dma(()), dma((4,)), dma((2, 4)), dma((2, NTGT)),
        ],
        compiler_params=pltpu.CompilerParams(
            collective_id=0, has_side_effects=True, vmem_limit_bytes=48 * 1024 * 1024),
    )(source, target.T, rotation)
    return tuple(2.0 * half for half in halves)


def solution(mesh):
    return jax.shard_map(
        shards, mesh=mesh, in_specs=(P(("src", "tgt"), None), P("tgt", "src"), P()),
        out_specs=(P(), P(("src", "tgt"), None)), check_vma=False)
```

```python
import functools
import math

import jax
import jax.numpy as jnp
from jax import lax
from jax.experimental import pallas as pl
from jax.experimental.pallas import tpu as pltpu
from jax.sharding import PartitionSpec as P

ROUNDS = 2
MESH = pl.DeviceIdType.MESH
FAR_FIRST = ((2, 2), (1, 2), (3, 2), (2, 1), (2, 3), (1, 1), (3, 3), (1, 3), (3, 1), (0, 2), (2, 0), (0, 1), (0, 3), (1, 0), (3, 0))
F32, BF16 = jnp.float32, jnp.bfloat16
NSRC, NTGT = 8, 16
D = 512
OWN = 128
ROWS = 2048
COLS = 1024
CH = 256
RB = 32
LOG_N = 14.0
SCALE = 1.0 / math.sqrt(D) * math.log2(math.e)


def mm(a, b):
    return jnp.dot(a, b, preferred_element_type=F32)


def split2(w):
    hi = w.astype(BF16)
    return hi, (w - hi.astype(F32)).astype(BF16)


def kernel(
    src_in, tgt_in, rot_in, aligned, moved,
    sblk, sblk_t, feats_t, feats, scores, plan, sblk_s, probs_a, probs_b, parts_a, parts_b, ucol, mrow, lrow,
    col_m, col_s, vrow, w2, cur, colx, rowx, sib1, tgt1, zred, mhalf, mother, gbuf, mvb, mvacc, ring1, ring2, ring3, ring4, mhold, mkeep, rlse,
    src_send, near, far, tgt_send, tgt_recv, col_send, col_recv, row_send_sem, row_recv,
    ar_send, ar_recv, mv_send, mv_recv,
):
    si, ti = lax.axis_index("src"), lax.axis_index("tgt")
    core, zed = lax.rem(si, 2), si // 2
    sibling = zed * 2 + 1 - core
    ty, tx = ti // 4, lax.rem(ti, 4)
    across = 4 * tx + ty

    def tgt_peer(d):
        return lax.rem(ti + d, NTGT)

    def src_peer(d):
        return lax.rem(si + d, NSRC)

    barrier = pltpu.get_barrier_semaphore()

    @pl.loop(1, NTGT)
    def _(d):
        pl.semaphore_signal(barrier, inc=1, device_id=(si, tgt_peer(d)), device_id_type=MESH)

    @pl.loop(1, NSRC)
    def _(d):
        pl.semaphore_signal(barrier, inc=1, device_id=(src_peer(d), ti), device_id_type=MESH)

    pl.semaphore_wait(barrier, NTGT + NSRC - 2)

    def to(src, dst, send, recv, s, t):
        return pltpu.make_async_remote_copy(
            src_ref=src, dst_ref=dst, send_sem=send, recv_sem=recv,
            device_id=(s, t), device_id_type=MESH)

    def slot128(k):
        return pl.ds(pl.multiple_of(k * OWN, OWN), OWN)

    def slot64(k):
        return pl.ds(pl.multiple_of(k * 64, 64), 64)

    def beside(c, d):
        return lax.rem(c + d, 4)

    x_ways = [(si, 4 * ty + beside(tx, d)) for d in (1, 3)]
    y_ways = [(si, 4 * beside(ty, d) + tx) for d in (1, 3)]
    z_ways = [(2 * beside(zed, d) + core, ti) for d in (1, 3)]

    def both_ways(ring, src, dst, ways, send):
        for side in range(2):
            to(src, dst, send, near.at[ring, side], *ways[side]).start()

    def relay(ring, ref, at, count, c, ways, send, after):
        for side, k in ((0, beside(c, 3)), (1, beside(c, 1))):
            land = ref.at[pl.ds(pl.multiple_of(at(k), count), count), :]
            pltpu.make_async_copy(land, land, near.at[ring, side]).wait()
            half = ref.at[pl.ds(pl.multiple_of(at(k) + side * (count // 2), count // 2), count // 2), :]
            to(half, half, send, far.at[ring, side], *ways[side]).start()
            after(land, k)

    def relayed(ring, ref, at, count, c, after):
        k = beside(c, 2)
        for side in range(2):
            half = ref.at[pl.ds(pl.multiple_of(at(k) + side * (count // 2), count // 2), count // 2), :]
            pltpu.make_async_copy(half, half, far.at[ring, side]).wait()
        after(ref.at[pl.ds(pl.multiple_of(at(k), count), count), :], k)

    def nothing(land, k):
        pass

    upper, lower = src_in.at[pl.ds(0, 64), :], src_in.at[pl.ds(64, 64), :]
    own_up, own_low = sblk.at[slot64(ti), :], sblk.at[slot64(16 + across), :]
    own_feats = feats_t.at[slot64(si), :]
    both_ways(2, tgt_in, own_feats, z_ways, tgt_send)
    both_ways(0, upper, own_up, x_ways, src_send)
    both_ways(1, lower, own_low, y_ways, src_send)
    both_ways(3, upper, own_up, y_ways, src_send)
    both_ways(4, lower, own_low, x_ways, src_send)
    to(tgt_in, own_feats, tgt_send, tgt_recv.at[zed], sibling, ti).start()

    sblk[slot64(ti), :] = src_in[0:64, :]
    sblk[slot64(16 + across), :] = src_in[64:128, :]
    feats_t[slot64(si), :] = tgt_in[...]
    cur[...] = rot_in[...]
    for part, piece in enumerate(split2(rot_in[...])):
        w2[part * D:(part + 1) * D, :] = piece

    def up_on(land, k):
        both_ways(3, land, land, y_ways, src_send)

    def low_on(land, k):
        both_ways(4, land, land, x_ways, src_send)

    def to_sibling(land, k):
        to(land, land, tgt_send, tgt_recv.at[k], sibling, ti).start()

    def up_at(k):
        return 64 * (4 * ty + k)

    def low_at(k):
        return ROWS // 2 + 64 * (4 * tx + k)

    def feats_at(k):
        return 64 * (2 * k + core)

    relay(0, sblk, up_at, 64, tx, x_ways, src_send, up_on)
    relay(1, sblk, low_at, 64, ty, y_ways, src_send, low_on)
    relay(2, feats_t, feats_at, 64, zed, z_ways, tgt_send, to_sibling)
    relayed(0, sblk, up_at, 64, tx, up_on)
    relayed(1, sblk, low_at, 64, ty, low_on)
    relayed(2, feats_t, feats_at, 64, zed, to_sibling)
    for k in range(4):
        land = feats_t.at[slot64(2 * k + 1 - core), :]
        pltpu.make_async_copy(land, land, tgt_recv.at[k]).wait()
    most_tgt = feats_t.at[pl.ds(0, D - 64), :]
    for part in range(D // 128):
        feats[:, 128 * part:128 * (part + 1)] = jnp.transpose(feats_t[128 * part:128 * (part + 1), :])

    def chunk(j):
        return pl.ds(pl.multiple_of(j * CH, CH), CH)

    def reset_cols():
        col_m[...] = jnp.full((8, COLS), -jnp.inf, F32)
        col_s[...] = jnp.zeros((8, COLS), F32)

    def col_update(rows, shifted):
        for ct in range(COLS // 128):
            cut = pl.ds(128 * ct, 128)
            x = scores[rows, cut]
            if shifted:
                x = x + ucol[rows, :]
            x = x.reshape(CH // 8, 8, 128)
            old = col_m[:, cut]
            new = jnp.maximum(old, jnp.max(x, axis=0))
            col_s[:, cut] = col_s[:, cut] * jnp.exp2(old - new) + jnp.sum(jnp.exp2(x - new[None]), axis=0)
            col_m[:, cut] = new

    def col_exchange(slot):
        for ct in range(COLS // 128):
            cut = pl.ds(128 * ct, 128)
            high = jnp.max(col_m[:, cut], axis=0, keepdims=True)
            total = jnp.sum(col_s[:, cut] * jnp.exp2(col_m[:, cut] - high), axis=0, keepdims=True)
            colx[slot, si, ct:ct + 1, :] = high + jnp.log2(total)

        for d in (4, 5, 2, 6, 3, 7, 1):
            s = 2 * beside(zed, d // 2) + lax.rem(core + d, 2)
            to(colx.at[slot, si], colx.at[slot, si], col_send.at[slot], col_recv.at[slot], s, ti).start()

        seven = colx.at[slot, pl.ds(0, NSRC - 1)]
        pltpu.make_async_copy(seven, seven, col_recv.at[slot]).wait()
        every = colx[slot]
        high = jnp.max(every, axis=0)
        v = -LOG_N - (high + jnp.log2(jnp.sum(jnp.exp2(every - high[None]), axis=0)))
        for ct in range(COLS // 128):
            vrow[:, 128 * ct:128 * (ct + 1)] = jnp.broadcast_to(v[ct:ct + 1, :], (8, 128))

    def lane_max(rows):
        top = None
        for ct in range(COLS // 128):
            x = row_tile(rows, ct)
            top = x if top is None else jnp.maximum(top, x)
        return top

    def row_tile(rows, ct):
        cut = pl.ds(128 * ct, 128)
        x = scores[rows, cut].reshape(RB // 8, 8, 128) + vrow[:, cut][None]
        return x.reshape(RB, 128)

    def row_pass(step):
        rows = pl.ds(pl.multiple_of(step * RB, RB), RB)
        top = lane_max(rows)
        total = jnp.exp2(row_tile(rows, 0) - top)
        for ct in range(1, COLS // 128):
            total = total + jnp.exp2(row_tile(rows, ct) - top)
        mrow[rows, :] = top
        lrow[rows, :] = total

    def row_send(slot, half, shared):
        for k in range(8 * half, 8 * half + 8):
            rows = slot128(k)
            if shared:
                high = jnp.transpose(mrow[rows, :])[0:1, :]
                total = jnp.transpose(lrow[rows, :])[0:1, :]
            else:
                tops = jnp.transpose(mrow[rows, :])
                high = jnp.max(tops, axis=0, keepdims=True)
                total = jnp.sum(jnp.transpose(lrow[rows, :]) * jnp.exp2(tops - high), axis=0, keepdims=True)
            rowx[slot, ti, k:k + 1, :] = high + jnp.log2(total)

        own = rowx.at[slot, ti, pl.ds(8 * half, 8), :]

        for dy, dx in FAR_FIRST:
            t = 4 * beside(ty, dy) + beside(tx, dx)
            to(own, own, row_send_sem.at[slot, half], row_recv.at[slot, half], si, t).start()

    def row_most(slot, half):
        return rowx.at[slot, pl.ds(0, NTGT - 1), pl.ds(8 * half, 8), :]

    def row_combine(slot, half):
        most = row_most(slot, half)
        pltpu.make_async_copy(most, most, row_recv.at[slot, half]).wait()
        every = rowx[slot, :, 8 * half:8 * half + 8, :]
        high = jnp.max(every, axis=0)
        rlse[8 * half:8 * half + 8, :] = high + jnp.log2(jnp.sum(jnp.exp2(every - high[None]), axis=0))

    def row_expanded(k):
        row = rlse[pl.ds(k, 1), :]
        return jnp.transpose(jnp.broadcast_to(row, (128, 128)))

    kinds = ((0, ty, y_ways, tx, x_ways), (1, tx, x_ways, ty, y_ways))

    def span(at, count):
        return pl.ds(pl.multiple_of(at, count), count)

    def arrived(step, kind, side, ring):
        land = ring.at[kind, side]
        pltpu.make_async_copy(land, land, mv_recv.at[step, kind, side]).wait()

    @pl.loop(0, ROUNDS)
    def _(r):
        first, final = r == 0, r == ROUNDS - 1
        reset_cols()

        @pl.loop(0, 4)
        def _(phase):
            offset = phase + phase // 2 - 2 * (phase // 3)
            pair = (chunk(beside(ty, offset)), chunk(4 + beside(tx, offset)))

            @pl.when(jnp.logical_and(first, phase == 1))
            def _():
                relay(3, sblk, lambda k: CH * k, CH, ty, y_ways, src_send, nothing)
                relay(4, sblk, lambda k: ROWS // 2 + CH * k, CH, tx, x_ways, src_send, nothing)

            @pl.when(jnp.logical_and(first, phase == 3))
            def _():
                relayed(3, sblk, lambda k: CH * k, CH, ty, nothing)
                relayed(4, sblk, lambda k: ROWS // 2 + CH * k, CH, tx, nothing)

            @pl.when(first)
            def _():
                for rows in pair:
                    sblk_t[:, rows] = jnp.transpose(sblk[rows, :])

            turned = [mm(jnp.concatenate([sblk[rows, :]] * 2, axis=1), w2[...]).astype(BF16) for rows in pair]
            for rows, z in zip(pair, turned):
                scores[rows, :] = mm(z, feats_t[...]) * SCALE
            for rows in pair:
                col_update(rows, False)

        col_exchange(2 * r)

        for half in range(2):
            @pl.loop(half * ROWS // RB // 2, (half + 1) * ROWS // RB // 2)
            def _(step):
                row_pass(step)

            row_send(2 * r, half, False)

        reset_cols()
        for half in range(2):
            row_combine(2 * r, half)
            for k in range(8 * half, 8 * half + 8):
                ucol[slot128(k), :] = -LOG_N - row_expanded(k)

            @pl.loop(half * ROWS // CH // 2, (half + 1) * ROWS // CH // 2)
            def _(j):
                col_update(chunk(j), True)

        col_exchange(2 * r + 1)

        @pl.loop(0, ROWS // RB)
        def _(step):
            rows = pl.ds(pl.multiple_of(step * RB, RB), RB)
            mrow[rows, :] = lane_max(rows)

        @pl.loop(0, ROWS // 512)
        def _(step):
            rows = pl.ds(pl.multiple_of(step * 512, 512), 512)
            mrow[rows, :] = jnp.broadcast_to(jnp.max(mrow[rows, :], axis=1, keepdims=True), (512, 128))

        def images(i):
            for side, (probs, parts) in enumerate(((probs_a, parts_a), (probs_b, parts_b))):
                j = 2 * i + side
                for step in range(CH // RB):
                    rows = pl.ds(pl.multiple_of(j * CH + step * RB, RB), RB)
                    top = mrow[rows, :]
                    total = None
                    for ct in range(COLS // 128):
                        p = jnp.exp2(row_tile(rows, ct) - top)
                        total = p if total is None else total + p
                        probs[step * RB:(step + 1) * RB, 128 * ct:128 * (ct + 1)] = p.astype(BF16)
                    parts[step * RB:(step + 1) * RB, :] = total
            for side, (probs, parts) in enumerate(((probs_a, parts_a), (probs_b, parts_b))):
                rows = chunk(2 * i + side)
                image = mm(probs[...], feats[...])
                sums = jnp.broadcast_to(jnp.sum(parts[...], axis=1, keepdims=True), (CH, 128))
                lrow[rows, :] = sums
                inverse = 1.0 / sums
                for cut in range(D // 128):
                    lane = slice(128 * cut, 128 * (cut + 1))
                    plan[rows, lane] = (image[:, lane] * inverse).astype(BF16)

        for half in range(2):
            pl.loop(half * ROWS // CH // 4, (half + 1) * ROWS // CH // 4)(images)
            row_send(2 * r + 1, half, True)

        for half in range(2):
            row_combine(2 * r + 1, half)
            factor = jnp.exp2(rowx[2 * r + 1, ti, 8 * half:8 * half + 8, :] - rlse[8 * half:8 * half + 8, :])
            for k in range(8):
                lane = slice(128 * (8 * half + k), 128 * (8 * half + k + 1))
                sblk_s[:, lane] = (sblk_t[:, lane].astype(F32) * factor[k:k + 1, :]).astype(BF16)

        @pl.when(final)
        def _():
            for k in range(NTGT):
                rows = slot128(k)
                row = jnp.exp2(rowx[2 * r + 1, ti, k:k + 1, :] - rlse[k:k + 1, :])
                factor = jnp.transpose(jnp.broadcast_to(row, (128, 128)))
                for cut in range(D // 128):
                    lane = slice(128 * cut, 128 * (cut + 1))
                    mvb[rows, lane] = (plan[rows, lane].astype(F32) * factor).astype(BF16)
            for kind, c, ways, _c, _w in kinds:
                for side in range(2):
                    part = mvb.at[span(1024 * kind + 256 * beside(c, 2) + 128 * side, 128), :]
                    to(part, ring1.at[kind, side], mv_send.at[0], mv_recv.at[0, kind, side], *ways[side]).start()

        theirs = pl.ds(pl.multiple_of((1 - core) * 256, 256), 256)
        ours = pl.ds(pl.multiple_of(core * 256, 256), 256)
        mhold[r] = mm(sblk_s[theirs, :], plan[...]).astype(BF16)
        pair = to(mhold.at[r], sib1.at[r], ar_send.at[0, r], ar_recv.at[0, r], sibling, ti)
        pair.start()
        mine = mm(sblk_s[ours, :], plan[...])
        pair.wait_recv()
        mkeep[r] = (mine + sib1[r].astype(F32)).astype(BF16)

        def lot(k):
            return pl.ds(pl.multiple_of(k * 16, 16), 16)

        for dy, dx in FAR_FIRST:
            t = 4 * beside(ty, dy) + beside(tx, dx)
            to(mkeep.at[r, lot(t), :], tgt1.at[r, ti], ar_send.at[1, r], ar_recv.at[1, r], si, t).start()

        @pl.when(final)
        def _():
            for kind, c, ways, _c, _w in kinds:
                for side in range(2):
                    arrived(0, kind, side, ring1)
                    unit = 1024 * kind + 256 * beside(c, 1 + 2 * side)
                    rows = span(unit + 128 * side, 128)
                    mvb[rows, :] = (mvb[rows, :].astype(F32) + ring1[kind, side].astype(F32)).astype(BF16)
                    to(mvb.at[span(unit, 256), :], ring2.at[kind, side], mv_send.at[1], mv_recv.at[1, kind, side],
                       *ways[side]).start()

        tgt1[r, ti] = mkeep[r, lot(ti), :]
        most = tgt1.at[r, pl.ds(0, NTGT - 1)]
        pltpu.make_async_copy(most, most, ar_recv.at[1, r]).wait()
        zred[r, zed] = jnp.sum(tgt1[r].astype(F32), axis=0).astype(BF16)

        @pl.loop(1, 4)
        def _(d):
            other = lax.rem(zed + d, 4) * 2 + core
            to(zred.at[r, zed], zred.at[r, zed], ar_send.at[2, r], ar_recv.at[2, r], other, ti).start()

        most_z = zred.at[r, pl.ds(0, 3)]
        pltpu.make_async_copy(most_z, most_z, ar_recv.at[2, r]).wait()
        mhalf[r, lot(ti), :] = jnp.sum(zred[r].astype(F32), axis=0).astype(BF16)

        for dy, dx in FAR_FIRST:
            t = 4 * beside(ty, dy) + beside(tx, dx)
            to(mhalf.at[r, lot(ti), :], mhalf.at[r, lot(ti), :], ar_send.at[3, r], ar_recv.at[3, r], si, t).start()

        @pl.when(final)
        def _():
            for kind, c, _w, c2, ways2 in kinds:
                arrived(1, kind, 0, ring2)
                arrived(1, kind, 1, ring2)
                own = mvb[span(1024 * kind + 256 * c, 256), :].astype(F32)
                mvacc[kind] = (own + ring2[kind, 0].astype(F32) + ring2[kind, 1].astype(F32)).astype(BF16)
                for side in range(2):
                    part = mvacc.at[kind, span(64 * beside(c2, 2) + 32 * side, 32), :]
                    to(part, ring3.at[kind, side], mv_send.at[2], mv_recv.at[2, kind, side], *ways2[side]).start()

        most_h = mhalf.at[r, pl.ds(0, 240), :]
        pltpu.make_async_copy(most_h, most_h, ar_recv.at[3, r]).wait()
        back = to(mhalf.at[r], mother.at[r], ar_send.at[4, r], ar_recv.at[4, r], sibling, ti)
        back.start()
        gbuf[ours, :] = mhalf[r].astype(F32)

        @pl.when(final)
        def _():
            for kind, _c, _w, c2, ways2 in kinds:
                for side in range(2):
                    arrived(2, kind, side, ring3)
                    block = 64 * beside(c2, 1 + 2 * side)
                    rows = span(block + 32 * side, 32)
                    mvacc[kind, rows, :] = (mvacc[kind, rows, :].astype(F32) + ring3[kind, side].astype(F32)).astype(BF16)
                    to(mvacc.at[kind, span(block, 64), :], ring4.at[kind, side], mv_send.at[3],
                       mv_recv.at[3, kind, side], *ways2[side]).start()

        back.wait_recv()
        gbuf[theirs, :] = mother[r].astype(F32)

        cross = gbuf[...]
        spread = jnp.sqrt(jnp.mean(cross * cross, axis=(0, 1), keepdims=True) + 1e-06)
        g = cur[...] + 0.1 * cross / (spread * math.sqrt(D))
        gh, gl = split2(g)
        gth, gtl = jnp.transpose(gh), jnp.transpose(gl)
        gram = mm(jnp.concatenate([gth, gth, gtl], axis=1), jnp.concatenate([gh, gl, gh], axis=0))
        rh, rl = split2(gram)
        step = mm(jnp.concatenate([gh, gh, gl], axis=1), jnp.concatenate([rh, rl, rh], axis=0))
        new = 1.5 * g - 0.5 * step
        cur[...] = new

        @pl.when(jnp.logical_not(final))
        def _():
            for part, piece in enumerate(split2(cur[...])):
                w2[part * D:(part + 1) * D, :] = piece

        for slot in (2 * r, 2 * r + 1):
            seven = colx.at[slot, pl.ds(0, NSRC - 1)]
            pltpu.make_async_copy(seven, seven, col_send.at[slot]).wait()
            for half in range(2):
                most_r = row_most(slot, half)
                pltpu.make_async_copy(most_r, most_r, row_send_sem.at[slot, half]).wait()
        pair.wait_send()
        pltpu.make_async_copy(most, most, ar_send.at[1, r]).wait()
        pltpu.make_async_copy(most_z, most_z, ar_send.at[2, r]).wait()
        pltpu.make_async_copy(most_h, most_h, ar_send.at[3, r]).wait()
        back.wait_send()

    aligned[...] = 0.5 * cur[...]
    for kind, _c, _w, c2, _w2 in kinds:
        arrived(3, kind, 0, ring4)
        arrived(3, kind, 1, ring4)
        own = mvacc[kind, span(64 * c2, 64), :].astype(F32)
        moved[64 * kind:64 * (kind + 1), :] = 0.5 * (own + ring4[kind, 0].astype(F32) + ring4[kind, 1].astype(F32))
    for step, ring in enumerate((ring1, ring2, ring3, ring4)):
        pltpu.make_async_copy(ring, ring, mv_send.at[step]).wait()
    pltpu.make_async_copy(most_tgt, most_tgt, tgt_send).wait()
    most_src = sblk.at[pl.ds(0, ROWS - OWN), :]
    pltpu.make_async_copy(most_src, most_src, src_send).wait()


def shards(source, target, rotation):
    vmem = pl.BlockSpec(memory_space=pltpu.VMEM)
    dma = pltpu.SemaphoreType.DMA
    v = pltpu.VMEM
    halves = pl.pallas_call(
        kernel,
        out_shape=(jax.ShapeDtypeStruct((D, D), F32), jax.ShapeDtypeStruct((OWN, D), F32)),
        in_specs=[vmem] * 3,
        out_specs=(vmem, vmem),
        scratch_shapes=[
            v((ROWS, D), BF16),
            v((D, ROWS), BF16),
            v((D, COLS), BF16),
            v((COLS, D), BF16),
            v((ROWS, COLS), F32),
            v((ROWS, D), BF16),
            v((D, ROWS), BF16),
            v((CH, COLS), BF16),
            v((CH, COLS), BF16),
            v((CH, 128), F32),
            v((CH, 128), F32),
            v((ROWS, 128), F32),
            v((ROWS, 128), F32),
            v((ROWS, 128), F32),
            v((8, COLS), F32),
            v((8, COLS), F32),
            v((8, COLS), F32),
            v((2 * D, D), BF16),
            v((D, D), F32),
            v((4, NSRC, 8, 128), F32),
            v((4, NTGT, 16, 128), F32),
            v((2, 256, D), BF16),
            v((2, NTGT, 16, D), BF16),
            v((2, 4, 16, D), BF16),
            v((2, 256, D), BF16),
            v((2, 256, D), BF16),
            v((D, D), F32),
            v((ROWS, D), BF16),
            v((2, 256, D), BF16),
            v((2, 2, 128, D), BF16),
            v((2, 2, 256, D), BF16),
            v((2, 2, 32, D), BF16),
            v((2, 2, 64, D), BF16),
            v((2, 256, D), BF16),
            v((2, 256, D), BF16),
            v((16, 128), F32),
            dma(()), dma((5, 2)), dma((5, 2)), dma(()), dma((4,)),
            dma((4,)), dma((4,)), dma((4, 2)), dma((4, 2)),
            dma((5, 2)), dma((5, 2)), dma((4,)), dma((4, 2, 2)),
        ],
        compiler_params=pltpu.CompilerParams(
            collective_id=0, has_side_effects=True, vmem_limit_bytes=48 * 1024 * 1024),
    )(source, target.T, rotation)
    return tuple(2.0 * half for half in halves)


def solution(mesh):
    return jax.shard_map(
        shards, mesh=mesh, in_specs=(P(("src", "tgt"), None), P("tgt", "src"), P()),
        out_specs=(P(), P(("src", "tgt"), None)), check_vma=False)
```

```python
import functools
import math

import jax
import jax.numpy as jnp
from jax import lax
from jax.experimental import pallas as pl
from jax.experimental.pallas import tpu as pltpu
from jax.sharding import PartitionSpec as P

ROUNDS = 2
MESH = pl.DeviceIdType.MESH
FAR_FIRST = ((2, 2), (1, 2), (3, 2), (2, 1), (2, 3), (1, 1), (3, 3), (1, 3), (3, 1), (0, 2), (2, 0), (0, 1), (0, 3), (1, 0), (3, 0))
F32, BF16 = jnp.float32, jnp.bfloat16
NSRC, NTGT = 8, 16
D = 512
OWN = 128
ROWS = 2048
COLS = 1024
CH = 256
RB = 32
LOG_N = 14.0
SCALE = 1.0 / math.sqrt(D) * math.log2(math.e)


def mm(a, b):
    return jnp.dot(a, b, preferred_element_type=F32)


def split2(w):
    hi = w.astype(BF16)
    return hi, (w - hi.astype(F32)).astype(BF16)


def kernel(
    src_in, tgt_in, rot_in, aligned, moved,
    sblk, sblk_t, feats_t, feats, scores, plan, sblk_s, probs, tops_row, ucol, mrow, lrow,
    col_m, col_s, vrow, w2, cur, colx, rowx, sib1, tgt1, zred, mhalf, mother, gbuf, mvb, mvacc, ring1, ring2, ring3, ring4, mhold, mkeep, rlse,
    src_send, near, far, tgt_send, tgt_recv, col_send, col_recv, row_send_sem, row_recv,
    ar_send, ar_recv, mv_send, mv_recv,
):
    si, ti = lax.axis_index("src"), lax.axis_index("tgt")
    core, zed = lax.rem(si, 2), si // 2
    sibling = zed * 2 + 1 - core
    ty, tx = ti // 4, lax.rem(ti, 4)
    across = 4 * tx + ty

    def tgt_peer(d):
        return lax.rem(ti + d, NTGT)

    def src_peer(d):
        return lax.rem(si + d, NSRC)

    barrier = pltpu.get_barrier_semaphore()

    @pl.loop(1, NTGT)
    def _(d):
        pl.semaphore_signal(barrier, inc=1, device_id=(si, tgt_peer(d)), device_id_type=MESH)

    @pl.loop(1, NSRC)
    def _(d):
        pl.semaphore_signal(barrier, inc=1, device_id=(src_peer(d), ti), device_id_type=MESH)

    def slot64(k):
        return pl.ds(pl.multiple_of(k * 64, 64), 64)

    sblk[slot64(ti), :] = src_in[0:64, :]
    sblk[slot64(16 + across), :] = src_in[64:128, :]
    feats_t[slot64(si), :] = tgt_in[...]
    cur[...] = rot_in[...]
    for part, piece in enumerate(split2(rot_in[...])):
        w2[part * D:(part + 1) * D, :] = piece

    pl.semaphore_wait(barrier, NTGT + NSRC - 2)

    def to(src, dst, send, recv, s, t):
        return pltpu.make_async_remote_copy(
            src_ref=src, dst_ref=dst, send_sem=send, recv_sem=recv,
            device_id=(s, t), device_id_type=MESH)

    def slot128(k):
        return pl.ds(pl.multiple_of(k * OWN, OWN), OWN)

    def beside(c, d):
        return lax.rem(c + d, 4)

    x_ways = [(si, 4 * ty + beside(tx, d)) for d in (1, 3)]
    y_ways = [(si, 4 * beside(ty, d) + tx) for d in (1, 3)]
    z_ways = [(2 * beside(zed, d) + core, ti) for d in (1, 3)]

    def both_ways(ring, src, dst, ways, send):
        for side in range(2):
            to(src, dst, send, near.at[ring, side], *ways[side]).start()

    def relay(ring, ref, at, count, c, ways, send, after):
        for side, k in ((0, beside(c, 3)), (1, beside(c, 1))):
            land = ref.at[pl.ds(pl.multiple_of(at(k), count), count), :]
            pltpu.make_async_copy(land, land, near.at[ring, side]).wait()
            half = ref.at[pl.ds(pl.multiple_of(at(k) + side * (count // 2), count // 2), count // 2), :]
            to(half, half, send, far.at[ring, side], *ways[side]).start()
            after(land, k)

    def relayed(ring, ref, at, count, c, after):
        k = beside(c, 2)
        for side in range(2):
            half = ref.at[pl.ds(pl.multiple_of(at(k) + side * (count // 2), count // 2), count // 2), :]
            pltpu.make_async_copy(half, half, far.at[ring, side]).wait()
        after(ref.at[pl.ds(pl.multiple_of(at(k), count), count), :], k)

    def nothing(land, k):
        pass

    upper, lower = src_in.at[pl.ds(0, 64), :], src_in.at[pl.ds(64, 64), :]
    own_up, own_low = sblk.at[slot64(ti), :], sblk.at[slot64(16 + across), :]
    own_feats = feats_t.at[slot64(si), :]
    both_ways(2, tgt_in, own_feats, z_ways, tgt_send)
    both_ways(0, upper, own_up, x_ways, src_send)
    both_ways(1, lower, own_low, y_ways, src_send)
    both_ways(3, upper, own_up, y_ways, src_send)
    both_ways(4, lower, own_low, x_ways, src_send)
    to(tgt_in, own_feats, tgt_send, tgt_recv.at[zed], sibling, ti).start()


    def up_on(land, k):
        both_ways(3, land, land, y_ways, src_send)

    def low_on(land, k):
        both_ways(4, land, land, x_ways, src_send)

    def to_sibling(land, k):
        to(land, land, tgt_send, tgt_recv.at[k], sibling, ti).start()

    def up_at(k):
        return 64 * (4 * ty + k)

    def low_at(k):
        return ROWS // 2 + 64 * (4 * tx + k)

    def feats_at(k):
        return 64 * (2 * k + core)

    relay(0, sblk, up_at, 64, tx, x_ways, src_send, up_on)
    relay(1, sblk, low_at, 64, ty, y_ways, src_send, low_on)
    relay(2, feats_t, feats_at, 64, zed, z_ways, tgt_send, to_sibling)
    relayed(0, sblk, up_at, 64, tx, up_on)
    relayed(1, sblk, low_at, 64, ty, low_on)
    relayed(2, feats_t, feats_at, 64, zed, to_sibling)
    for k in range(4):
        land = feats_t.at[slot64(2 * k + 1 - core), :]
        pltpu.make_async_copy(land, land, tgt_recv.at[k]).wait()
    most_tgt = feats_t.at[pl.ds(0, D - 64), :]

    def chunk(j):
        return pl.ds(pl.multiple_of(j * CH, CH), CH)

    def reset_cols():
        col_m[...] = jnp.full((8, COLS), -jnp.inf, F32)
        col_s[...] = jnp.zeros((8, COLS), F32)

    def col_update(rows, shifted):
        for ct in range(COLS // 128):
            cut = pl.ds(128 * ct, 128)
            x = scores[rows, cut]
            if shifted:
                x = x + ucol[rows, :]
            x = x.reshape(CH // 8, 8, 128)
            old = col_m[:, cut]
            new = jnp.maximum(old, jnp.max(x, axis=0))
            col_s[:, cut] = col_s[:, cut] * jnp.exp2(old - new) + jnp.sum(jnp.exp2(x - new[None]), axis=0)
            col_m[:, cut] = new

    def col_start(slot):
        for ct in range(COLS // 128):
            cut = pl.ds(128 * ct, 128)
            high = jnp.max(col_m[:, cut], axis=0, keepdims=True)
            total = jnp.sum(col_s[:, cut] * jnp.exp2(col_m[:, cut] - high), axis=0, keepdims=True)
            colx[slot, si, ct:ct + 1, :] = high + jnp.log2(total)

        for d in (4, 5, 2, 6, 3, 7, 1):
            s = 2 * beside(zed, d // 2) + lax.rem(core + d, 2)
            to(colx.at[slot, si], colx.at[slot, si], col_send.at[slot], col_recv.at[slot], s, ti).start()

    def col_finish(slot):
        seven = colx.at[slot, pl.ds(0, NSRC - 1)]
        pltpu.make_async_copy(seven, seven, col_recv.at[slot]).wait()
        every = colx[slot]
        high = jnp.max(every, axis=0)
        v = -LOG_N - (high + jnp.log2(jnp.sum(jnp.exp2(every - high[None]), axis=0)))
        for ct in range(COLS // 128):
            vrow[:, 128 * ct:128 * (ct + 1)] = jnp.broadcast_to(v[ct:ct + 1, :], (8, 128))

    def lane_max(rows):
        top = None
        for ct in range(COLS // 128):
            x = row_tile(rows, ct)
            top = x if top is None else jnp.maximum(top, x)
        return top

    def row_tile(rows, ct):
        cut = pl.ds(128 * ct, 128)
        x = scores[rows, cut].reshape(RB // 8, 8, 128) + vrow[:, cut][None]
        return x.reshape(RB, 128)

    def row_pass(step):
        rows = pl.ds(pl.multiple_of(step * RB, RB), RB)
        top = lane_max(rows)
        total = jnp.exp2(row_tile(rows, 0) - top)
        for ct in range(1, COLS // 128):
            total = total + jnp.exp2(row_tile(rows, ct) - top)
        mrow[rows, :] = top
        lrow[rows, :] = total

    def row_send(slot, half, shared):
        for k in range(8 * half, 8 * half + 8):
            rows = slot128(k)
            if shared:
                high = jnp.transpose(mrow[rows, :])[0:1, :]
                total = jnp.sum(jnp.transpose(lrow[rows, :]), axis=0, keepdims=True)
                tops_row[k:k + 1, :] = high
            else:
                tops = jnp.transpose(mrow[rows, :])
                high = jnp.max(tops, axis=0, keepdims=True)
                total = jnp.sum(jnp.transpose(lrow[rows, :]) * jnp.exp2(tops - high), axis=0, keepdims=True)
            rowx[slot, ti, k:k + 1, :] = high + jnp.log2(total)

        own = rowx.at[slot, ti, pl.ds(8 * half, 8), :]

        for dy, dx in FAR_FIRST:
            t = 4 * beside(ty, dy) + beside(tx, dx)
            to(own, own, row_send_sem.at[slot, half], row_recv.at[slot, half], si, t).start()

    def row_most(slot, half):
        return rowx.at[slot, pl.ds(0, NTGT - 1), pl.ds(8 * half, 8), :]

    def row_combine(slot, half):
        most = row_most(slot, half)
        pltpu.make_async_copy(most, most, row_recv.at[slot, half]).wait()
        every = rowx[slot, :, 8 * half:8 * half + 8, :]
        high = jnp.max(every, axis=0)
        rlse[8 * half:8 * half + 8, :] = high + jnp.log2(jnp.sum(jnp.exp2(every - high[None]), axis=0))

    def row_expanded(k):
        row = rlse[pl.ds(k, 1), :]
        return jnp.transpose(jnp.broadcast_to(row, (128, 128)))

    kinds = ((0, ty, y_ways, tx, x_ways), (1, tx, x_ways, ty, y_ways))

    def span(at, count):
        return pl.ds(pl.multiple_of(at, count), count)

    def arrived(step, kind, side, ring):
        land = ring.at[kind, side]
        pltpu.make_async_copy(land, land, mv_recv.at[step, kind, side]).wait()

    @pl.loop(0, ROUNDS)
    def _(r):
        first, final = r == 0, r == ROUNDS - 1
        reset_cols()

        @pl.loop(0, 4)
        def _(phase):
            offset = phase + phase // 2 - 2 * (phase // 3)
            pair = (chunk(beside(ty, offset)), chunk(4 + beside(tx, offset)))

            @pl.when(jnp.logical_and(first, phase == 1))
            def _():
                relay(3, sblk, lambda k: CH * k, CH, ty, y_ways, src_send, nothing)
                relay(4, sblk, lambda k: ROWS // 2 + CH * k, CH, tx, x_ways, src_send, nothing)

            @pl.when(jnp.logical_and(first, phase == 3))
            def _():
                relayed(3, sblk, lambda k: CH * k, CH, ty, nothing)
                relayed(4, sblk, lambda k: ROWS // 2 + CH * k, CH, tx, nothing)

            turned = [mm(jnp.concatenate([sblk[rows, :]] * 2, axis=1), w2[...]).astype(BF16) for rows in pair]
            for rows, z in zip(pair, turned):
                scores[rows, :] = mm(z, feats_t[...]) * SCALE
            for rows in pair:
                col_update(rows, False)

        col_start(2 * r)

        @pl.when(first)
        def _():
            for part in range(D // 128):
                feats[:, 128 * part:128 * (part + 1)] = jnp.transpose(feats_t[128 * part:128 * (part + 1), :])
            for j in range(ROWS // CH):
                sblk_t[:, CH * j:CH * (j + 1)] = jnp.transpose(sblk[CH * j:CH * (j + 1), :])

        col_finish(2 * r)

        for half in range(2):
            @pl.loop(half * ROWS // RB // 2, (half + 1) * ROWS // RB // 2)
            def _(step):
                row_pass(step)

            row_send(2 * r, half, False)

        reset_cols()
        for half in range(2):
            row_combine(2 * r, half)
            for k in range(8 * half, 8 * half + 8):
                ucol[slot128(k), :] = -LOG_N - row_expanded(k)

            @pl.loop(half * ROWS // CH // 2, (half + 1) * ROWS // CH // 2)
            def _(j):
                col_update(chunk(j), True)

        col_start(2 * r + 1)
        col_finish(2 * r + 1)

        @pl.loop(0, ROWS // RB)
        def _(step):
            rows = pl.ds(pl.multiple_of(step * RB, RB), RB)
            mrow[rows, :] = lane_max(rows)

        @pl.loop(0, ROWS // 512)
        def _(step):
            rows = pl.ds(pl.multiple_of(step * 512, 512), 512)
            mrow[rows, :] = jnp.broadcast_to(jnp.max(mrow[rows, :], axis=1, keepdims=True), (512, 128))

        for half in range(2):
            @pl.loop(half * ROWS // RB // 4, (half + 1) * ROWS // RB // 4)
            def _(step):
                for side in range(2):
                    rows = pl.ds(pl.multiple_of((2 * step + side) * RB, RB), RB)
                    top = mrow[rows, :]
                    total = None
                    for ct in range(COLS // 128):
                        p = jnp.exp2(row_tile(rows, ct) - top)
                        total = p if total is None else total + p
                        probs[rows, 128 * ct:128 * (ct + 1)] = p.astype(BF16)
                    lrow[rows, :] = total

            row_send(2 * r + 1, half, True)

        @pl.loop(0, ROWS // 512)
        def _(step):
            rows = pl.ds(pl.multiple_of(step * 512, 512), 512)
            plan[rows, :] = mm(probs[rows, :], feats[...]).astype(BF16)

        for half in range(2):
            row_combine(2 * r + 1, half)
            factor = jnp.exp2(tops_row[8 * half:8 * half + 8, :] - rlse[8 * half:8 * half + 8, :])
            for k in range(8):
                lane = slice(128 * (8 * half + k), 128 * (8 * half + k + 1))
                sblk_s[:, lane] = (sblk_t[:, lane].astype(F32) * factor[k:k + 1, :]).astype(BF16)

        theirs = pl.ds(pl.multiple_of((1 - core) * 256, 256), 256)
        ours = pl.ds(pl.multiple_of(core * 256, 256), 256)
        mhold[r] = mm(sblk_s[theirs, :], plan[...]).astype(BF16)
        pair = to(mhold.at[r], sib1.at[r], ar_send.at[0, r], ar_recv.at[0, r], sibling, ti)
        pair.start()
        mine = mm(sblk_s[ours, :], plan[...])
        @pl.when(final)
        def _():
            for k in range(NTGT):
                rows = slot128(k)
                row = jnp.exp2(tops_row[k:k + 1, :] - rlse[k:k + 1, :])
                factor = jnp.transpose(jnp.broadcast_to(row, (128, 128)))
                for cut in range(D // 128):
                    lane = slice(128 * cut, 128 * (cut + 1))
                    mvb[rows, lane] = (plan[rows, lane].astype(F32) * factor).astype(BF16)

        pair.wait_recv()
        mkeep[r] = (mine + sib1[r].astype(F32)).astype(BF16)

        def lot(k):
            return pl.ds(pl.multiple_of(k * 16, 16), 16)

        for dy, dx in FAR_FIRST:
            t = 4 * beside(ty, dy) + beside(tx, dx)
            to(mkeep.at[r, lot(t), :], tgt1.at[r, ti], ar_send.at[1, r], ar_recv.at[1, r], si, t).start()

        @pl.when(final)
        def _():
            for kind, c, ways, _c, _w in kinds:
                for side in range(2):
                    part = mvb.at[span(1024 * kind + 256 * beside(c, 2) + 128 * side, 128), :]
                    to(part, ring1.at[kind, side], mv_send.at[0], mv_recv.at[0, kind, side], *ways[side]).start()

        tgt1[r, ti] = mkeep[r, lot(ti), :]
        most = tgt1.at[r, pl.ds(0, NTGT - 1)]
        pltpu.make_async_copy(most, most, ar_recv.at[1, r]).wait()
        zred[r, zed] = jnp.sum(tgt1[r].astype(F32), axis=0).astype(BF16)

        @pl.loop(1, 4)
        def _(d):
            other = lax.rem(zed + d, 4) * 2 + core
            to(zred.at[r, zed], zred.at[r, zed], ar_send.at[2, r], ar_recv.at[2, r], other, ti).start()

        @pl.when(final)
        def _():
            for kind, c, ways, _c, _w in kinds:
                for side in range(2):
                    arrived(0, kind, side, ring1)
                    unit = 1024 * kind + 256 * beside(c, 1 + 2 * side)
                    rows = span(unit + 128 * side, 128)
                    mvb[rows, :] = (mvb[rows, :].astype(F32) + ring1[kind, side].astype(F32)).astype(BF16)
                    to(mvb.at[span(unit, 256), :], ring2.at[kind, side], mv_send.at[1], mv_recv.at[1, kind, side],
                       *ways[side]).start()

        most_z = zred.at[r, pl.ds(0, 3)]
        pltpu.make_async_copy(most_z, most_z, ar_recv.at[2, r]).wait()
        mhalf[r, lot(ti), :] = jnp.sum(zred[r].astype(F32), axis=0).astype(BF16)

        for dy, dx in FAR_FIRST:
            t = 4 * beside(ty, dy) + beside(tx, dx)
            to(mhalf.at[r, lot(ti), :], mhalf.at[r, lot(ti), :], ar_send.at[3, r], ar_recv.at[3, r], si, t).start()

        @pl.when(final)
        def _():
            for kind, c, _w, c2, ways2 in kinds:
                arrived(1, kind, 0, ring2)
                arrived(1, kind, 1, ring2)
                own = mvb[span(1024 * kind + 256 * c, 256), :].astype(F32)
                mvacc[kind] = (own + ring2[kind, 0].astype(F32) + ring2[kind, 1].astype(F32)).astype(BF16)
                for side in range(2):
                    part = mvacc.at[kind, span(64 * beside(c2, 2) + 32 * side, 32), :]
                    to(part, ring3.at[kind, side], mv_send.at[2], mv_recv.at[2, kind, side], *ways2[side]).start()

        most_h = mhalf.at[r, pl.ds(0, 240), :]
        pltpu.make_async_copy(most_h, most_h, ar_recv.at[3, r]).wait()
        back = to(mhalf.at[r], mother.at[r], ar_send.at[4, r], ar_recv.at[4, r], sibling, ti)
        back.start()
        gbuf[ours, :] = mhalf[r].astype(F32)

        @pl.when(final)
        def _():
            for kind, _c, _w, c2, ways2 in kinds:
                for side in range(2):
                    arrived(2, kind, side, ring3)
                    block = 64 * beside(c2, 1 + 2 * side)
                    rows = span(block + 32 * side, 32)
                    mvacc[kind, rows, :] = (mvacc[kind, rows, :].astype(F32) + ring3[kind, side].astype(F32)).astype(BF16)
                    to(mvacc.at[kind, span(block, 64), :], ring4.at[kind, side], mv_send.at[3],
                       mv_recv.at[3, kind, side], *ways2[side]).start()

        back.wait_recv()
        gbuf[theirs, :] = mother[r].astype(F32)

        cross = gbuf[...]
        spread = jnp.sqrt(jnp.mean(cross * cross, axis=(0, 1), keepdims=True) + 1e-06)
        g = cur[...] + 0.1 * cross / (spread * math.sqrt(D))
        gh, gl = split2(g)
        gth, gtl = jnp.transpose(gh), jnp.transpose(gl)
        gram = mm(jnp.concatenate([gth, gth, gtl], axis=1), jnp.concatenate([gh, gl, gh], axis=0))
        rh, rl = split2(gram)
        step = mm(jnp.concatenate([gh, gh, gl], axis=1), jnp.concatenate([rh, rl, rh], axis=0))
        new = 1.5 * g - 0.5 * step
        cur[...] = new

        @pl.when(jnp.logical_not(final))
        def _():
            for part, piece in enumerate(split2(cur[...])):
                w2[part * D:(part + 1) * D, :] = piece

        for slot in (2 * r, 2 * r + 1):
            seven = colx.at[slot, pl.ds(0, NSRC - 1)]
            pltpu.make_async_copy(seven, seven, col_send.at[slot]).wait()
            for half in range(2):
                most_r = row_most(slot, half)
                pltpu.make_async_copy(most_r, most_r, row_send_sem.at[slot, half]).wait()
        pair.wait_send()
        pltpu.make_async_copy(most, most, ar_send.at[1, r]).wait()
        pltpu.make_async_copy(most_z, most_z, ar_send.at[2, r]).wait()
        pltpu.make_async_copy(most_h, most_h, ar_send.at[3, r]).wait()
        back.wait_send()

    aligned[...] = 0.5 * cur[...]
    for kind, _c, _w, c2, _w2 in kinds:
        arrived(3, kind, 0, ring4)
        arrived(3, kind, 1, ring4)
        own = mvacc[kind, span(64 * c2, 64), :].astype(F32)
        moved[64 * kind:64 * (kind + 1), :] = 0.5 * (own + ring4[kind, 0].astype(F32) + ring4[kind, 1].astype(F32))
    for step, ring in enumerate((ring1, ring2, ring3, ring4)):
        pltpu.make_async_copy(ring, ring, mv_send.at[step]).wait()
    pltpu.make_async_copy(most_tgt, most_tgt, tgt_send).wait()
    most_src = sblk.at[pl.ds(0, ROWS - OWN), :]
    pltpu.make_async_copy(most_src, most_src, src_send).wait()


def shards(source, target, rotation):
    vmem = pl.BlockSpec(memory_space=pltpu.VMEM)
    dma = pltpu.SemaphoreType.DMA
    v = pltpu.VMEM
    halves = pl.pallas_call(
        kernel,
        out_shape=(jax.ShapeDtypeStruct((D, D), F32), jax.ShapeDtypeStruct((OWN, D), F32)),
        in_specs=[vmem] * 3,
        out_specs=(vmem, vmem),
        scratch_shapes=[
            v((ROWS, D), BF16),
            v((D, ROWS), BF16),
            v((D, COLS), BF16),
            v((COLS, D), BF16),
            v((ROWS, COLS), F32),
            v((ROWS, D), BF16),
            v((D, ROWS), BF16),
            v((ROWS, COLS), BF16),
            v((16, 128), F32),
            v((ROWS, 128), F32),
            v((ROWS, 128), F32),
            v((ROWS, 128), F32),
            v((8, COLS), F32),
            v((8, COLS), F32),
            v((8, COLS), F32),
            v((2 * D, D), BF16),
            v((D, D), F32),
            v((4, NSRC, 8, 128), F32),
            v((4, NTGT, 16, 128), F32),
            v((2, 256, D), BF16),
            v((2, NTGT, 16, D), BF16),
            v((2, 4, 16, D), BF16),
            v((2, 256, D), BF16),
            v((2, 256, D), BF16),
            v((D, D), F32),
            v((ROWS, D), BF16),
            v((2, 256, D), BF16),
            v((2, 2, 128, D), BF16),
            v((2, 2, 256, D), BF16),
            v((2, 2, 32, D), BF16),
            v((2, 2, 64, D), BF16),
            v((2, 256, D), BF16),
            v((2, 256, D), BF16),
            v((16, 128), F32),
            dma(()), dma((5, 2)), dma((5, 2)), dma(()), dma((4,)),
            dma((4,)), dma((4,)), dma((4, 2)), dma((4, 2)),
            dma((5, 2)), dma((5, 2)), dma((4,)), dma((4, 2, 2)),
        ],
        compiler_params=pltpu.CompilerParams(
            collective_id=0, has_side_effects=True, vmem_limit_bytes=48 * 1024 * 1024),
    )(source, target.T, rotation)
    return tuple(2.0 * half for half in halves)


def solution(mesh):
    return jax.shard_map(
        shards, mesh=mesh, in_specs=(P(("src", "tgt"), None), P("tgt", "src"), P()),
        out_specs=(P(), P(("src", "tgt"), None)), check_vma=False)
```

```python
import functools
import math

import jax
import jax.numpy as jnp
from jax import lax
from jax.experimental import pallas as pl
from jax.experimental.pallas import tpu as pltpu
from jax.sharding import PartitionSpec as P

ROUNDS = 2
MESH = pl.DeviceIdType.MESH
FAR_FIRST = ((2, 2), (1, 2), (3, 2), (2, 1), (2, 3), (1, 1), (3, 3), (1, 3), (3, 1), (0, 2), (2, 0), (0, 1), (0, 3), (1, 0), (3, 0))
F32, BF16 = jnp.float32, jnp.bfloat16
NSRC, NTGT = 8, 16
D = 512
OWN = 128
ROWS = 2048
COLS = 1024
CH = 256
RB = 32
LOG_N = 14.0
SCALE = 1.0 / math.sqrt(D) * math.log2(math.e)


def mm(a, b):
    return jnp.dot(a, b, preferred_element_type=F32)


def split2(w):
    hi = w.astype(BF16)
    return hi, (w - hi.astype(F32)).astype(BF16)


def kernel(
    src_in, tgt_in, rot_in, aligned, moved,
    sblk, sblk_t, feats_t, feats, scores, plan, sblk_s, probs, tops_row, ucol, mrow, lrow,
    col_m, col_s, vrow, w2, cur, colx, rowx, sib1, tgt1, zred, mhalf, mother, gbuf, mvb, mvacc, ring1, ring2, ring3, ring4, mhold, mkeep, rlse,
    src_send, near, far, tgt_send, tgt_recv, col_send, col_recv, row_send_sem, row_recv,
    ar_send, ar_recv, mv_send, mv_recv,
):
    si, ti = lax.axis_index("src"), lax.axis_index("tgt")
    core, zed = lax.rem(si, 2), si // 2
    sibling = zed * 2 + 1 - core
    ty, tx = ti // 4, lax.rem(ti, 4)
    across = 4 * tx + ty

    def tgt_peer(d):
        return lax.rem(ti + d, NTGT)

    def src_peer(d):
        return lax.rem(si + d, NSRC)

    barrier = pltpu.get_barrier_semaphore()

    @pl.loop(1, NTGT)
    def _(d):
        pl.semaphore_signal(barrier, inc=1, device_id=(si, tgt_peer(d)), device_id_type=MESH)

    @pl.loop(1, NSRC)
    def _(d):
        pl.semaphore_signal(barrier, inc=1, device_id=(src_peer(d), ti), device_id_type=MESH)

    def slot64(k):
        return pl.ds(pl.multiple_of(k * 64, 64), 64)

    sblk[slot64(ti), :] = src_in[0:64, :]
    sblk[slot64(16 + across), :] = src_in[64:128, :]
    feats_t[slot64(si), :] = tgt_in[...]
    cur[...] = rot_in[...]
    for part, piece in enumerate(split2(rot_in[...])):
        w2[part * D:(part + 1) * D, :] = piece

    pl.semaphore_wait(barrier, NTGT + NSRC - 2)

    def to(src, dst, send, recv, s, t):
        return pltpu.make_async_remote_copy(
            src_ref=src, dst_ref=dst, send_sem=send, recv_sem=recv,
            device_id=(s, t), device_id_type=MESH)

    def slot128(k):
        return pl.ds(pl.multiple_of(k * OWN, OWN), OWN)

    def beside(c, d):
        return lax.rem(c + d, 4)

    x_ways = [(si, 4 * ty + beside(tx, d)) for d in (1, 3)]
    y_ways = [(si, 4 * beside(ty, d) + tx) for d in (1, 3)]
    z_ways = [(2 * beside(zed, d) + core, ti) for d in (1, 3)]

    def both_ways(ring, src, dst, ways, send):
        for side in range(2):
            to(src, dst, send, near.at[ring, side], *ways[side]).start()

    def relay(ring, ref, at, count, c, ways, send, after):
        for side, k in ((0, beside(c, 3)), (1, beside(c, 1))):
            land = ref.at[pl.ds(pl.multiple_of(at(k), count), count), :]
            pltpu.make_async_copy(land, land, near.at[ring, side]).wait()
            half = ref.at[pl.ds(pl.multiple_of(at(k) + side * (count // 2), count // 2), count // 2), :]
            to(half, half, send, far.at[ring, side], *ways[side]).start()
            after(land, k)

    def relayed(ring, ref, at, count, c, after):
        k = beside(c, 2)
        for side in range(2):
            half = ref.at[pl.ds(pl.multiple_of(at(k) + side * (count // 2), count // 2), count // 2), :]
            pltpu.make_async_copy(half, half, far.at[ring, side]).wait()
        after(ref.at[pl.ds(pl.multiple_of(at(k), count), count), :], k)

    def nothing(land, k):
        pass

    upper, lower = src_in.at[pl.ds(0, 64), :], src_in.at[pl.ds(64, 64), :]
    own_up, own_low = sblk.at[slot64(ti), :], sblk.at[slot64(16 + across), :]
    own_feats = feats_t.at[slot64(si), :]
    both_ways(2, tgt_in, own_feats, z_ways, tgt_send)
    both_ways(0, upper, own_up, x_ways, src_send)
    both_ways(1, lower, own_low, y_ways, src_send)
    both_ways(3, upper, own_up, y_ways, src_send)
    both_ways(4, lower, own_low, x_ways, src_send)
    to(tgt_in, own_feats, tgt_send, tgt_recv.at[zed], sibling, ti).start()


    def up_on(land, k):
        both_ways(3, land, land, y_ways, src_send)

    def low_on(land, k):
        both_ways(4, land, land, x_ways, src_send)

    def to_sibling(land, k):
        to(land, land, tgt_send, tgt_recv.at[k], sibling, ti).start()

    def up_at(k):
        return 64 * (4 * ty + k)

    def low_at(k):
        return ROWS // 2 + 64 * (4 * tx + k)

    def feats_at(k):
        return 64 * (2 * k + core)

    relay(0, sblk, up_at, 64, tx, x_ways, src_send, up_on)
    relay(1, sblk, low_at, 64, ty, y_ways, src_send, low_on)
    relay(2, feats_t, feats_at, 64, zed, z_ways, tgt_send, to_sibling)
    relayed(0, sblk, up_at, 64, tx, up_on)
    relayed(1, sblk, low_at, 64, ty, low_on)
    relayed(2, feats_t, feats_at, 64, zed, to_sibling)
    for k in range(4):
        land = feats_t.at[slot64(2 * k + 1 - core), :]
        pltpu.make_async_copy(land, land, tgt_recv.at[k]).wait()
    most_tgt = feats_t.at[pl.ds(0, D - 64), :]

    def chunk(j):
        return pl.ds(pl.multiple_of(j * CH, CH), CH)

    def reset_cols():
        col_m[...] = jnp.full((8, COLS), -jnp.inf, F32)
        col_s[...] = jnp.zeros((8, COLS), F32)

    def col_update(rows, shifted):
        for ct in range(COLS // 128):
            cut = pl.ds(128 * ct, 128)
            x = scores[rows, cut]
            if shifted:
                x = x + ucol[rows, :]
            x = x.reshape(CH // 8, 8, 128)
            old = col_m[:, cut]
            new = jnp.maximum(old, jnp.max(x, axis=0))
            col_s[:, cut] = col_s[:, cut] * jnp.exp2(old - new) + jnp.sum(jnp.exp2(x - new[None]), axis=0)
            col_m[:, cut] = new

    def col_start(slot):
        for ct in range(COLS // 128):
            cut = pl.ds(128 * ct, 128)
            high = jnp.max(col_m[:, cut], axis=0, keepdims=True)
            total = jnp.sum(col_s[:, cut] * jnp.exp2(col_m[:, cut] - high), axis=0, keepdims=True)
            colx[slot, si, ct:ct + 1, :] = high + jnp.log2(total)

        for d in (4, 5, 2, 6, 3, 7, 1):
            s = 2 * beside(zed, d // 2) + lax.rem(core + d, 2)
            to(colx.at[slot, si], colx.at[slot, si], col_send.at[slot], col_recv.at[slot], s, ti).start()

    def col_finish(slot):
        seven = colx.at[slot, pl.ds(0, NSRC - 1)]
        pltpu.make_async_copy(seven, seven, col_recv.at[slot]).wait()
        every = colx[slot]
        high = jnp.max(every, axis=0)
        v = -LOG_N - (high + jnp.log2(jnp.sum(jnp.exp2(every - high[None]), axis=0)))
        for ct in range(COLS // 128):
            vrow[:, 128 * ct:128 * (ct + 1)] = jnp.broadcast_to(v[ct:ct + 1, :], (8, 128))

    def lane_max(rows):
        top = None
        for ct in range(COLS // 128):
            x = row_tile(rows, ct)
            top = x if top is None else jnp.maximum(top, x)
        return top

    def row_tile(rows, ct):
        cut = pl.ds(128 * ct, 128)
        x = scores[rows, cut].reshape(RB // 8, 8, 128) + vrow[:, cut][None]
        return x.reshape(RB, 128)

    def row_pass(step):
        rows = pl.ds(pl.multiple_of(step * RB, RB), RB)
        top = lane_max(rows)
        total = jnp.exp2(row_tile(rows, 0) - top)
        for ct in range(1, COLS // 128):
            total = total + jnp.exp2(row_tile(rows, ct) - top)
        mrow[rows, :] = top
        lrow[rows, :] = total

    def row_send(slot, half, shared):
        for k in range(8 * half, 8 * half + 8):
            rows = slot128(k)
            if shared:
                high = jnp.transpose(mrow[rows, :])[0:1, :]
                total = jnp.sum(jnp.transpose(lrow[rows, :]), axis=0, keepdims=True)
                tops_row[k:k + 1, :] = high
            else:
                tops = jnp.transpose(mrow[rows, :])
                high = jnp.max(tops, axis=0, keepdims=True)
                total = jnp.sum(jnp.transpose(lrow[rows, :]) * jnp.exp2(tops - high), axis=0, keepdims=True)
            rowx[slot, ti, k:k + 1, :] = high + jnp.log2(total)

        own = rowx.at[slot, ti, pl.ds(8 * half, 8), :]

        for dy, dx in FAR_FIRST:
            t = 4 * beside(ty, dy) + beside(tx, dx)
            to(own, own, row_send_sem.at[slot, half], row_recv.at[slot, half], si, t).start()

    def row_most(slot, half):
        return rowx.at[slot, pl.ds(0, NTGT - 1), pl.ds(8 * half, 8), :]

    def row_combine(slot, half):
        most = row_most(slot, half)
        pltpu.make_async_copy(most, most, row_recv.at[slot, half]).wait()
        every = rowx[slot, :, 8 * half:8 * half + 8, :]
        high = jnp.max(every, axis=0)
        rlse[8 * half:8 * half + 8, :] = high + jnp.log2(jnp.sum(jnp.exp2(every - high[None]), axis=0))

    def row_expanded(k):
        row = rlse[pl.ds(k, 1), :]
        return jnp.transpose(jnp.broadcast_to(row, (128, 128)))

    kinds = ((0, ty, y_ways, tx, x_ways), (1, tx, x_ways, ty, y_ways))

    def span(at, count):
        return pl.ds(pl.multiple_of(at, count), count)

    def arrived(step, kind, side, ring):
        land = ring.at[kind, side]
        pltpu.make_async_copy(land, land, mv_recv.at[step, kind, side]).wait()

    @pl.loop(0, ROUNDS)
    def _(r):
        first, final = r == 0, r == ROUNDS - 1
        reset_cols()

        @pl.loop(0, 4)
        def _(phase):
            offset = phase + phase // 2 - 2 * (phase // 3)
            pair = (chunk(beside(ty, offset)), chunk(4 + beside(tx, offset)))

            @pl.when(jnp.logical_and(first, phase == 1))
            def _():
                relay(3, sblk, lambda k: CH * k, CH, ty, y_ways, src_send, nothing)
                relay(4, sblk, lambda k: ROWS // 2 + CH * k, CH, tx, x_ways, src_send, nothing)

            @pl.when(jnp.logical_and(first, phase == 3))
            def _():
                relayed(3, sblk, lambda k: CH * k, CH, ty, nothing)
                relayed(4, sblk, lambda k: ROWS // 2 + CH * k, CH, tx, nothing)

            turned = [mm(jnp.concatenate([sblk[rows, :]] * 2, axis=1), w2[...]).astype(BF16) for rows in pair]
            for rows, z in zip(pair, turned):
                scores[rows, :] = mm(z, feats_t[...]) * SCALE
            for rows in pair:
                col_update(rows, False)

        col_start(2 * r)

        @pl.when(first)
        def _():
            for part in range(D // 128):
                feats[:, 128 * part:128 * (part + 1)] = jnp.transpose(feats_t[128 * part:128 * (part + 1), :])
            for j in range(ROWS // CH):
                sblk_t[:, CH * j:CH * (j + 1)] = jnp.transpose(sblk[CH * j:CH * (j + 1), :])

        col_finish(2 * r)

        for half in range(2):
            @pl.loop(half * ROWS // RB // 2, (half + 1) * ROWS // RB // 2)
            def _(step):
                row_pass(step)

            row_send(2 * r, half, False)

        reset_cols()
        for half in range(2):
            row_combine(2 * r, half)
            for k in range(8 * half, 8 * half + 8):
                ucol[slot128(k), :] = -LOG_N - row_expanded(k)

            @pl.loop(half * ROWS // CH // 2, (half + 1) * ROWS // CH // 2)
            def _(j):
                col_update(chunk(j), True)

        col_start(2 * r + 1)
        col_finish(2 * r + 1)

        @pl.loop(0, ROWS // RB)
        def _(step):
            rows = pl.ds(pl.multiple_of(step * RB, RB), RB)
            mrow[rows, :] = lane_max(rows)

        @pl.loop(0, ROWS // 512)
        def _(step):
            rows = pl.ds(pl.multiple_of(step * 512, 512), 512)
            mrow[rows, :] = jnp.broadcast_to(jnp.max(mrow[rows, :], axis=1, keepdims=True), (512, 128))

        for half in range(2):
            @pl.loop(half * ROWS // RB // 4, (half + 1) * ROWS // RB // 4)
            def _(step):
                for side in range(2):
                    rows = pl.ds(pl.multiple_of((2 * step + side) * RB, RB), RB)
                    top = mrow[rows, :]
                    total = None
                    for ct in range(COLS // 128):
                        p = jnp.exp2(row_tile(rows, ct) - top)
                        total = p if total is None else total + p
                        probs[rows, 128 * ct:128 * (ct + 1)] = p.astype(BF16)
                    lrow[rows, :] = total

            row_send(2 * r + 1, half, True)

        @pl.loop(0, ROWS // 512)
        def _(step):
            rows = pl.ds(pl.multiple_of(step * 512, 512), 512)
            plan[rows, :] = mm(probs[rows, :], feats[...]).astype(BF16)

        for half in range(2):
            row_combine(2 * r + 1, half)
            factor = jnp.exp2(tops_row[8 * half:8 * half + 8, :] - rlse[8 * half:8 * half + 8, :])
            for k in range(8):
                lane = slice(128 * (8 * half + k), 128 * (8 * half + k + 1))
                sblk_s[:, lane] = (sblk_t[:, lane].astype(F32) * factor[k:k + 1, :]).astype(BF16)

        @pl.when(final)
        def _():
            for k in range(NTGT):
                rows = slot128(k)
                row = jnp.exp2(tops_row[k:k + 1, :] - rlse[k:k + 1, :])
                factor = jnp.transpose(jnp.broadcast_to(row, (128, 128)))
                for cut in range(D // 128):
                    lane = slice(128 * cut, 128 * (cut + 1))
                    mvb[rows, lane] = (plan[rows, lane].astype(F32) * factor).astype(BF16)
            for kind, c, ways, _c, _w in kinds:
                for side in range(2):
                    part = mvb.at[span(1024 * kind + 256 * beside(c, 2) + 128 * side, 128), :]
                    to(part, ring1.at[kind, side], mv_send.at[0], mv_recv.at[0, kind, side], *ways[side]).start()

        theirs = pl.ds(pl.multiple_of((1 - core) * 256, 256), 256)
        ours = pl.ds(pl.multiple_of(core * 256, 256), 256)
        mhold[r] = mm(sblk_s[theirs, :], plan[...]).astype(BF16)
        pair = to(mhold.at[r], sib1.at[r], ar_send.at[0, r], ar_recv.at[0, r], sibling, ti)
        pair.start()
        mine = mm(sblk_s[ours, :], plan[...])
        pair.wait_recv()
        mkeep[r] = (mine + sib1[r].astype(F32)).astype(BF16)

        def lot(k):
            return pl.ds(pl.multiple_of(k * 16, 16), 16)

        for dy, dx in FAR_FIRST:
            t = 4 * beside(ty, dy) + beside(tx, dx)
            to(mkeep.at[r, lot(t), :], tgt1.at[r, ti], ar_send.at[1, r], ar_recv.at[1, r], si, t).start()

        @pl.when(final)
        def _():
            for kind, c, ways, _c, _w in kinds:
                for side in range(2):
                    arrived(0, kind, side, ring1)
                    unit = 1024 * kind + 256 * beside(c, 1 + 2 * side)
                    rows = span(unit + 128 * side, 128)
                    mvb[rows, :] = (mvb[rows, :].astype(F32) + ring1[kind, side].astype(F32)).astype(BF16)
                    to(mvb.at[span(unit, 256), :], ring2.at[kind, side], mv_send.at[1], mv_recv.at[1, kind, side],
                       *ways[side]).start()

        tgt1[r, ti] = mkeep[r, lot(ti), :]
        most = tgt1.at[r, pl.ds(0, NTGT - 1)]
        pltpu.make_async_copy(most, most, ar_recv.at[1, r]).wait()
        zred[r, zed] = jnp.sum(tgt1[r].astype(F32), axis=0).astype(BF16)

        @pl.loop(1, 4)
        def _(d):
            other = lax.rem(zed + d, 4) * 2 + core
            to(zred.at[r, zed], zred.at[r, zed], ar_send.at[2, r], ar_recv.at[2, r], other, ti).start()

        most_z = zred.at[r, pl.ds(0, 3)]
        pltpu.make_async_copy(most_z, most_z, ar_recv.at[2, r]).wait()
        mhalf[r, lot(ti), :] = jnp.sum(zred[r].astype(F32), axis=0).astype(BF16)

        for dy, dx in FAR_FIRST:
            t = 4 * beside(ty, dy) + beside(tx, dx)
            to(mhalf.at[r, lot(ti), :], mhalf.at[r, lot(ti), :], ar_send.at[3, r], ar_recv.at[3, r], si, t).start()

        @pl.when(final)
        def _():
            for kind, c, _w, c2, ways2 in kinds:
                arrived(1, kind, 0, ring2)
                arrived(1, kind, 1, ring2)
                own = mvb[span(1024 * kind + 256 * c, 256), :].astype(F32)
                mvacc[kind] = (own + ring2[kind, 0].astype(F32) + ring2[kind, 1].astype(F32)).astype(BF16)
                for side in range(2):
                    part = mvacc.at[kind, span(64 * beside(c2, 2) + 32 * side, 32), :]
                    to(part, ring3.at[kind, side], mv_send.at[2], mv_recv.at[2, kind, side], *ways2[side]).start()

        most_h = mhalf.at[r, pl.ds(0, 240), :]
        pltpu.make_async_copy(most_h, most_h, ar_recv.at[3, r]).wait()
        back = to(mhalf.at[r], mother.at[r], ar_send.at[4, r], ar_recv.at[4, r], sibling, ti)
        back.start()
        gbuf[ours, :] = mhalf[r].astype(F32)

        @pl.when(final)
        def _():
            for kind, _c, _w, c2, ways2 in kinds:
                for side in range(2):
                    arrived(2, kind, side, ring3)
                    block = 64 * beside(c2, 1 + 2 * side)
                    rows = span(block + 32 * side, 32)
                    mvacc[kind, rows, :] = (mvacc[kind, rows, :].astype(F32) + ring3[kind, side].astype(F32)).astype(BF16)
                    to(mvacc.at[kind, span(block, 64), :], ring4.at[kind, side], mv_send.at[3],
                       mv_recv.at[3, kind, side], *ways2[side]).start()

        back.wait_recv()
        gbuf[theirs, :] = mother[r].astype(F32)

        cross = gbuf[...]
        spread = jnp.sqrt(jnp.mean(cross * cross, axis=(0, 1), keepdims=True) + 1e-06)
        g = cur[...] + 0.1 * cross / (spread * math.sqrt(D))
        gh, gl = split2(g)
        gth, gtl = jnp.transpose(gh), jnp.transpose(gl)
        gram = mm(jnp.concatenate([gth, gth, gtl], axis=1), jnp.concatenate([gh, gl, gh], axis=0))
        rh, rl = split2(gram)
        step = mm(jnp.concatenate([gh, gh, gl], axis=1), jnp.concatenate([rh, rl, rh], axis=0))
        new = 1.5 * g - 0.5 * step
        cur[...] = new

        @pl.when(jnp.logical_not(final))
        def _():
            for part, piece in enumerate(split2(cur[...])):
                w2[part * D:(part + 1) * D, :] = piece

        for slot in (2 * r, 2 * r + 1):
            seven = colx.at[slot, pl.ds(0, NSRC - 1)]
            pltpu.make_async_copy(seven, seven, col_send.at[slot]).wait()
            for half in range(2):
                most_r = row_most(slot, half)
                pltpu.make_async_copy(most_r, most_r, row_send_sem.at[slot, half]).wait()
        pair.wait_send()
        pltpu.make_async_copy(most, most, ar_send.at[1, r]).wait()
        pltpu.make_async_copy(most_z, most_z, ar_send.at[2, r]).wait()
        pltpu.make_async_copy(most_h, most_h, ar_send.at[3, r]).wait()
        back.wait_send()

    aligned[...] = 0.5 * cur[...]
    for kind, _c, _w, c2, _w2 in kinds:
        arrived(3, kind, 0, ring4)
        arrived(3, kind, 1, ring4)
        own = mvacc[kind, span(64 * c2, 64), :].astype(F32)
        moved[64 * kind:64 * (kind + 1), :] = 0.5 * (own + ring4[kind, 0].astype(F32) + ring4[kind, 1].astype(F32))
    for step, ring in enumerate((ring1, ring2, ring3, ring4)):
        pltpu.make_async_copy(ring, ring, mv_send.at[step]).wait()
    pltpu.make_async_copy(most_tgt, most_tgt, tgt_send).wait()
    most_src = sblk.at[pl.ds(0, ROWS - OWN), :]
    pltpu.make_async_copy(most_src, most_src, src_send).wait()


def shards(source, target, rotation):
    vmem = pl.BlockSpec(memory_space=pltpu.VMEM)
    dma = pltpu.SemaphoreType.DMA
    v = pltpu.VMEM
    halves = pl.pallas_call(
        kernel,
        out_shape=(jax.ShapeDtypeStruct((D, D), F32), jax.ShapeDtypeStruct((OWN, D), F32)),
        in_specs=[vmem] * 3,
        out_specs=(vmem, vmem),
        scratch_shapes=[
            v((ROWS, D), BF16),
            v((D, ROWS), BF16),
            v((D, COLS), BF16),
            v((COLS, D), BF16),
            v((ROWS, COLS), F32),
            v((ROWS, D), BF16),
            v((D, ROWS), BF16),
            v((ROWS, COLS), BF16),
            v((16, 128), F32),
            v((ROWS, 128), F32),
            v((ROWS, 128), F32),
            v((ROWS, 128), F32),
            v((8, COLS), F32),
            v((8, COLS), F32),
            v((8, COLS), F32),
            v((2 * D, D), BF16),
            v((D, D), F32),
            v((4, NSRC, 8, 128), F32),
            v((4, NTGT, 16, 128), F32),
            v((2, 256, D), BF16),
            v((2, NTGT, 16, D), BF16),
            v((2, 4, 16, D), BF16),
            v((2, 256, D), BF16),
            v((2, 256, D), BF16),
            v((D, D), F32),
            v((ROWS, D), BF16),
            v((2, 256, D), BF16),
            v((2, 2, 128, D), BF16),
            v((2, 2, 256, D), BF16),
            v((2, 2, 32, D), BF16),
            v((2, 2, 64, D), BF16),
            v((2, 256, D), BF16),
            v((2, 256, D), BF16),
            v((16, 128), F32),
            dma(()), dma((5, 2)), dma((5, 2)), dma(()), dma((4,)),
            dma((4,)), dma((4,)), dma((4, 2)), dma((4, 2)),
            dma((5, 2)), dma((5, 2)), dma((4,)), dma((4, 2, 2)),
        ],
        compiler_params=pltpu.CompilerParams(
            collective_id=0, has_side_effects=True, vmem_limit_bytes=48 * 1024 * 1024),
    )(source, target.T, rotation)
    return tuple(2.0 * half for half in halves)


def solution(mesh):
    return jax.shard_map(
        shards, mesh=mesh, in_specs=(P(("src", "tgt"), None), P("tgt", "src"), P()),
        out_specs=(P(), P(("src", "tgt"), None)), check_vma=False)
```

```python
import functools
import math

import jax
import jax.numpy as jnp
from jax import lax
from jax.experimental import pallas as pl
from jax.experimental.pallas import tpu as pltpu
from jax.sharding import PartitionSpec as P

ROUNDS = 2
MESH = pl.DeviceIdType.MESH
FAR_FIRST = ((2, 2), (1, 2), (3, 2), (2, 1), (2, 3), (1, 1), (3, 3), (1, 3), (3, 1), (0, 2), (2, 0), (0, 1), (0, 3), (1, 0), (3, 0))
F32, BF16 = jnp.float32, jnp.bfloat16
NSRC, NTGT = 8, 16
D = 512
OWN = 128
ROWS = 2048
COLS = 1024
CH = 256
RB = 32
LOG_N = 14.0
SCALE = 1.0 / math.sqrt(D) * math.log2(math.e)


def mm(a, b):
    return jnp.dot(a, b, preferred_element_type=F32)


def split2(w):
    hi = w.astype(BF16)
    return hi, (w - hi.astype(F32)).astype(BF16)


def kernel(
    src_in, tgt_in, rot_in, aligned, moved,
    sblk, sblk_t, feats_t, feats, scores, plan, sblk_s, probs, tops_row, ucol, mrow, lrow,
    col_m, col_s, vrow, w2, cur, colx, rowx, sib1, tgt1, zred, mhalf, mother, gbuf, mvb, mvacc, ring1, ring2, ring3, ring4, mhold, mkeep, rlse,
    src_send, near, far, tgt_send, tgt_recv, col_send, col_recv, row_send_sem, row_recv,
    ar_send, ar_recv, mv_send, mv_recv,
):
    si, ti = lax.axis_index("src"), lax.axis_index("tgt")
    core, zed = lax.rem(si, 2), si // 2
    sibling = zed * 2 + 1 - core
    ty, tx = ti // 4, lax.rem(ti, 4)
    across = 4 * tx + ty

    def tgt_peer(d):
        return lax.rem(ti + d, NTGT)

    def src_peer(d):
        return lax.rem(si + d, NSRC)

    barrier = pltpu.get_barrier_semaphore()

    @pl.loop(1, NTGT)
    def _(d):
        pl.semaphore_signal(barrier, inc=1, device_id=(si, tgt_peer(d)), device_id_type=MESH)

    @pl.loop(1, NSRC)
    def _(d):
        pl.semaphore_signal(barrier, inc=1, device_id=(src_peer(d), ti), device_id_type=MESH)

    def slot64(k):
        return pl.ds(pl.multiple_of(k * 64, 64), 64)

    sblk[slot64(ti), :] = src_in[0:64, :]
    sblk[slot64(16 + across), :] = src_in[64:128, :]
    feats_t[slot64(si), :] = tgt_in[...]
    cur[...] = rot_in[...]
    for part, piece in enumerate(split2(rot_in[...])):
        w2[part * D:(part + 1) * D, :] = piece

    pl.semaphore_wait(barrier, NTGT + NSRC - 2)

    def to(src, dst, send, recv, s, t):
        return pltpu.make_async_remote_copy(
            src_ref=src, dst_ref=dst, send_sem=send, recv_sem=recv,
            device_id=(s, t), device_id_type=MESH)

    def slot128(k):
        return pl.ds(pl.multiple_of(k * OWN, OWN), OWN)

    def beside(c, d):
        return lax.rem(c + d, 4)

    x_ways = [(si, 4 * ty + beside(tx, d)) for d in (1, 3)]
    y_ways = [(si, 4 * beside(ty, d) + tx) for d in (1, 3)]
    z_ways = [(2 * beside(zed, d) + core, ti) for d in (1, 3)]

    def both_ways(ring, src, dst, ways, send):
        for side in range(2):
            to(src, dst, send, near.at[ring, side], *ways[side]).start()

    def relay(ring, ref, at, count, c, ways, send, after):
        for side, k in ((0, beside(c, 3)), (1, beside(c, 1))):
            land = ref.at[pl.ds(pl.multiple_of(at(k), count), count), :]
            pltpu.make_async_copy(land, land, near.at[ring, side]).wait()
            half = ref.at[pl.ds(pl.multiple_of(at(k) + side * (count // 2), count // 2), count // 2), :]
            to(half, half, send, far.at[ring, side], *ways[side]).start()
            after(land, k)

    def relayed(ring, ref, at, count, c, after):
        k = beside(c, 2)
        for side in range(2):
            half = ref.at[pl.ds(pl.multiple_of(at(k) + side * (count // 2), count // 2), count // 2), :]
            pltpu.make_async_copy(half, half, far.at[ring, side]).wait()
        after(ref.at[pl.ds(pl.multiple_of(at(k), count), count), :], k)

    def nothing(land, k):
        pass

    upper, lower = src_in.at[pl.ds(0, 64), :], src_in.at[pl.ds(64, 64), :]
    own_up, own_low = sblk.at[slot64(ti), :], sblk.at[slot64(16 + across), :]
    own_feats = feats_t.at[slot64(si), :]
    both_ways(2, tgt_in, own_feats, z_ways, tgt_send)
    both_ways(0, upper, own_up, x_ways, src_send)
    both_ways(1, lower, own_low, y_ways, src_send)
    both_ways(3, upper, own_up, y_ways, src_send)
    both_ways(4, lower, own_low, x_ways, src_send)
    to(tgt_in, own_feats, tgt_send, tgt_recv.at[zed], sibling, ti).start()


    def up_on(land, k):
        both_ways(3, land, land, y_ways, src_send)

    def low_on(land, k):
        both_ways(4, land, land, x_ways, src_send)

    def to_sibling(land, k):
        to(land, land, tgt_send, tgt_recv.at[k], sibling, ti).start()

    def up_at(k):
        return 64 * (4 * ty + k)

    def low_at(k):
        return ROWS // 2 + 64 * (4 * tx + k)

    def feats_at(k):
        return 64 * (2 * k + core)

    relay(0, sblk, up_at, 64, tx, x_ways, src_send, up_on)
    relay(1, sblk, low_at, 64, ty, y_ways, src_send, low_on)
    relay(2, feats_t, feats_at, 64, zed, z_ways, tgt_send, to_sibling)
    relayed(0, sblk, up_at, 64, tx, up_on)
    relayed(1, sblk, low_at, 64, ty, low_on)
    relayed(2, feats_t, feats_at, 64, zed, to_sibling)
    for k in range(4):
        land = feats_t.at[slot64(2 * k + 1 - core), :]
        pltpu.make_async_copy(land, land, tgt_recv.at[k]).wait()
    most_tgt = feats_t.at[pl.ds(0, D - 64), :]

    def chunk(j):
        return pl.ds(pl.multiple_of(j * CH, CH), CH)

    def reset_cols():
        col_m[...] = jnp.full((8, COLS), -jnp.inf, F32)
        col_s[...] = jnp.zeros((8, COLS), F32)

    def col_update(rows, shifted):
        for ct in range(COLS // 128):
            cut = pl.ds(128 * ct, 128)
            x = scores[rows, cut]
            if shifted:
                x = x + ucol[rows, :]
            x = x.reshape(CH // 8, 8, 128)
            old = col_m[:, cut]
            new = jnp.maximum(old, jnp.max(x, axis=0))
            col_s[:, cut] = col_s[:, cut] * jnp.exp2(old - new) + jnp.sum(jnp.exp2(x - new[None]), axis=0)
            col_m[:, cut] = new

    def col_start(slot):
        for ct in range(COLS // 128):
            cut = pl.ds(128 * ct, 128)
            high = jnp.max(col_m[:, cut], axis=0, keepdims=True)
            total = jnp.sum(col_s[:, cut] * jnp.exp2(col_m[:, cut] - high), axis=0, keepdims=True)
            colx[slot, si, ct:ct + 1, :] = high + jnp.log2(total)

        for d in (4, 5, 2, 6, 3, 7, 1):
            s = 2 * beside(zed, d // 2) + lax.rem(core + d, 2)
            to(colx.at[slot, si], colx.at[slot, si], col_send.at[slot], col_recv.at[slot], s, ti).start()

    def col_finish(slot):
        seven = colx.at[slot, pl.ds(0, NSRC - 1)]
        pltpu.make_async_copy(seven, seven, col_recv.at[slot]).wait()
        every = colx[slot]
        high = jnp.max(every, axis=0)
        v = -LOG_N - (high + jnp.log2(jnp.sum(jnp.exp2(every - high[None]), axis=0)))
        for ct in range(COLS // 128):
            vrow[:, 128 * ct:128 * (ct + 1)] = jnp.broadcast_to(v[ct:ct + 1, :], (8, 128))

    def lane_max(rows):
        top = None
        for ct in range(COLS // 128):
            x = row_tile(rows, ct)
            top = x if top is None else jnp.maximum(top, x)
        return top

    def row_tile(rows, ct):
        cut = pl.ds(128 * ct, 128)
        x = scores[rows, cut].reshape(RB // 8, 8, 128) + vrow[:, cut][None]
        return x.reshape(RB, 128)

    def row_pass(step):
        rows = pl.ds(pl.multiple_of(step * RB, RB), RB)
        top = lane_max(rows)
        total = jnp.exp2(row_tile(rows, 0) - top)
        for ct in range(1, COLS // 128):
            total = total + jnp.exp2(row_tile(rows, ct) - top)
        mrow[rows, :] = top
        lrow[rows, :] = total

    def row_send(slot, half, shared):
        for k in range(8 * half, 8 * half + 8):
            rows = slot128(k)
            if shared:
                high = jnp.transpose(mrow[rows, :])[0:1, :]
                total = jnp.sum(jnp.transpose(lrow[rows, :]), axis=0, keepdims=True)
                tops_row[k:k + 1, :] = high
            else:
                tops = jnp.transpose(mrow[rows, :])
                high = jnp.max(tops, axis=0, keepdims=True)
                total = jnp.sum(jnp.transpose(lrow[rows, :]) * jnp.exp2(tops - high), axis=0, keepdims=True)
            rowx[slot, ti, k:k + 1, :] = high + jnp.log2(total)

        own = rowx.at[slot, ti, pl.ds(8 * half, 8), :]

        for dy, dx in FAR_FIRST:
            t = 4 * beside(ty, dy) + beside(tx, dx)
            to(own, own, row_send_sem.at[slot, half], row_recv.at[slot, half], si, t).start()

    def row_most(slot, half):
        return rowx.at[slot, pl.ds(0, NTGT - 1), pl.ds(8 * half, 8), :]

    def row_combine(slot, half):
        most = row_most(slot, half)
        pltpu.make_async_copy(most, most, row_recv.at[slot, half]).wait()
        every = rowx[slot, :, 8 * half:8 * half + 8, :]
        high = jnp.max(every, axis=0)
        rlse[8 * half:8 * half + 8, :] = high + jnp.log2(jnp.sum(jnp.exp2(every - high[None]), axis=0))

    def row_expanded(k):
        row = rlse[pl.ds(k, 1), :]
        return jnp.transpose(jnp.broadcast_to(row, (128, 128)))

    kinds = ((0, ty, y_ways, tx, x_ways), (1, tx, x_ways, ty, y_ways))

    def span(at, count):
        return pl.ds(pl.multiple_of(at, count), count)

    def arrived(step, kind, side, ring):
        land = ring.at[kind, side]
        pltpu.make_async_copy(land, land, mv_recv.at[step, kind, side]).wait()

    @pl.loop(0, ROUNDS)
    def _(r):
        first, final = r == 0, r == ROUNDS - 1
        reset_cols()

        @pl.loop(0, 4)
        def _(phase):
            offset = phase + phase // 2 - 2 * (phase // 3)
            pair = (chunk(beside(ty, offset)), chunk(4 + beside(tx, offset)))

            @pl.when(jnp.logical_and(first, phase == 1))
            def _():
                relay(3, sblk, lambda k: CH * k, CH, ty, y_ways, src_send, nothing)
                relay(4, sblk, lambda k: ROWS // 2 + CH * k, CH, tx, x_ways, src_send, nothing)

            @pl.when(jnp.logical_and(first, phase == 3))
            def _():
                relayed(3, sblk, lambda k: CH * k, CH, ty, nothing)
                relayed(4, sblk, lambda k: ROWS // 2 + CH * k, CH, tx, nothing)

            turned = [mm(jnp.concatenate([sblk[rows, :]] * 2, axis=1), w2[...]).astype(BF16) for rows in pair]
            for rows, z in zip(pair, turned):
                scores[rows, :] = mm(z, feats_t[...]) * SCALE
            for rows in pair:
                col_update(rows, False)

        col_start(2 * r)

        @pl.when(first)
        def _():
            for part in range(D // 128):
                feats[:, 128 * part:128 * (part + 1)] = jnp.transpose(feats_t[128 * part:128 * (part + 1), :])
            for j in range(ROWS // CH):
                sblk_t[:, CH * j:CH * (j + 1)] = jnp.transpose(sblk[CH * j:CH * (j + 1), :])

        col_finish(2 * r)

        for half in range(2):
            @pl.loop(half * ROWS // RB // 4, (half + 1) * ROWS // RB // 4)
            def _(step):
                row_pass(2 * step)
                row_pass(2 * step + 1)

            row_send(2 * r, half, False)

        reset_cols()
        for half in range(2):
            row_combine(2 * r, half)
            for k in range(8 * half, 8 * half + 8):
                ucol[slot128(k), :] = -LOG_N - row_expanded(k)

            @pl.loop(half * ROWS // CH // 2, (half + 1) * ROWS // CH // 2)
            def _(j):
                col_update(chunk(j), True)

        col_start(2 * r + 1)
        col_finish(2 * r + 1)

        @pl.loop(0, ROWS // RB // 4)
        def _(step):
            for side in range(4):
                rows = pl.ds(pl.multiple_of((4 * step + side) * RB, RB), RB)
                mrow[rows, :] = lane_max(rows)

        @pl.loop(0, ROWS // 512)
        def _(step):
            rows = pl.ds(pl.multiple_of(step * 512, 512), 512)
            mrow[rows, :] = jnp.broadcast_to(jnp.max(mrow[rows, :], axis=1, keepdims=True), (512, 128))

        for half in range(2):
            @pl.loop(half * ROWS // RB // 4, (half + 1) * ROWS // RB // 4)
            def _(step):
                for side in range(2):
                    rows = pl.ds(pl.multiple_of((2 * step + side) * RB, RB), RB)
                    top = mrow[rows, :]
                    total = None
                    for ct in range(COLS // 128):
                        p = jnp.exp2(row_tile(rows, ct) - top)
                        total = p if total is None else total + p
                        probs[rows, 128 * ct:128 * (ct + 1)] = p.astype(BF16)
                    lrow[rows, :] = total

            row_send(2 * r + 1, half, True)

        @pl.loop(0, ROWS // 512)
        def _(step):
            rows = pl.ds(pl.multiple_of(step * 512, 512), 512)
            plan[rows, :] = mm(probs[rows, :], feats[...]).astype(BF16)

        for half in range(2):
            row_combine(2 * r + 1, half)
            factor = jnp.exp2(tops_row[8 * half:8 * half + 8, :] - rlse[8 * half:8 * half + 8, :])
            for k in range(8):
                lane = slice(128 * (8 * half + k), 128 * (8 * half + k + 1))
                sblk_s[:, lane] = (sblk_t[:, lane].astype(F32) * factor[k:k + 1, :]).astype(BF16)
            if half == 0:
                gbuf[...] = mm(sblk_s[:, 0:ROWS // 2], plan[0:ROWS // 2, :])

        @pl.when(final)
        def _():
            for k in range(NTGT):
                rows = slot128(k)
                row = jnp.exp2(tops_row[k:k + 1, :] - rlse[k:k + 1, :])
                factor = jnp.transpose(jnp.broadcast_to(row, (128, 128)))
                for cut in range(D // 128):
                    lane = slice(128 * cut, 128 * (cut + 1))
                    mvb[rows, lane] = (plan[rows, lane].astype(F32) * factor).astype(BF16)
            for kind, c, ways, _c, _w in kinds:
                for side in range(2):
                    part = mvb.at[span(1024 * kind + 256 * beside(c, 2) + 128 * side, 128), :]
                    to(part, ring1.at[kind, side], mv_send.at[0], mv_recv.at[0, kind, side], *ways[side]).start()

        theirs = pl.ds(pl.multiple_of((1 - core) * 256, 256), 256)
        ours = pl.ds(pl.multiple_of(core * 256, 256), 256)
        mhold[r] = (gbuf[theirs, :] + mm(sblk_s[theirs, ROWS // 2:], plan[ROWS // 2:, :])).astype(BF16)
        pair = to(mhold.at[r], sib1.at[r], ar_send.at[0, r], ar_recv.at[0, r], sibling, ti)
        pair.start()
        mine = gbuf[ours, :] + mm(sblk_s[ours, ROWS // 2:], plan[ROWS // 2:, :])
        pair.wait_recv()
        mkeep[r] = (mine + sib1[r].astype(F32)).astype(BF16)

        def lot(k):
            return pl.ds(pl.multiple_of(k * 16, 16), 16)

        for dy, dx in FAR_FIRST:
            t = 4 * beside(ty, dy) + beside(tx, dx)
            to(mkeep.at[r, lot(t), :], tgt1.at[r, ti], ar_send.at[1, r], ar_recv.at[1, r], si, t).start()

        @pl.when(final)
        def _():
            for kind, c, ways, _c, _w in kinds:
                for side in range(2):
                    arrived(0, kind, side, ring1)
                    unit = 1024 * kind + 256 * beside(c, 1 + 2 * side)
                    rows = span(unit + 128 * side, 128)
                    mvb[rows, :] = (mvb[rows, :].astype(F32) + ring1[kind, side].astype(F32)).astype(BF16)
                    to(mvb.at[span(unit, 256), :], ring2.at[kind, side], mv_send.at[1], mv_recv.at[1, kind, side],
                       *ways[side]).start()

        tgt1[r, ti] = mkeep[r, lot(ti), :]
        most = tgt1.at[r, pl.ds(0, NTGT - 1)]
        pltpu.make_async_copy(most, most, ar_recv.at[1, r]).wait()
        zred[r, zed] = jnp.sum(tgt1[r].astype(F32), axis=0).astype(BF16)

        @pl.loop(1, 4)
        def _(d):
            other = lax.rem(zed + d, 4) * 2 + core
            to(zred.at[r, zed], zred.at[r, zed], ar_send.at[2, r], ar_recv.at[2, r], other, ti).start()

        most_z = zred.at[r, pl.ds(0, 3)]
        pltpu.make_async_copy(most_z, most_z, ar_recv.at[2, r]).wait()
        mhalf[r, lot(ti), :] = jnp.sum(zred[r].astype(F32), axis=0).astype(BF16)

        for dy, dx in FAR_FIRST:
            t = 4 * beside(ty, dy) + beside(tx, dx)
            to(mhalf.at[r, lot(ti), :], mhalf.at[r, lot(ti), :], ar_send.at[3, r], ar_recv.at[3, r], si, t).start()

        @pl.when(final)
        def _():
            for kind, c, _w, c2, ways2 in kinds:
                arrived(1, kind, 0, ring2)
                arrived(1, kind, 1, ring2)
                own = mvb[span(1024 * kind + 256 * c, 256), :].astype(F32)
                mvacc[kind] = (own + ring2[kind, 0].astype(F32) + ring2[kind, 1].astype(F32)).astype(BF16)
                for side in range(2):
                    part = mvacc.at[kind, span(64 * beside(c2, 2) + 32 * side, 32), :]
                    to(part, ring3.at[kind, side], mv_send.at[2], mv_recv.at[2, kind, side], *ways2[side]).start()

        most_h = mhalf.at[r, pl.ds(0, 240), :]
        pltpu.make_async_copy(most_h, most_h, ar_recv.at[3, r]).wait()
        back = to(mhalf.at[r], mother.at[r], ar_send.at[4, r], ar_recv.at[4, r], sibling, ti)
        back.start()
        gbuf[ours, :] = mhalf[r].astype(F32)

        @pl.when(final)
        def _():
            for kind, _c, _w, c2, ways2 in kinds:
                for side in range(2):
                    arrived(2, kind, side, ring3)
                    block = 64 * beside(c2, 1 + 2 * side)
                    rows = span(block + 32 * side, 32)
                    mvacc[kind, rows, :] = (mvacc[kind, rows, :].astype(F32) + ring3[kind, side].astype(F32)).astype(BF16)
                    to(mvacc.at[kind, span(block, 64), :], ring4.at[kind, side], mv_send.at[3],
                       mv_recv.at[3, kind, side], *ways2[side]).start()

        back.wait_recv()
        gbuf[theirs, :] = mother[r].astype(F32)

        cross = gbuf[...]
        spread = jnp.sqrt(jnp.mean(cross * cross, axis=(0, 1), keepdims=True) + 1e-06)
        g = cur[...] + 0.1 * cross / (spread * math.sqrt(D))
        gh, gl = split2(g)
        gth, gtl = jnp.transpose(gh), jnp.transpose(gl)
        gram = mm(jnp.concatenate([gth, gth, gtl], axis=1), jnp.concatenate([gh, gl, gh], axis=0))
        rh, rl = split2(gram)
        step = mm(jnp.concatenate([gh, gh, gl], axis=1), jnp.concatenate([rh, rl, rh], axis=0))
        new = 1.5 * g - 0.5 * step
        cur[...] = new

        @pl.when(jnp.logical_not(final))
        def _():
            for part, piece in enumerate(split2(cur[...])):
                w2[part * D:(part + 1) * D, :] = piece

        for slot in (2 * r, 2 * r + 1):
            seven = colx.at[slot, pl.ds(0, NSRC - 1)]
            pltpu.make_async_copy(seven, seven, col_send.at[slot]).wait()
            for half in range(2):
                most_r = row_most(slot, half)
                pltpu.make_async_copy(most_r, most_r, row_send_sem.at[slot, half]).wait()
        pair.wait_send()
        pltpu.make_async_copy(most, most, ar_send.at[1, r]).wait()
        pltpu.make_async_copy(most_z, most_z, ar_send.at[2, r]).wait()
        pltpu.make_async_copy(most_h, most_h, ar_send.at[3, r]).wait()
        back.wait_send()

    aligned[...] = 0.5 * cur[...]
    for kind, _c, _w, c2, _w2 in kinds:
        arrived(3, kind, 0, ring4)
        arrived(3, kind, 1, ring4)
        own = mvacc[kind, span(64 * c2, 64), :].astype(F32)
        moved[64 * kind:64 * (kind + 1), :] = 0.5 * (own + ring4[kind, 0].astype(F32) + ring4[kind, 1].astype(F32))
    for step, ring in enumerate((ring1, ring2, ring3, ring4)):
        pltpu.make_async_copy(ring, ring, mv_send.at[step]).wait()
    pltpu.make_async_copy(most_tgt, most_tgt, tgt_send).wait()
    most_src = sblk.at[pl.ds(0, ROWS - OWN), :]
    pltpu.make_async_copy(most_src, most_src, src_send).wait()


def shards(source, target, rotation):
    vmem = pl.BlockSpec(memory_space=pltpu.VMEM)
    dma = pltpu.SemaphoreType.DMA
    v = pltpu.VMEM
    halves = pl.pallas_call(
        kernel,
        out_shape=(jax.ShapeDtypeStruct((D, D), F32), jax.ShapeDtypeStruct((OWN, D), F32)),
        in_specs=[vmem] * 3,
        out_specs=(vmem, vmem),
        scratch_shapes=[
            v((ROWS, D), BF16),
            v((D, ROWS), BF16),
            v((D, COLS), BF16),
            v((COLS, D), BF16),
            v((ROWS, COLS), F32),
            v((ROWS, D), BF16),
            v((D, ROWS), BF16),
            v((ROWS, COLS), BF16),
            v((16, 128), F32),
            v((ROWS, 128), F32),
            v((ROWS, 128), F32),
            v((ROWS, 128), F32),
            v((8, COLS), F32),
            v((8, COLS), F32),
            v((8, COLS), F32),
            v((2 * D, D), BF16),
            v((D, D), F32),
            v((4, NSRC, 8, 128), F32),
            v((4, NTGT, 16, 128), F32),
            v((2, 256, D), BF16),
            v((2, NTGT, 16, D), BF16),
            v((2, 4, 16, D), BF16),
            v((2, 256, D), BF16),
            v((2, 256, D), BF16),
            v((D, D), F32),
            v((ROWS, D), BF16),
            v((2, 256, D), BF16),
            v((2, 2, 128, D), BF16),
            v((2, 2, 256, D), BF16),
            v((2, 2, 32, D), BF16),
            v((2, 2, 64, D), BF16),
            v((2, 256, D), BF16),
            v((2, 256, D), BF16),
            v((16, 128), F32),
            dma(()), dma((5, 2)), dma((5, 2)), dma(()), dma((4,)),
            dma((4,)), dma((4,)), dma((4, 2)), dma((4, 2)),
            dma((5, 2)), dma((5, 2)), dma((4,)), dma((4, 2, 2)),
        ],
        compiler_params=pltpu.CompilerParams(
            collective_id=0, has_side_effects=True, vmem_limit_bytes=48 * 1024 * 1024),
    )(source, target.T, rotation)
    return tuple(2.0 * half for half in halves)


def solution(mesh):
    return jax.shard_map(
        shards, mesh=mesh, in_specs=(P(("src", "tgt"), None), P("tgt", "src"), P()),
        out_specs=(P(), P(("src", "tgt"), None)), check_vma=False)
```

```python
import functools
import math

import jax
import jax.numpy as jnp
from jax import lax
from jax.experimental import pallas as pl
from jax.experimental.pallas import tpu as pltpu
from jax.sharding import PartitionSpec as P

ROUNDS = 2
MESH = pl.DeviceIdType.MESH
FAR_FIRST = ((2, 2), (1, 2), (3, 2), (2, 1), (2, 3), (1, 1), (3, 3), (1, 3), (3, 1), (0, 2), (2, 0), (0, 1), (0, 3), (1, 0), (3, 0))
F32, BF16 = jnp.float32, jnp.bfloat16
NSRC, NTGT = 8, 16
D = 512
OWN = 128
ROWS = 2048
COLS = 1024
CH = 256
RB = 32
LOG_N = 14.0
SCALE = 1.0 / math.sqrt(D) * math.log2(math.e)


def mm(a, b):
    return jnp.dot(a, b, preferred_element_type=F32)


def split2(w):
    hi = w.astype(BF16)
    return hi, (w - hi.astype(F32)).astype(BF16)


def kernel(
    src_in, tgt_in, rot_in, aligned, moved,
    sblk, sblk_t, feats_t, feats, scores, plan, sblk_s, probs, tops_row, ucol, mrow, lrow,
    col_m, col_s, vrow, w2, cur, colx, rowx, sib1, tgt1, zred, mhalf, mother, gbuf, mvb, mvacc, ring1, ring2, ring3, ring4, mhold, mkeep, rlse,
    src_send, near, far, tgt_send, tgt_recv, col_send, col_recv, row_send_sem, row_recv,
    ar_send, ar_recv, mv_send, mv_recv,
):
    si, ti = lax.axis_index("src"), lax.axis_index("tgt")
    core, zed = lax.rem(si, 2), si // 2
    sibling = zed * 2 + 1 - core
    ty, tx = ti // 4, lax.rem(ti, 4)
    across = 4 * tx + ty

    def tgt_peer(d):
        return lax.rem(ti + d, NTGT)

    def src_peer(d):
        return lax.rem(si + d, NSRC)

    barrier = pltpu.get_barrier_semaphore()

    @pl.loop(1, NTGT)
    def _(d):
        pl.semaphore_signal(barrier, inc=1, device_id=(si, tgt_peer(d)), device_id_type=MESH)

    @pl.loop(1, NSRC)
    def _(d):
        pl.semaphore_signal(barrier, inc=1, device_id=(src_peer(d), ti), device_id_type=MESH)

    def slot64(k):
        return pl.ds(pl.multiple_of(k * 64, 64), 64)

    sblk[slot64(ti), :] = src_in[0:64, :]
    sblk[slot64(16 + across), :] = src_in[64:128, :]
    feats_t[slot64(si), :] = tgt_in[...]
    cur[...] = rot_in[...]
    for part, piece in enumerate(split2(rot_in[...])):
        w2[part * D:(part + 1) * D, :] = piece

    pl.semaphore_wait(barrier, NTGT + NSRC - 2)

    def to(src, dst, send, recv, s, t):
        return pltpu.make_async_remote_copy(
            src_ref=src, dst_ref=dst, send_sem=send, recv_sem=recv,
            device_id=(s, t), device_id_type=MESH)

    def slot128(k):
        return pl.ds(pl.multiple_of(k * OWN, OWN), OWN)

    def beside(c, d):
        return lax.rem(c + d, 4)

    x_ways = [(si, 4 * ty + beside(tx, d)) for d in (1, 3)]
    y_ways = [(si, 4 * beside(ty, d) + tx) for d in (1, 3)]
    z_ways = [(2 * beside(zed, d) + core, ti) for d in (1, 3)]

    def both_ways(ring, src, dst, ways, send):
        for side in range(2):
            to(src, dst, send, near.at[ring, side], *ways[side]).start()

    def relay(ring, ref, at, count, c, ways, send, after):
        for side, k in ((0, beside(c, 3)), (1, beside(c, 1))):
            land = ref.at[pl.ds(pl.multiple_of(at(k), count), count), :]
            pltpu.make_async_copy(land, land, near.at[ring, side]).wait()
            half = ref.at[pl.ds(pl.multiple_of(at(k) + side * (count // 2), count // 2), count // 2), :]
            to(half, half, send, far.at[ring, side], *ways[side]).start()
            after(land, k)

    def relayed(ring, ref, at, count, c, after):
        k = beside(c, 2)
        for side in range(2):
            half = ref.at[pl.ds(pl.multiple_of(at(k) + side * (count // 2), count // 2), count // 2), :]
            pltpu.make_async_copy(half, half, far.at[ring, side]).wait()
        after(ref.at[pl.ds(pl.multiple_of(at(k), count), count), :], k)

    def nothing(land, k):
        pass

    upper, lower = src_in.at[pl.ds(0, 64), :], src_in.at[pl.ds(64, 64), :]
    own_up, own_low = sblk.at[slot64(ti), :], sblk.at[slot64(16 + across), :]
    own_feats = feats_t.at[slot64(si), :]
    both_ways(2, tgt_in, own_feats, z_ways, tgt_send)
    both_ways(0, upper, own_up, x_ways, src_send)
    both_ways(1, lower, own_low, y_ways, src_send)
    both_ways(3, upper, own_up, y_ways, src_send)
    both_ways(4, lower, own_low, x_ways, src_send)
    to(tgt_in, own_feats, tgt_send, tgt_recv.at[zed], sibling, ti).start()


    def up_on(land, k):
        both_ways(3, land, land, y_ways, src_send)

    def low_on(land, k):
        both_ways(4, land, land, x_ways, src_send)

    def to_sibling(land, k):
        to(land, land, tgt_send, tgt_recv.at[k], sibling, ti).start()

    def up_at(k):
        return 64 * (4 * ty + k)

    def low_at(k):
        return ROWS // 2 + 64 * (4 * tx + k)

    def feats_at(k):
        return 64 * (2 * k + core)

    relay(0, sblk, up_at, 64, tx, x_ways, src_send, up_on)
    relay(1, sblk, low_at, 64, ty, y_ways, src_send, low_on)
    relay(2, feats_t, feats_at, 64, zed, z_ways, tgt_send, to_sibling)
    relayed(0, sblk, up_at, 64, tx, up_on)
    relayed(1, sblk, low_at, 64, ty, low_on)
    relayed(2, feats_t, feats_at, 64, zed, to_sibling)
    for k in range(4):
        land = feats_t.at[slot64(2 * k + 1 - core), :]
        pltpu.make_async_copy(land, land, tgt_recv.at[k]).wait()
    most_tgt = feats_t.at[pl.ds(0, D - 64), :]

    def chunk(j):
        return pl.ds(pl.multiple_of(j * CH, CH), CH)

    def reset_cols():
        col_m[...] = jnp.full((8, COLS), -jnp.inf, F32)
        col_s[...] = jnp.zeros((8, COLS), F32)

    def col_update(rows, shifted):
        for ct in range(COLS // 128):
            cut = pl.ds(128 * ct, 128)
            x = scores[rows, cut]
            if shifted:
                x = x + ucol[rows, :]
            x = x.reshape(CH // 8, 8, 128)
            old = col_m[:, cut]
            new = jnp.maximum(old, jnp.max(x, axis=0))
            col_s[:, cut] = col_s[:, cut] * jnp.exp2(old - new) + jnp.sum(jnp.exp2(x - new[None]), axis=0)
            col_m[:, cut] = new

    def col_start(slot):
        for ct in range(COLS // 128):
            cut = pl.ds(128 * ct, 128)
            high = jnp.max(col_m[:, cut], axis=0, keepdims=True)
            total = jnp.sum(col_s[:, cut] * jnp.exp2(col_m[:, cut] - high), axis=0, keepdims=True)
            colx[slot, si, ct:ct + 1, :] = high + jnp.log2(total)

        for d in (4, 5, 2, 6, 3, 7, 1):
            s = 2 * beside(zed, d // 2) + lax.rem(core + d, 2)
            to(colx.at[slot, si], colx.at[slot, si], col_send.at[slot], col_recv.at[slot], s, ti).start()

    def col_finish(slot):
        seven = colx.at[slot, pl.ds(0, NSRC - 1)]
        pltpu.make_async_copy(seven, seven, col_recv.at[slot]).wait()
        every = colx[slot]
        high = jnp.max(every, axis=0)
        v = -LOG_N - (high + jnp.log2(jnp.sum(jnp.exp2(every - high[None]), axis=0)))
        for ct in range(COLS // 128):
            vrow[:, 128 * ct:128 * (ct + 1)] = jnp.broadcast_to(v[ct:ct + 1, :], (8, 128))

    def lane_max(rows):
        top = None
        for ct in range(COLS // 128):
            x = row_tile(rows, ct)
            top = x if top is None else jnp.maximum(top, x)
        return top

    def row_tile(rows, ct):
        cut = pl.ds(128 * ct, 128)
        x = scores[rows, cut].reshape(RB // 8, 8, 128) + vrow[:, cut][None]
        return x.reshape(RB, 128)

    def row_pass(step):
        rows = pl.ds(pl.multiple_of(step * RB, RB), RB)
        top = lane_max(rows)
        total = jnp.exp2(row_tile(rows, 0) - top)
        for ct in range(1, COLS // 128):
            total = total + jnp.exp2(row_tile(rows, ct) - top)
        mrow[rows, :] = top
        lrow[rows, :] = total

    def row_send(slot, half, shared):
        for k in range(8 * half, 8 * half + 8):
            rows = slot128(k)
            if shared:
                high = jnp.transpose(mrow[rows, :])[0:1, :]
                total = jnp.sum(jnp.transpose(lrow[rows, :]), axis=0, keepdims=True)
                tops_row[k:k + 1, :] = high
            else:
                tops = jnp.transpose(mrow[rows, :])
                high = jnp.max(tops, axis=0, keepdims=True)
                total = jnp.sum(jnp.transpose(lrow[rows, :]) * jnp.exp2(tops - high), axis=0, keepdims=True)
            rowx[slot, ti, k:k + 1, :] = high + jnp.log2(total)

        own = rowx.at[slot, ti, pl.ds(8 * half, 8), :]

        for dy, dx in FAR_FIRST:
            t = 4 * beside(ty, dy) + beside(tx, dx)
            to(own, own, row_send_sem.at[slot, half], row_recv.at[slot, half], si, t).start()

    def row_most(slot, half):
        return rowx.at[slot, pl.ds(0, NTGT - 1), pl.ds(8 * half, 8), :]

    def row_combine(slot, half):
        most = row_most(slot, half)
        pltpu.make_async_copy(most, most, row_recv.at[slot, half]).wait()
        every = rowx[slot, :, 8 * half:8 * half + 8, :]
        high = jnp.max(every, axis=0)
        rlse[8 * half:8 * half + 8, :] = high + jnp.log2(jnp.sum(jnp.exp2(every - high[None]), axis=0))

    def row_expanded(k):
        row = rlse[pl.ds(k, 1), :]
        return jnp.transpose(jnp.broadcast_to(row, (128, 128)))

    kinds = ((0, ty, y_ways, tx, x_ways), (1, tx, x_ways, ty, y_ways))

    def span(at, count):
        return pl.ds(pl.multiple_of(at, count), count)

    def arrived(step, kind, side, ring):
        land = ring.at[kind, side]
        pltpu.make_async_copy(land, land, mv_recv.at[step, kind, side]).wait()

    @pl.loop(0, ROUNDS)
    def _(r):
        first, final = r == 0, r == ROUNDS - 1
        reset_cols()

        @pl.loop(0, 4)
        def _(phase):
            offset = phase + phase // 2 - 2 * (phase // 3)
            pair = (chunk(beside(ty, offset)), chunk(4 + beside(tx, offset)))

            @pl.when(jnp.logical_and(first, phase == 1))
            def _():
                relay(3, sblk, lambda k: CH * k, CH, ty, y_ways, src_send, nothing)
                relay(4, sblk, lambda k: ROWS // 2 + CH * k, CH, tx, x_ways, src_send, nothing)

            @pl.when(jnp.logical_and(first, phase == 3))
            def _():
                relayed(3, sblk, lambda k: CH * k, CH, ty, nothing)
                relayed(4, sblk, lambda k: ROWS // 2 + CH * k, CH, tx, nothing)

            turned = [mm(jnp.concatenate([sblk[rows, :]] * 2, axis=1), w2[...]).astype(BF16) for rows in pair]
            for rows, z in zip(pair, turned):
                scores[rows, :] = mm(z, feats_t[...]) * SCALE
            for rows in pair:
                col_update(rows, False)

        col_start(2 * r)

        @pl.when(first)
        def _():
            for part in range(D // 128):
                feats[:, 128 * part:128 * (part + 1)] = jnp.transpose(feats_t[128 * part:128 * (part + 1), :])
            for j in range(ROWS // CH):
                sblk_t[:, CH * j:CH * (j + 1)] = jnp.transpose(sblk[CH * j:CH * (j + 1), :])

        col_finish(2 * r)

        for half in range(2):
            @pl.loop(half * ROWS // RB // 4, (half + 1) * ROWS // RB // 4)
            def _(step):
                row_pass(2 * step)
                row_pass(2 * step + 1)

            row_send(2 * r, half, False)

        reset_cols()
        for half in range(2):
            row_combine(2 * r, half)
            for k in range(8 * half, 8 * half + 8):
                ucol[slot128(k), :] = -LOG_N - row_expanded(k)

            @pl.loop(half * ROWS // CH // 4, (half + 1) * ROWS // CH // 4)
            def _(j):
                col_update(chunk(2 * j), True)
                col_update(chunk(2 * j + 1), True)

        col_start(2 * r + 1)
        col_finish(2 * r + 1)

        @pl.loop(0, ROWS // RB // 4)
        def _(step):
            for side in range(4):
                rows = pl.ds(pl.multiple_of((4 * step + side) * RB, RB), RB)
                mrow[rows, :] = lane_max(rows)

        @pl.loop(0, ROWS // 512)
        def _(step):
            rows = pl.ds(pl.multiple_of(step * 512, 512), 512)
            mrow[rows, :] = jnp.broadcast_to(jnp.max(mrow[rows, :], axis=1, keepdims=True), (512, 128))

        for half in range(2):
            @pl.loop(half * ROWS // RB // 4, (half + 1) * ROWS // RB // 4)
            def _(step):
                for side in range(2):
                    rows = pl.ds(pl.multiple_of((2 * step + side) * RB, RB), RB)
                    top = mrow[rows, :]
                    total = None
                    for ct in range(COLS // 128):
                        p = jnp.exp2(row_tile(rows, ct) - top)
                        total = p if total is None else total + p
                        probs[rows, 128 * ct:128 * (ct + 1)] = p.astype(BF16)
                    lrow[rows, :] = total

            row_send(2 * r + 1, half, True)

        @pl.loop(0, ROWS // 512)
        def _(step):
            rows = pl.ds(pl.multiple_of(step * 512, 512), 512)
            plan[rows, :] = mm(probs[rows, :], feats[...]).astype(BF16)

        for half in range(2):
            row_combine(2 * r + 1, half)
            factor = jnp.exp2(tops_row[8 * half:8 * half + 8, :] - rlse[8 * half:8 * half + 8, :])
            for k in range(8):
                lane = slice(128 * (8 * half + k), 128 * (8 * half + k + 1))
                sblk_s[:, lane] = (sblk_t[:, lane].astype(F32) * factor[k:k + 1, :]).astype(BF16)
            if half == 0:
                gbuf[...] = mm(sblk_s[:, 0:ROWS // 2], plan[0:ROWS // 2, :])

        @pl.when(final)
        def _():
            for k in range(NTGT):
                rows = slot128(k)
                row = jnp.exp2(tops_row[k:k + 1, :] - rlse[k:k + 1, :])
                factor = jnp.transpose(jnp.broadcast_to(row, (128, 128)))
                for cut in range(D // 128):
                    lane = slice(128 * cut, 128 * (cut + 1))
                    mvb[rows, lane] = (plan[rows, lane].astype(F32) * factor).astype(BF16)
            for kind, c, ways, _c, _w in kinds:
                for side in range(2):
                    part = mvb.at[span(1024 * kind + 256 * beside(c, 2) + 128 * side, 128), :]
                    to(part, ring1.at[kind, side], mv_send.at[0], mv_recv.at[0, kind, side], *ways[side]).start()

        theirs = pl.ds(pl.multiple_of((1 - core) * 256, 256), 256)
        ours = pl.ds(pl.multiple_of(core * 256, 256), 256)
        mhold[r] = (gbuf[theirs, :] + mm(sblk_s[theirs, ROWS // 2:], plan[ROWS // 2:, :])).astype(BF16)
        pair = to(mhold.at[r], sib1.at[r], ar_send.at[0, r], ar_recv.at[0, r], sibling, ti)
        pair.start()
        mine = gbuf[ours, :] + mm(sblk_s[ours, ROWS // 2:], plan[ROWS // 2:, :])
        pair.wait_recv()
        mkeep[r] = (mine + sib1[r].astype(F32)).astype(BF16)

        def lot(k):
            return pl.ds(pl.multiple_of(k * 16, 16), 16)

        for dy, dx in FAR_FIRST:
            t = 4 * beside(ty, dy) + beside(tx, dx)
            to(mkeep.at[r, lot(t), :], tgt1.at[r, ti], ar_send.at[1, r], ar_recv.at[1, r], si, t).start()

        @pl.when(final)
        def _():
            for kind, c, ways, _c, _w in kinds:
                for side in range(2):
                    arrived(0, kind, side, ring1)
                    unit = 1024 * kind + 256 * beside(c, 1 + 2 * side)
                    rows = span(unit + 128 * side, 128)
                    mvb[rows, :] = (mvb[rows, :].astype(F32) + ring1[kind, side].astype(F32)).astype(BF16)
                    to(mvb.at[span(unit, 256), :], ring2.at[kind, side], mv_send.at[1], mv_recv.at[1, kind, side],
                       *ways[side]).start()

        tgt1[r, ti] = mkeep[r, lot(ti), :]
        most = tgt1.at[r, pl.ds(0, NTGT - 1)]
        pltpu.make_async_copy(most, most, ar_recv.at[1, r]).wait()
        zred[r, zed] = jnp.sum(tgt1[r].astype(F32), axis=0).astype(BF16)

        @pl.loop(1, 4)
        def _(d):
            other = lax.rem(zed + d, 4) * 2 + core
            to(zred.at[r, zed], zred.at[r, zed], ar_send.at[2, r], ar_recv.at[2, r], other, ti).start()

        most_z = zred.at[r, pl.ds(0, 3)]
        pltpu.make_async_copy(most_z, most_z, ar_recv.at[2, r]).wait()
        mhalf[r, lot(ti), :] = jnp.sum(zred[r].astype(F32), axis=0).astype(BF16)

        for dy, dx in FAR_FIRST:
            t = 4 * beside(ty, dy) + beside(tx, dx)
            to(mhalf.at[r, lot(ti), :], mhalf.at[r, lot(ti), :], ar_send.at[3, r], ar_recv.at[3, r], si, t).start()

        @pl.when(final)
        def _():
            for kind, c, _w, c2, ways2 in kinds:
                arrived(1, kind, 0, ring2)
                arrived(1, kind, 1, ring2)
                own = mvb[span(1024 * kind + 256 * c, 256), :].astype(F32)
                mvacc[kind] = (own + ring2[kind, 0].astype(F32) + ring2[kind, 1].astype(F32)).astype(BF16)
                for side in range(2):
                    part = mvacc.at[kind, span(64 * beside(c2, 2) + 32 * side, 32), :]
                    to(part, ring3.at[kind, side], mv_send.at[2], mv_recv.at[2, kind, side], *ways2[side]).start()

        most_h = mhalf.at[r, pl.ds(0, 240), :]
        pltpu.make_async_copy(most_h, most_h, ar_recv.at[3, r]).wait()
        back = to(mhalf.at[r], mother.at[r], ar_send.at[4, r], ar_recv.at[4, r], sibling, ti)
        back.start()
        gbuf[ours, :] = mhalf[r].astype(F32)

        @pl.when(final)
        def _():
            for kind, _c, _w, c2, ways2 in kinds:
                for side in range(2):
                    arrived(2, kind, side, ring3)
                    block = 64 * beside(c2, 1 + 2 * side)
                    rows = span(block + 32 * side, 32)
                    mvacc[kind, rows, :] = (mvacc[kind, rows, :].astype(F32) + ring3[kind, side].astype(F32)).astype(BF16)
                    to(mvacc.at[kind, span(block, 64), :], ring4.at[kind, side], mv_send.at[3],
                       mv_recv.at[3, kind, side], *ways2[side]).start()

        back.wait_recv()
        gbuf[theirs, :] = mother[r].astype(F32)

        cross = gbuf[...]
        spread = jnp.sqrt(jnp.mean(cross * cross, axis=(0, 1), keepdims=True) + 1e-06)
        g = cur[...] + 0.1 * cross / (spread * math.sqrt(D))
        gh, gl = split2(g)
        gth, gtl = jnp.transpose(gh), jnp.transpose(gl)
        gram = mm(jnp.concatenate([gth, gth, gtl], axis=1), jnp.concatenate([gh, gl, gh], axis=0))
        rh, rl = split2(gram)
        step = mm(jnp.concatenate([gh, gh, gl], axis=1), jnp.concatenate([rh, rl, rh], axis=0))
        new = 1.5 * g - 0.5 * step
        cur[...] = new

        @pl.when(jnp.logical_not(final))
        def _():
            for part, piece in enumerate(split2(cur[...])):
                w2[part * D:(part + 1) * D, :] = piece

        for slot in (2 * r, 2 * r + 1):
            seven = colx.at[slot, pl.ds(0, NSRC - 1)]
            pltpu.make_async_copy(seven, seven, col_send.at[slot]).wait()
            for half in range(2):
                most_r = row_most(slot, half)
                pltpu.make_async_copy(most_r, most_r, row_send_sem.at[slot, half]).wait()
        pair.wait_send()
        pltpu.make_async_copy(most, most, ar_send.at[1, r]).wait()
        pltpu.make_async_copy(most_z, most_z, ar_send.at[2, r]).wait()
        pltpu.make_async_copy(most_h, most_h, ar_send.at[3, r]).wait()
        back.wait_send()

    aligned[...] = 0.5 * cur[...]
    for kind, _c, _w, c2, _w2 in kinds:
        arrived(3, kind, 0, ring4)
        arrived(3, kind, 1, ring4)
        own = mvacc[kind, span(64 * c2, 64), :].astype(F32)
        moved[64 * kind:64 * (kind + 1), :] = 0.5 * (own + ring4[kind, 0].astype(F32) + ring4[kind, 1].astype(F32))
    for step, ring in enumerate((ring1, ring2, ring3, ring4)):
        pltpu.make_async_copy(ring, ring, mv_send.at[step]).wait()
    pltpu.make_async_copy(most_tgt, most_tgt, tgt_send).wait()
    most_src = sblk.at[pl.ds(0, ROWS - OWN), :]
    pltpu.make_async_copy(most_src, most_src, src_send).wait()


def shards(source, target, rotation):
    vmem = pl.BlockSpec(memory_space=pltpu.VMEM)
    dma = pltpu.SemaphoreType.DMA
    v = pltpu.VMEM
    halves = pl.pallas_call(
        kernel,
        out_shape=(jax.ShapeDtypeStruct((D, D), F32), jax.ShapeDtypeStruct((OWN, D), F32)),
        in_specs=[vmem] * 3,
        out_specs=(vmem, vmem),
        scratch_shapes=[
            v((ROWS, D), BF16),
            v((D, ROWS), BF16),
            v((D, COLS), BF16),
            v((COLS, D), BF16),
            v((ROWS, COLS), F32),
            v((ROWS, D), BF16),
            v((D, ROWS), BF16),
            v((ROWS, COLS), BF16),
            v((16, 128), F32),
            v((ROWS, 128), F32),
            v((ROWS, 128), F32),
            v((ROWS, 128), F32),
            v((8, COLS), F32),
            v((8, COLS), F32),
            v((8, COLS), F32),
            v((2 * D, D), BF16),
            v((D, D), F32),
            v((4, NSRC, 8, 128), F32),
            v((4, NTGT, 16, 128), F32),
            v((2, 256, D), BF16),
            v((2, NTGT, 16, D), BF16),
            v((2, 4, 16, D), BF16),
            v((2, 256, D), BF16),
            v((2, 256, D), BF16),
            v((D, D), F32),
            v((ROWS, D), BF16),
            v((2, 256, D), BF16),
            v((2, 2, 128, D), BF16),
            v((2, 2, 256, D), BF16),
            v((2, 2, 32, D), BF16),
            v((2, 2, 64, D), BF16),
            v((2, 256, D), BF16),
            v((2, 256, D), BF16),
            v((16, 128), F32),
            dma(()), dma((5, 2)), dma((5, 2)), dma(()), dma((4,)),
            dma((4,)), dma((4,)), dma((4, 2)), dma((4, 2)),
            dma((5, 2)), dma((5, 2)), dma((4,)), dma((4, 2, 2)),
        ],
        compiler_params=pltpu.CompilerParams(
            collective_id=0, has_side_effects=True, vmem_limit_bytes=48 * 1024 * 1024),
    )(source, target.T, rotation)
    return tuple(2.0 * half for half in halves)


def solution(mesh):
    return jax.shard_map(
        shards, mesh=mesh, in_specs=(P(("src", "tgt"), None), P("tgt", "src"), P()),
        out_specs=(P(), P(("src", "tgt"), None)), check_vma=False)
```
